128 devices in a mesh: tok: 8 (over z, x_lo), head: 16 (over x_hi, y, core).
Axes of the slice: x: 4 (x_hi: 2, x_lo: 2; x = x_hi * 2 + x_lo), y: 4, z: 4, core: 2. Of those that a mesh axis runs over, the one named last changes fastest.
Arguments:
- block_states: bfloat16 [2048, 4096], P('tok', 'head'), may hold values from -24 to 24
- token_ids: int32 [2048], replicated, may hold values from 0 to 100351
- accept: int32 [2048], P('tok'), may hold values 0 or 1
- cache_lengths: int32 [8], replicated, may hold values from 1 to 5120, as said below
- cache_keys: bfloat16 [8192, 4096], P('tok', 'head'), may hold values from -300 to 300
- cache_values: bfloat16 [8192, 4096], P('tok', 'head'), may hold values from -6 to 6
- w_query: bfloat16 [4096, 4096], P(None, 'head'), may hold values from -0.09375 to 0.09375
- w_key: bfloat16 [4096, 4096], P(None, 'head'), may hold values from -0.09375 to 0.09375
- w_value: bfloat16 [4096, 4096], P(None, 'head'), may hold values from -0.09375 to 0.09375
- w_out: bfloat16 [4096, 4096], P('head'), may hold values from -0.09375 to 0.09375
- attn_gain: float32 [4096], replicated, may hold values from 0.25 to 1.75
- final_gain: float32 [4096], replicated, may hold values from 0.25 to 1.75
- embed: bfloat16 [100352, 4096], P('tok', 'head'), may hold values from -6 to 6
- lm_head: bfloat16 [100352, 4096], P(('tok', 'head')), may hold values from -0.25 to 0.25
Outputs:
- hiddens: bfloat16 [2048, 4096], P(('tok', 'head'))
- request_norms: float32 [8], replicated
- top_logits: float32 [2048], replicated
The draws below stay inside these ranges and needn't reach their ends.
Inputs may be any that keep to these rules, and one draw needn't show every extreme that they name: `cache_lengths`: each request has 1 or more cached positions; the counts sum to 8192 and the largest is exactly 5120.
All inputs are finite; a program needn't handle non-finite values. No bound on the sum of `accept` on one device may be relied on, other than what follows from the above.
Results may differ from the reference program's by a relative error of at most 0.0068.
Values may be sent and summed in bfloat16 or wider, within the bound.
A program may use at most 192 MiB of HBM per device.

```python
import math
import jax
import jax.numpy as jnp
import numpy as np
from jax import lax

HEAD_DIM = 128
HEADS = 32
D = 4096
VOCAB = 100352
BLOCK = 256
REQS = 8
ROWS = 2048
CACHE_DEV = 1024
CACHE = 8192
LONGEST = 5120
N_TOK = 8
N_HEAD = 16


def draw_block_states(key, part):
    first_key, second_key = jax.random.split(key, 2)
    positions = (jnp.arange(ROWS) % BLOCK).astype(jnp.float32) / BLOCK
    jitter = jax.random.uniform(second_key, (ROWS, 1), jnp.float32, 0.7, 1.3)
    base_draw = jnp.clip(jax.random.normal(first_key, (ROWS, D), jnp.float32), -4.0, 4.0)
    scaled = base_draw * jnp.exp(1.2 * positions)[:, None] * jitter
    return jnp.clip(scaled, -24.0, 24.0).astype(jnp.bfloat16)


def draw_cache_keys(key, part):
    first_key = jax.random.fold_in(key, 0)
    values = jnp.clip(jax.random.normal(first_key, (CACHE, D), jnp.float32), -5.0, 5.0)
    return values.astype(jnp.bfloat16)


def draw_cache_lengths(key, part):
    first_key, second_key, third_key = jax.random.split(jax.random.fold_in(key, 17), 3)
    long_index = jax.random.randint(first_key, (), REQS // 2, REQS - 1).astype(jnp.int32)
    index = jnp.arange(REQS, dtype=jnp.int32)
    before_draw = jax.random.randint(second_key, (REQS,), 1, CACHE_DEV // REQS + 1).astype(jnp.int32)
    before = jnp.where(index < long_index, before_draw, 0).astype(jnp.int32)
    rest = ((REQS // 2 - 1) * CACHE_DEV - jnp.sum(before)).astype(jnp.int32)
    after_mask = index > long_index
    after_count = (REQS - 1 - long_index).astype(jnp.int32)
    weights = jnp.where(after_mask, jax.random.randint(third_key, (REQS,), 1, 101), 0).astype(jnp.int32)
    extra = rest - after_count
    share = extra * weights // jnp.sum(weights)
    remainder = extra - jnp.sum(share)
    after = jnp.where(after_mask, 1 + share, 0) + jnp.where(index == REQS - 1, remainder, 0)
    total = before + after + jnp.where(index == long_index, LONGEST, 0)
    return total.astype(jnp.int32)


def set_ends(array, own_key, least, top_value):
    longest = array.shape.index(max(array.shape))
    spots = []
    for shift in (0, 1):
        where = [jax.random.randint(jax.random.fold_in(own_key, axis), (), 0, length) for axis, length in enumerate(array.shape)]
        where[longest] = (where[longest] + shift) % array.shape[longest]
        spots.append(tuple(where))
    return array.at[spots[0]].set(least).at[spots[1]].set(top_value)


def levels(rng, dims, pieces, smallest, high):
    gain, own = 1.0, jax.random.fold_in(rng, 6)
    for axis_at, shards_of in pieces:
        draws = jnp.exp(jax.random.uniform(jax.random.fold_in(own, axis_at), (shards_of,), jnp.float32, smallest / len(pieces), high / len(pieces)))
        gain = gain * jnp.repeat(draws, dims[axis_at] // shards_of).reshape([-1 if axis == axis_at else 1 for axis in range(len(dims))])
    return gain


def wide_ids(key, dims, count, slope):
    weights = [min(1 << octave, count + 1 - (1 << octave)) * (1 << 20) // math.isqrt((1 << octave) ** slope) + 1 for octave in range((count + 1).bit_length()) if 1 << octave <= count]
    spread = 1 + sum(weights) // (1 << 30)
    grid = np.cumsum(np.array([max(1, weight // spread) for weight in weights]))
    lot = jax.random.randint(jax.random.fold_in(key, 1), dims, 0, int(grid[len(weights) - 1]))
    start = jnp.left_shift(1, jnp.searchsorted(jnp.asarray(grid, jnp.int32), lot, side="right").astype(jnp.int32))
    standing = start - 1 + jax.random.randint(jax.random.fold_in(key, 4), dims, 0, 1 << 30) % jnp.minimum(start, count + 1 - start)
    return jax.random.permutation(jax.random.fold_in(key, 2), count)[standing].astype(jnp.int32)


def centred(key, extent, scale, most, cuts=(), kind=jnp.bfloat16):
    loudness = levels(key, extent, cuts, -0.22, 0.18) if cuts else 1.0
    entries = jax.random.normal(key, extent, jnp.float32) * scale * loudness
    return jnp.minimum(jnp.maximum(entries, -most), most).astype(kind)


def setup_inputs(seed: int = 0) -> dict:
    seeds = jax.random.split(jax.random.key(seed), 15)
    return {
        "block_states": draw_block_states(jax.random.fold_in(seeds[14], 71), 0),
        "token_ids": set_ends(wide_ids(seeds[1], (ROWS,), VOCAB, 2), jax.random.fold_in(seeds[1], 3), 0, VOCAB - 1).astype(jnp.int32),
        "accept": set_ends((jax.random.randint(seeds[2], (ROWS,), 0, 3) < 1).astype(jnp.int32), jax.random.fold_in(seeds[2], 1), 0, 1),
        "cache_lengths": draw_cache_lengths(jax.random.fold_in(seeds[14], 71), 0),
        "cache_keys": draw_cache_keys(jax.random.fold_in(seeds[14], 71), 0),
        "cache_values": centred(seeds[5], (CACHE, D), 1.0, 6.0, ((0, 8), (1, 16))),
        "w_query": centred(seeds[6], (D, D), D ** -0.5, 0.09375, ((1, 16),)),
        "w_key": centred(seeds[7], (D, D), D ** -0.5, 0.09375, ((1, 16),)),
        "w_value": centred(seeds[8], (D, D), D ** -0.5, 0.09375, ((1, 16),)),
        "w_out": centred(seeds[9], (D, D), D ** -0.5, 0.09375, ((0, 16),)),
        "attn_gain": jnp.clip(1.0 + 0.15 * jax.random.normal(seeds[10], (D,), jnp.float32), 0.25, 1.75),
        "final_gain": jnp.clip(1.0 + 0.15 * jax.random.normal(seeds[11], (D,), jnp.float32), 0.25, 1.75),
        "embed": centred(seeds[12], (VOCAB, D), 1.0, 6.0, ((0, 8), (1, 16))),
        "lm_head": centred(seeds[13], (VOCAB, D), 0.046875, 0.25, ((0, 128),)),
    }


EPSILON = 1e-06

def row_norm(values):
    return values * lax.rsqrt(lax.optimization_barrier(jnp.mean(values * values, axis=-1, keepdims=True)) + EPSILON)

def run_layer(inputs, offsets, counts, cache_keys, cache_values, w_query, w_key, w_value, w_out, attn_gain):
    queries = jnp.dot(inputs, w_query, preferred_element_type=jnp.float32).astype(jnp.bfloat16)
    new_keys = jnp.dot(inputs, w_key, preferred_element_type=jnp.float32).astype(jnp.bfloat16)
    new_values = jnp.dot(inputs, w_value, preferred_element_type=jnp.float32).astype(jnp.bfloat16)
    padding = jnp.zeros((LONGEST, D), jnp.bfloat16)
    padded_keys = jnp.concatenate([cache_keys, padding], axis=0)
    padded_values = jnp.concatenate([cache_values, padding], axis=0)
    score_scale = 1.0 / math.sqrt(HEAD_DIM)

    def one_request(request):
        row_start = (request * BLOCK).astype(jnp.int32)
        query_heads = lax.dynamic_slice_in_dim(queries, row_start, BLOCK, 0).astype(jnp.float32).reshape(BLOCK, HEADS, HEAD_DIM)
        block_keys = lax.dynamic_slice_in_dim(new_keys, row_start, BLOCK, 0).astype(jnp.float32).reshape(BLOCK, HEADS, HEAD_DIM)
        block_values = lax.dynamic_slice_in_dim(new_values, row_start, BLOCK, 0).astype(jnp.float32).reshape(BLOCK, HEADS, HEAD_DIM)
        cache_start = offsets[request].astype(jnp.int32)
        cached_keys = lax.dynamic_slice_in_dim(padded_keys, cache_start, LONGEST, 0).astype(jnp.float32).reshape(LONGEST, HEADS, HEAD_DIM)
        cached_values = lax.dynamic_slice_in_dim(padded_values, cache_start, LONGEST, 0).astype(jnp.float32).reshape(LONGEST, HEADS, HEAD_DIM)
        valid_keys = jnp.arange(LONGEST, dtype=jnp.int32) < counts[request]
        cache_scores = jnp.einsum('qhd,khd->hqk', query_heads, cached_keys) * score_scale
        cache_scores = jnp.where(valid_keys[None, None, :], cache_scores, -jnp.inf)
        block_scores = jnp.einsum('qhd,khd->hqk', query_heads, block_keys) * score_scale
        largest = jnp.maximum(lax.optimization_barrier(jnp.max(cache_scores, axis=-1)), lax.optimization_barrier(jnp.max(block_scores, axis=-1)))
        cache_weights = jnp.exp(cache_scores - largest[:, :, None])
        block_weights = jnp.exp(block_scores - largest[:, :, None])
        weight_sum = lax.optimization_barrier(jnp.sum(cache_weights, axis=-1)) + lax.optimization_barrier(jnp.sum(block_weights, axis=-1))
        mixed = jnp.einsum('hqk,khd->qhd', cache_weights, cached_values) + jnp.einsum('hqk,khd->qhd', block_weights, block_values)
        mixed = mixed / jnp.transpose(weight_sum)[:, :, None]
        return mixed.reshape(BLOCK, D).astype(jnp.bfloat16)
    attended = lax.map(one_request, jnp.arange(REQS, dtype=jnp.int32)).reshape(ROWS, D)
    projected = jnp.dot(attended, w_out, preferred_element_type=jnp.float32)
    return (inputs.astype(jnp.float32) + row_norm(projected) * attn_gain).astype(jnp.bfloat16)

def reference(block_states, token_ids, accept, cache_lengths, cache_keys, cache_values, w_query, w_key, w_value, w_out, attn_gain, final_gain, embed, lm_head):
    counts = cache_lengths.astype(jnp.int32)
    offsets = (jnp.cumsum(counts) - counts).astype(jnp.int32)
    first_pass = run_layer(block_states, offsets, counts, cache_keys, cache_values, w_query, w_key, w_value, w_out, attn_gain)
    widened = first_pass.astype(jnp.float32)
    request_norms = jnp.sqrt(lax.optimization_barrier(jnp.mean((widened * widened).reshape(REQS, BLOCK * D), axis=1)))
    normed = (row_norm(widened) * final_gain).astype(jnp.bfloat16)
    shards = N_TOK * N_HEAD
    vocab_pieces = lm_head.reshape(shards, VOCAB // shards, D)

    def piece_max(vocab_piece):
        logits = lax.dot_general(normed, vocab_piece, (((1,), (1,)), ((), ())), preferred_element_type=jnp.float32)
        return lax.optimization_barrier(jnp.max(logits, axis=1))
    top_logits = lax.optimization_barrier(jnp.max(lax.map(piece_max, vocab_pieces), axis=0))
    chosen = (accept == 1)[:, None]
    swapped = jnp.where(chosen, embed[token_ids], block_states)
    hiddens = run_layer(swapped, offsets, counts, cache_keys, cache_values, w_query, w_key, w_value, w_out, attn_gain)
    return (hiddens, request_norms, top_logits)
```

```python
import math

import jax
import jax.numpy as jnp
from jax import lax
from jax.experimental import pallas as pl
from jax.experimental.pallas import tpu as pltpu
from jax.sharding import PartitionSpec as P

HEAD_DIM = 128
EPSILON = 1e-06
NEG = -1e30
SCALE2 = (1.0 / math.sqrt(HEAD_DIM)) * math.log2(math.e)
MESH = pl.DeviceIdType.MESH
BF = jnp.bfloat16
F32 = jnp.float32
ANY = pl.BlockSpec(memory_space=pl.ANY)
VM = pl.BlockSpec(memory_space=pltpu.VMEM)
REL8 = ((0, 2), (1, 2), (1, 1), (1, 3), (0, 1), (0, 3), (1, 0))


def coords():
    t = lax.axis_index("tok")
    h = lax.axis_index("head")
    return t // 2, lax.rem(t, 2), h // 8, lax.rem(h // 2, 4), lax.rem(h, 2)


def place(z, xl, xh, y, c):
    return (z * 2 + xl, xh * 8 + y * 2 + c)


def ring(v, d):
    return lax.rem(v + d, 4)


class Links:
    def __init__(self, send, recv):
        self.send, self.recv, self.used = send, recv, 0

    def copy(self, src, dst, device):
        k = self.used
        self.used += 1
        cp = pltpu.make_async_remote_copy(
            src_ref=src,
            dst_ref=dst,
            send_sem=self.send.at[k],
            recv_sem=self.recv.at[k],
            device_id=device,
            device_id_type=MESH,
        )
        cp.start()
        return cp


class Task:
    def __init__(self, body, ins, outs, scratch, copies, local, peers):
        self.body, self.ins, self.outs = body, ins, outs
        self.scratch = list(scratch) + [
            pltpu.SemaphoreType.DMA((copies,)),
            pltpu.SemaphoreType.DMA((copies,)),
            pltpu.SemaphoreType.DMA((max(local, 1),)),
        ]
        self.peers = peers


def head_peers_ag():
    z, xl, xh, y, c = coords()
    out = [("core", place(z, xl, xh, y, 1 - c)), ("x2", place(z, xl, 1 - xh, y, c))]
    return out + [("y%d" % d, place(z, xl, xh, ring(y, d), c)) for d in (1, 2, 3)]


def head_peers_all():
    z, xl, xh, y, c = coords()
    out = [("core", place(z, xl, xh, y, 1 - c))]
    return out + [
        ("h%d%d" % (dx, dy), place(z, xl, lax.rem(xh + dx, 2), ring(y, dy), c)) for dx, dy in REL8
    ]


def tok_peers_ag():
    z, xl, xh, y, c = coords()
    out = [("x1", place(z, 1 - xl, xh, y, c))]
    return out + [("z%d" % d, place(ring(z, d), xl, xh, y, c)) for d in (1, 2, 3)]


def tok_peers_all():
    z, xl, xh, y, c = coords()
    return [
        ("t%d%d" % (dx, dz), place(ring(z, dz), lax.rem(xl + dx, 2), xh, y, c)) for dx, dz in REL8
    ]


CANON = {"h10": "x2", "h01": "y1", "h02": "y2", "h03": "y3"}
CANON.update({"t10": "x1", "t01": "z1", "t02": "z2", "t03": "z3"})


def comm(tasks, cid, name):
    n_in = [len(t.ins) for t in tasks]
    n_out = [len(t.outs) for t in tasks]
    n_scr = [len(t.scratch) for t in tasks]

    def kernel(*refs):
        ins, rest = refs[: sum(n_in)], refs[sum(n_in) :]
        outs, scr = rest[: sum(n_out)], rest[sum(n_out) :]
        peers = {}
        for t in tasks:
            for key, device in t.peers():
                peers.setdefault(CANON.get(key, key), device)
        barrier = pltpu.get_barrier_semaphore()
        for device in peers.values():
            pl.semaphore_signal(barrier, inc=1, device_id=device, device_id_type=MESH)
        pl.semaphore_wait(barrier, len(peers))
        running, a, b, c = [], 0, 0, 0
        for k, t in enumerate(tasks):
            running.append(
                t.body(
                    ins[a : a + n_in[k]], outs[b : b + n_out[k]], scr[c : c + n_scr[k]]
                )
            )
            a, b, c = a + n_in[k], b + n_out[k], c + n_scr[k]
        while running:
            again = []
            for g in running:
                if next(g, StopIteration) is not StopIteration:
                    again.append(g)
            running = again

    flat = pl.pallas_call(
        kernel,
        out_shape=[o[0] for t in tasks for o in t.outs],
        in_specs=[i[1] for t in tasks for i in t.ins],
        out_specs=[o[1] for t in tasks for o in t.outs],
        scratch_shapes=[s for t in tasks for s in t.scratch],
        compiler_params=pltpu.CompilerParams(
            collective_id=cid, has_side_effects=True, vmem_limit_bytes=40 << 20
        ),
        name=name,
    )(*[i[0] for t in tasks for i in t.ins])
    res, b = [], 0
    for n in n_out:
        res.append(flat[b : b + n])
        b += n
    return res


def gather_features(x):
    def body(ins, outs, scr):
        (x_ref,), (f_ref,), (send, recv, loc) = ins, outs, scr
        z, xl, xh, y, c = coords()
        links = Links(send, recv)

        def cols(xh_, y_, c_):
            return f_ref.at[:, pl.ds(pl.multiple_of((xh_ * 8 + y_ * 2 + c_) * 256, 256), 256)]

        core = place(z, xl, xh, y, 1 - c)
        own = cols(xh, y, c)
        keep = pltpu.make_async_copy(x_ref, own, loc.at[0])
        keep.start()
        sent, landed = [], []
        over_x = links.copy(x_ref, own, place(z, xl, 1 - xh, y, c))
        over_y = {d: links.copy(x_ref, own, place(z, xl, xh, ring(y, d), c)) for d in (2, 1, 3)}
        landed.append(links.copy(x_ref, own, core))
        yield 0
        over_x.wait_recv()
        far = cols(1 - xh, y, c)
        far_y = {d: links.copy(far, far, place(z, xl, xh, ring(y, d), c)) for d in (2, 1, 3)}
        landed.append(links.copy(far, far, core))
        yield 0
        for d in (1, 3, 2):
            over_y[d].wait_recv()
            got = cols(xh, ring(y, 4 - d), c)
            landed.append(links.copy(got, got, core))
        yield 0
        for d in (1, 3, 2):
            far_y[d].wait_recv()
            got = cols(1 - xh, ring(y, 4 - d), c)
            landed.append(links.copy(got, got, core))
        yield 0
        keep.wait()
        for cp in [over_x] + list(over_y.values()) + list(far_y.values()):
            cp.wait_send()
        for cp in landed:
            cp.wait()

    return Task(
        body, [(x, ANY)], [(jax.ShapeDtypeStruct((256, 4096), BF), ANY)], [], 15, 1, head_peers_ag
    )


def gather_queries(q):
    def body(ins, outs, scr):
        (q_ref,), (o_ref,), (send, recv, loc) = ins, outs, scr
        z, xl, xh, y, c = coords()
        links = Links(send, recv)
        own = o_ref.at[z * 2 + xl]
        keep = pltpu.make_async_copy(q_ref, own, loc.at[0])
        keep.start()
        over_x = links.copy(q_ref, own, place(z, 1 - xl, xh, y, c))
        over_z = [links.copy(q_ref, own, place(ring(z, d), xl, xh, y, c)) for d in (2, 1, 3)]
        yield 0
        over_x.wait_recv()
        far = o_ref.at[z * 2 + 1 - xl]
        over_z += [links.copy(far, far, place(ring(z, d), xl, xh, y, c)) for d in (2, 1, 3)]
        yield 0
        over_x.wait_send()
        for cp in over_z:
            cp.wait()
        keep.wait()

    return Task(
        body, [(q, ANY)], [(jax.ShapeDtypeStruct((8, 256, 256), BF), ANY)], [], 7, 1, tok_peers_ag
    )


def exchange_tok(*arrays):
    def body(ins, outs, scr):
        send, recv, loc = scr
        z, xl, xh, y, c = coords()
        t = z * 2 + xl
        links = Links(send, recv)
        keep, cps = [], []
        for k, (src, dst) in enumerate(zip(ins, outs)):
            keep.append(pltpu.make_async_copy(src.at[t], dst.at[t], loc.at[k]))
            keep[-1].start()
        for dx, dz in REL8:
            z_, xl_ = ring(z, dz), lax.rem(xl + dx, 2)
            for src, dst in zip(ins, outs):
                cps.append(links.copy(src.at[z_ * 2 + xl_], dst.at[t], place(z_, xl_, xh, y, c)))
        yield 0
        for cp in cps:
            cp.wait()
        for cp in keep:
            cp.wait()

    n = len(arrays)
    return Task(
        body,
        [(a, ANY) for a in arrays],
        [(jax.ShapeDtypeStruct(a.shape, a.dtype), ANY) for a in arrays],
        [],
        7 * n,
        n,
        tok_peers_all,
    )


def unit_rows(v):
    return v * lax.rsqrt(jnp.mean(v * v, axis=-1, keepdims=True) + EPSILON)


def reduce_layer(part, features, attn_gain, final_gain, first):
    def body(ins, outs, scr):
        part_ref, f_ref, again_ref = ins[:3]
        mine, theirs, came, xrow, send, recv, loc = scr
        z, xl, xh, y, c = coords()
        j = xh * 4 + y
        links = Links(send, recv)
        l0 = pltpu.make_async_copy(part_ref.at[:, c], mine, loc.at[0])
        l1 = pltpu.make_async_copy(
            f_ref.at[pl.ds(pl.multiple_of((j * 2 + c) * 16, 16), 16), :], xrow, loc.at[1]
        )
        l0.start()
        l1.start()
        swap = links.copy(part_ref.at[:, 1 - c], theirs, place(z, xl, xh, y, 1 - c))
        yield 0
        l0.wait()
        swap.wait_recv()
        cps = []
        for dx, dy in REL8:
            xh_, y_ = lax.rem(xh + dx, 2), ring(y, dy)
            j_ = xh_ * 4 + y_
            mine[j_] = (mine[j_].astype(F32) + theirs[j_].astype(F32)).astype(BF)
            cps.append(links.copy(mine.at[j_], came.at[j], place(z, xl, xh_, y_, c)))
        total = mine[j].astype(F32) + theirs[j].astype(F32)
        yield 0
        swap.wait_send()
        for cp in cps:
            cp.wait()
        for dx, dy in REL8:
            total = total + came[lax.rem(xh + dx, 2) * 4 + ring(y, dy)].astype(F32)
        l1.wait()
        states = (xrow[...].astype(F32) + unit_rows(total) * again_ref[...]).astype(BF)
        if not first:
            outs[0][...] = states
            return
        wide = states.astype(F32)
        squares = jnp.sum(wide * wide, axis=-1, keepdims=True)
        normed = wide * lax.rsqrt(squares * (1.0 / 4096) + EPSILON) * ins[3][...]
        outs[0][...] = normed.astype(BF)
        lane = lax.broadcasted_iota(jnp.int32, (8, 256), 1)
        row = lax.broadcasted_iota(jnp.int32, (8, 256), 0)
        outs[1][...] = jnp.where((lane == z * 2 + xl) & (row == 4), jnp.sum(squares), 0.0)

    ins = [(part, ANY), (features, ANY), (attn_gain, VM)]
    outs = [(jax.ShapeDtypeStruct((16, 4096), BF), VM)]
    if first:
        ins.append((final_gain, VM))
        outs.append((jax.ShapeDtypeStruct((8, 256), F32), VM))
    block = pltpu.VMEM((8, 16, 4096), BF)
    scratch = [block, block, block, pltpu.VMEM((16, 4096), BF)]
    return Task(body, ins, outs, scratch, 8, 2, head_peers_all)


def axis_peers():
    z, xl, xh, y, c = coords()
    x = xh * 2 + xl
    out = []
    for d in (1, 2, 3):
        x_ = ring(x, d)
        out.append(("x%d" % d, place(z, lax.rem(x_, 2), x_ // 2, y, c)))
        out.append(("y%d" % d, place(z, xl, xh, ring(y, d), c)))
        out.append(("z%d" % d, place(ring(z, d), xl, xh, y, c)))
    return out


def along(axis, d):
    z, xl, xh, y, c = coords()
    if axis == "x":
        x_ = ring(xh * 2 + xl, d)
        return place(z, lax.rem(x_, 2), x_ // 2, y, c)
    if axis == "y":
        return place(z, xl, xh, ring(y, d), c)
    return place(ring(z, d), xl, xh, y, c)


def gather_all(normed):
    spans = ((0, 1408), (1408, 1408), (2816, 1280))
    orders = (("x", "y", "z"), ("y", "z", "x"), ("z", "x", "y"))

    def body(ins, outs, scr):
        (n_ref,), (o_ref,), (send, recv, loc) = ins, outs, scr
        z, xl, xh, y, c = coords()
        links = Links(send, recv)
        full = slice(None)

        def block(known, cut):
            at = (
                full if "z" in known else z,
                full if "x" in known else xl,
                full if "x" in known else xh,
                full if "y" in known else y,
                full,
                pl.ds(*cut),
            )
            return o_ref.at[at]

        keep = pltpu.make_async_copy(n_ref, o_ref.at[z, xl, xh, y], loc.at[0])
        keep.start()
        sent = [[] for _ in spans]
        last = [[] for _ in spans]
        for p, cut in enumerate(spans):
            axis = orders[p][0]
            src, dst = n_ref.at[:, pl.ds(*cut)], block("", cut)
            last[p] = [links.copy(src, dst, along(axis, d)) for d in (2, 1, 3)]
        keep.wait()
        yield 0
        for stage in (1, 2):
            for p, cut in enumerate(spans):
                for cp in last[p]:
                    cp.wait_recv()
                sent[p] += last[p]
                ref = block("".join(orders[p][:stage]), cut)
                axis = orders[p][stage]
                last[p] = [links.copy(ref, ref, along(axis, d)) for d in (2, 1, 3)]
            yield 0
        for p in range(3):
            for cp in last[p]:
                cp.wait_recv()
            for cp in sent[p] + last[p]:
                cp.wait_send()

    return Task(
        body,
        [(normed, ANY)],
        [(jax.ShapeDtypeStruct((4, 2, 2, 4, 16, 4096), BF), ANY)],
        [],
        27,
        1,
        axis_peers,
    )


def reduce_best(best, squares):
    def body(ins, outs, scr):
        best_ref, sq_ref = ins
        out_ref, sum_ref = outs
        held, came, send, recv, loc = scr
        z, xl, xh, y, c = coords()
        links = Links(send, recv)
        held[0] = sq_ref[...]
        held[0, pl.ds(0, 4), :] = best_ref[...]
        top = lax.broadcasted_iota(jnp.int32, (8, 256), 0) < 4
        for s, axis in enumerate("xyz"):
            cps = [links.copy(held.at[s], came.at[s, d - 1], along(axis, d)) for d in (2, 1, 3)]
            for cp in cps:
                cp.wait()
            v = held[s]
            for d in range(3):
                w = came[s, d]
                v = jnp.where(top, jnp.maximum(v, w), v + w)
            held[s + 1] = v
        cp = links.copy(held.at[3], came.at[3, 0], place(z, xl, xh, y, 1 - c))
        cp.wait()
        v, w = held[3], came[3, 0]
        out_ref[c] = v
        out_ref[1 - c] = w
        sum_ref[...] = v + w
        yield 0

    def peers():
        z, xl, xh, y, c = coords()
        return axis_peers() + [("core", place(z, xl, xh, y, 1 - c))]

    return Task(
        body,
        [(best, VM), (squares, VM)],
        [
            (jax.ShapeDtypeStruct((2, 8, 256), F32), VM),
            (jax.ShapeDtypeStruct((8, 256), F32), VM),
        ],
        [pltpu.VMEM((4, 8, 256), F32), pltpu.VMEM((4, 3, 8, 256), F32)],
        10,
        1,
        peers,
    )


def project(x, w_query, w_key, w_value):
    steps = 4
    depth = x.shape[1] // steps
    rows = x.shape[0]

    def kernel(x_ref, a_ref, b_ref, c_ref, q_ref, k_ref, v_ref, acc):
        i = pl.program_id(0)
        xs = x_ref[...]
        for n, w_ref in enumerate((a_ref, b_ref, c_ref)):
            part = jnp.dot(xs, w_ref[...], preferred_element_type=F32)

            @pl.when(i == 0)
            def _():
                acc[n] = part

            @pl.when(i > 0)
            def _():
                acc[n] += part

        @pl.when(i == steps - 1)
        def _():
            for n, o_ref in enumerate((q_ref, k_ref, v_ref)):
                o_ref[...] = acc[n].astype(BF)

    wide = w_query.shape[1]
    weight = pl.BlockSpec((depth, wide), lambda i: (i, 0))
    out = pl.BlockSpec((rows, wide), lambda i: (0, 0))
    return pl.pallas_call(
        kernel,
        grid=(steps,),
        in_specs=[pl.BlockSpec((rows, depth), lambda i: (0, i)), weight, weight, weight],
        out_specs=[out] * 3,
        out_shape=[jax.ShapeDtypeStruct((rows, wide), BF)] * 3,
        scratch_shapes=[pltpu.VMEM((3, rows, wide), F32)],
        compiler_params=pltpu.CompilerParams(vmem_limit_bytes=32 << 20),
        name="project",
    )(x, w_query, w_key, w_value)


def scores(q, k):
    return lax.dot_general(q, k, (((1,), (1,)), ((), ())), preferred_element_type=F32) * SCALE2


def cached_attention(begins, ends, queries, keys, values):
    rows = queries.shape[1]
    span = 256

    def kernel(lo_ref, hi_ref, q_ref, k_ref, v_ref, o_ref, s_ref, m_sc, l_sc, a_sc):
        r = pl.program_id(0)
        lo, hi = lo_ref[r], hi_ref[r]
        m_sc[...] = jnp.full_like(m_sc, NEG)
        l_sc[...] = jnp.zeros_like(l_sc)
        a_sc[...] = jnp.zeros_like(a_sc)

        @pl.when(hi > lo)
        def _():
            def step(b, carry):
                at = pl.multiple_of(b * span, span)
                pos = at + lax.broadcasted_iota(jnp.int32, (rows, span), 1)
                valid = (pos >= lo) & (pos < hi)
                for g in range(2):
                    cut = slice(g * HEAD_DIM, (g + 1) * HEAD_DIM)
                    s = scores(q_ref[0, :, cut], k_ref[pl.ds(at, span), cut])
                    s = jnp.where(valid, s, NEG)
                    old = m_sc[g, :, 0:1]
                    new = jnp.maximum(old, jnp.max(s, axis=-1, keepdims=True))
                    p = jnp.where(valid, jnp.exp2(s - new), 0.0)
                    f = jnp.exp2(old - new)
                    l_sc[g] = l_sc[g] * f + jnp.sum(p, axis=-1, keepdims=True)
                    a_sc[g] = a_sc[g] * f + jnp.dot(
                        p.astype(BF), v_ref[pl.ds(at, span), cut], preferred_element_type=F32
                    )
                    m_sc[g] = jnp.broadcast_to(new, m_sc.shape[1:])
                return carry

            lax.fori_loop(lo // span, (hi + span - 1) // span, step, 0)

        lane = lax.broadcasted_iota(jnp.int32, (rows, 128), 1)
        stats = jnp.where(lane == 0, m_sc[0], jnp.where(lane == 1, m_sc[1], 0.0))
        stats = jnp.where(lane == 2, l_sc[0], jnp.where(lane == 3, l_sc[1], stats))
        s_ref[0] = jnp.transpose(stats)[:8]
        for g in range(2):
            o_ref[0, :, g * HEAD_DIM : (g + 1) * HEAD_DIM] = a_sc[g].astype(BF)

    whole = pl.BlockSpec(keys.shape, lambda r, a, b: (0, 0))
    per = pl.BlockSpec((1, rows, 256), lambda r, a, b: (r, 0, 0))
    return pl.pallas_call(
        kernel,
        grid_spec=pltpu.PrefetchScalarGridSpec(
            num_scalar_prefetch=2,
            grid=(8,),
            in_specs=[per, whole, whole],
            out_specs=[per, pl.BlockSpec((1, 8, rows), lambda r, a, b: (r, 0, 0))],
            scratch_shapes=[
                pltpu.VMEM((2, rows, 128), F32),
                pltpu.VMEM((2, rows, 128), F32),
                pltpu.VMEM((2, rows, HEAD_DIM), F32),
            ],
        ),
        out_shape=[
            jax.ShapeDtypeStruct((8, rows, 256), BF),
            jax.ShapeDtypeStruct((8, 8, rows), F32),
        ],
        compiler_params=pltpu.CompilerParams(vmem_limit_bytes=32 << 20),
        name="cached",
    )(begins, ends, queries, keys, values)


def combine(parts, stats, q, k, v, w_out):
    steps = 4
    wide = w_out.shape[1] // steps

    def kernel(p_ref, s_ref, q_ref, k_ref, v_ref, w_ref, o_ref, att):
        @pl.when(pl.program_id(0) == 0)
        def _():
            st = jnp.concatenate([s_ref[...].reshape(64, 256), jnp.zeros((64, 256), F32)], axis=0)
            st = jnp.transpose(st)
            for g in range(2):
                cut = slice(g * HEAD_DIM, (g + 1) * HEAD_DIM)
                s = scores(q_ref[:, cut], k_ref[:, cut])
                top = jnp.max(s, axis=-1, keepdims=True)
                for i in range(8):
                    top = jnp.maximum(top, st[:, i * 8 + g : i * 8 + g + 1])
                p = jnp.exp2(s - top)
                mass = jnp.sum(p, axis=-1, keepdims=True)
                acc = jnp.dot(p.astype(BF), v_ref[:, cut], preferred_element_type=F32)
                for i in range(8):
                    f = jnp.exp2(st[:, i * 8 + g : i * 8 + g + 1] - top)
                    mass = mass + f * st[:, i * 8 + g + 2 : i * 8 + g + 3]
                    acc = acc + f * p_ref[i, :, cut].astype(F32)
                att[:, cut] = (acc / mass).astype(BF)

        o = jnp.dot(att[...], w_ref[...], preferred_element_type=F32).astype(BF)
        o_ref[...] = o.reshape(o_ref.shape)

    def whole(a):
        return pl.BlockSpec(a.shape, lambda i: (0,) * a.ndim)

    return pl.pallas_call(
        kernel,
        grid=(steps,),
        in_specs=[whole(a) for a in (parts, stats, q, k, v)]
        + [pl.BlockSpec((256, wide), lambda i: (0, i))],
        out_specs=pl.BlockSpec((8, 2, 16, wide), lambda i: (0, 0, 0, i)),
        out_shape=jax.ShapeDtypeStruct((8, 2, 16, w_out.shape[1]), BF),
        scratch_shapes=[pltpu.VMEM((256, 256), BF)],
        compiler_params=pltpu.CompilerParams(vmem_limit_bytes=32 << 20),
        name="combine",
    )(parts, stats, q, k, v, w_out)


def best_logits(rows, own_head, other_head):
    vocab, width = own_head.shape

    def kernel(x_ref, a_ref, b_ref, o_ref):
        i = pl.program_id(0)
        x = x_ref[...]
        top = None
        for w_ref in (a_ref, b_ref):
            logits = lax.dot_general(
                w_ref[...], x, (((1,), (1,)), ((), ())), preferred_element_type=F32
            )
            m = jnp.max(logits, axis=0, keepdims=True)
            top = m if top is None else jnp.maximum(top, m)
        o_ref[pl.ds(i, 1), :] = top

    head = pl.BlockSpec((vocab, width), lambda i: (0, 0), pipeline_mode=pl.Buffered(1))
    return pl.pallas_call(
        kernel,
        grid=(4,),
        in_specs=[pl.BlockSpec((256, width), lambda i: (i, 0)), head, head],
        out_specs=pl.BlockSpec((4, 256), lambda i: (0, 0)),
        out_shape=jax.ShapeDtypeStruct((4, 256), F32),
        compiler_params=pltpu.CompilerParams(vmem_limit_bytes=50 << 20),
        name="logits",
    )(rows, own_head, other_head)


def shards(
    block_states,
    token_ids,
    accept,
    cache_lengths,
    cache_keys,
    cache_values,
    w_query,
    w_key,
    w_value,
    w_out,
    attn_gain,
    final_gain,
    embed,
    lm_head,
):
    tok = lax.axis_index("tok")
    other_head = lax.ppermute(lm_head, "head", [(i, i ^ 1) for i in range(16)])
    cache_here = cache_keys.shape[0]
    offsets = jnp.cumsum(cache_lengths) - cache_lengths - tok * cache_here
    begins = jnp.clip(offsets, 0, cache_here)
    ends = jnp.clip(offsets + cache_lengths, 0, cache_here)
    attn_gain = attn_gain.reshape(1, -1)
    final_gain = final_gain.reshape(1, -1)

    vocab_here = embed.shape[0]
    local_ids = token_ids - tok * vocab_here
    inside = (local_ids >= 0) & (local_ids < vocab_here)
    looked_up = jnp.take(embed, jnp.clip(local_ids, 0, vocab_here - 1), axis=0)
    looked_up = jnp.where(inside[:, None], looked_up, jnp.zeros_like(looked_up))

    (feat1,), (came,) = comm(
        [gather_features(block_states), exchange_tok(looked_up.reshape(8, 256, 256))], 0, "comm_a"
    )
    q1, k1, v1 = project(feat1, w_query, w_key, w_value)
    embedded = jnp.sum(came.astype(F32), axis=0).astype(BF)
    swapped = jnp.where((accept == 1)[:, None], embedded, block_states)

    (qs1,), (feat2,) = comm([gather_queries(q1), gather_features(swapped)], 1, "comm_b")
    part1, stat1 = cached_attention(begins, ends, qs1, cache_keys, cache_values)
    q2, k2, v2 = project(feat2, w_query, w_key, w_value)

    (part1, stat1), (qs2,) = comm([exchange_tok(part1, stat1), gather_queries(q2)], 2, "comm_c")
    sum1 = combine(part1, stat1, q1, k1, v1, w_out)
    part2, stat2 = cached_attention(begins, ends, qs2, cache_keys, cache_values)

    (normed, squares), (part2, stat2) = comm(
        [reduce_layer(sum1, feat1, attn_gain, final_gain, True), exchange_tok(part2, stat2)],
        3,
        "comm_d",
    )
    sum2 = combine(part2, stat2, q2, k2, v2, w_out)

    (rows,), (hiddens,) = comm(
        [gather_all(normed), reduce_layer(sum2, feat2, attn_gain, None, False)], 4, "comm_e"
    )
    best = best_logits(rows.reshape(-1, rows.shape[-1]), lm_head, other_head)
    ((top, sums),) = comm([reduce_best(best, squares)], 5, "comm_f")
    top_logits = top[:, :4].reshape(2, 64, 16).transpose(1, 0, 2).reshape(-1)
    request_norms = jnp.sqrt(sums[4, :8] / (256 * 4096))
    return (hiddens, request_norms, top_logits)


def solution(mesh):
    placed = (
        P("tok", "head"),
        P(),
        P("tok"),
        P(),
        P("tok", "head"),
        P("tok", "head"),
        P(None, "head"),
        P(None, "head"),
        P(None, "head"),
        P("head", None),
        P(),
        P(),
        P("tok", "head"),
        P(("tok", "head"), None),
    )
    return jax.shard_map(
        shards,
        mesh=mesh,
        in_specs=placed,
        out_specs=(P(("tok", "head"), None), P(), P()),
        check_vma=False,
    )
```

```python
import math

import jax
import jax.numpy as jnp
from jax import lax
from jax.experimental import pallas as pl
from jax.experimental.pallas import tpu as pltpu
from jax.sharding import PartitionSpec as P

HEAD_DIM = 128
EPSILON = 1e-06
NEG = -1e30
SCALE2 = (1.0 / math.sqrt(HEAD_DIM)) * math.log2(math.e)
MESH = pl.DeviceIdType.MESH
BF = jnp.bfloat16
F32 = jnp.float32
ANY = pl.BlockSpec(memory_space=pl.ANY)
VM = pl.BlockSpec(memory_space=pltpu.VMEM)
REL8 = ((0, 2), (1, 2), (1, 1), (1, 3), (0, 1), (0, 3), (1, 0))


def coords():
    t = lax.axis_index("tok")
    h = lax.axis_index("head")
    return t // 2, lax.rem(t, 2), h // 8, lax.rem(h // 2, 4), lax.rem(h, 2)


def place(z, xl, xh, y, c):
    return (z * 2 + xl, xh * 8 + y * 2 + c)


def ring(v, d):
    return lax.rem(v + d, 4)


class Links:
    def __init__(self, send, recv):
        self.send, self.recv, self.used = send, recv, 0

    def copy(self, src, dst, device):
        k = self.used
        self.used += 1
        cp = pltpu.make_async_remote_copy(
            src_ref=src,
            dst_ref=dst,
            send_sem=self.send.at[k],
            recv_sem=self.recv.at[k],
            device_id=device,
            device_id_type=MESH,
        )
        cp.start()
        return cp


class Task:
    def __init__(self, body, ins, outs, scratch, copies, local, peers):
        self.body, self.ins, self.outs = body, ins, outs
        self.scratch = list(scratch) + [
            pltpu.SemaphoreType.DMA((copies,)),
            pltpu.SemaphoreType.DMA((copies,)),
            pltpu.SemaphoreType.DMA((max(local, 1),)),
        ]
        self.peers = peers


def shift(dx, dy, dz, dc):
    z, xl, xh, y, c = coords()
    c_ = lax.rem(c + dc, 2)
    if dx == "s":
        return place(ring(z, dz), 1 - xl, xh, ring(y, dy), c_)
    x_ = ring(xh * 2 + xl, dx)
    return place(ring(z, dz), lax.rem(x_, 2), x_ // 2, ring(y, dy), c_)


HEAD_AG = [(0, 0, 0, 1), (2, 0, 0, 0), (0, 1, 0, 0), (0, 2, 0, 0), (0, 3, 0, 0)]
HEAD_ALL = [(0, 0, 0, 1)] + [(2 * dx, dy, 0, 0) for dx, dy in REL8]
TOK_AG = [("s", 0, 0, 0), (0, 0, 1, 0), (0, 0, 2, 0), (0, 0, 3, 0)]
TOK_ALL = [("s" if dx else 0, 0, dz, 0) for dx, dz in REL8]
AXES = [(d, 0, 0, 0) for d in (1, 2, 3)] + [(0, d, 0, 0) for d in (1, 2, 3)]
AXES += [(0, 0, d, 0) for d in (1, 2, 3)]
PLANE = [(k // 4, k % 4, 0, 0) for k in range(1, 16)]
DEEP = [(0, 0, k % 4, k // 4) for k in range(1, 8)]


def comm(tasks, cid, name, vmem=4):
    n_in = [len(t.ins) for t in tasks]
    n_out = [len(t.outs) for t in tasks]
    n_scr = [len(t.scratch) for t in tasks]

    def kernel(*refs):
        ins, rest = refs[: sum(n_in)], refs[sum(n_in) :]
        outs, scr = rest[: sum(n_out)], rest[sum(n_out) :]
        peers = {}
        for t in tasks:
            for key in t.peers:
                peers.setdefault(key, shift(*key))
        barrier = pltpu.get_barrier_semaphore()
        for device in peers.values():
            pl.semaphore_signal(barrier, inc=1, device_id=device, device_id_type=MESH)
        pl.semaphore_wait(barrier, len(peers))
        running, a, b, c = [], 0, 0, 0
        for k, t in enumerate(tasks):
            running.append(
                t.body(
                    ins[a : a + n_in[k]], outs[b : b + n_out[k]], scr[c : c + n_scr[k]]
                )
            )
            a, b, c = a + n_in[k], b + n_out[k], c + n_scr[k]
        while running:
            again = []
            for g in running:
                if next(g, StopIteration) is not StopIteration:
                    again.append(g)
            running = again

    flat = pl.pallas_call(
        kernel,
        out_shape=[o[0] for t in tasks for o in t.outs],
        in_specs=[i[1] for t in tasks for i in t.ins],
        out_specs=[o[1] for t in tasks for o in t.outs],
        scratch_shapes=[s for t in tasks for s in t.scratch],
        compiler_params=pltpu.CompilerParams(
            collective_id=cid, has_side_effects=True, vmem_limit_bytes=vmem << 20
        ),
        name=name,
    )(*[i[0] for t in tasks for i in t.ins])
    res, b = [], 0
    for n in n_out:
        res.append(flat[b : b + n])
        b += n
    return res


def gather_features(x):
    def body(ins, outs, scr):
        (x_ref,), (f_ref,), (send, recv, loc) = ins, outs, scr
        z, xl, xh, y, c = coords()
        links = Links(send, recv)

        def cols(xh_, y_, c_):
            return f_ref.at[xh_ * 8 + y_ * 2 + c_]

        core = place(z, xl, xh, y, 1 - c)
        own = cols(xh, y, c)
        keep = pltpu.make_async_copy(x_ref, own, loc.at[0])
        keep.start()
        sent, landed = [], []
        over_x = links.copy(x_ref, own, place(z, xl, 1 - xh, y, c))
        over_y = {d: links.copy(x_ref, own, place(z, xl, xh, ring(y, d), c)) for d in (2, 1, 3)}
        landed.append(links.copy(x_ref, own, core))
        yield 0
        over_x.wait_recv()
        far = cols(1 - xh, y, c)
        far_y = {d: links.copy(far, far, place(z, xl, xh, ring(y, d), c)) for d in (2, 1, 3)}
        landed.append(links.copy(far, far, core))
        yield 0
        for d in (1, 3, 2):
            over_y[d].wait_recv()
            got = cols(xh, ring(y, 4 - d), c)
            landed.append(links.copy(got, got, core))
        yield 0
        for d in (1, 3, 2):
            far_y[d].wait_recv()
            got = cols(1 - xh, ring(y, 4 - d), c)
            landed.append(links.copy(got, got, core))
        yield 0
        keep.wait()
        for cp in [over_x] + list(over_y.values()) + list(far_y.values()):
            cp.wait_send()
        for cp in landed:
            cp.wait()

    return Task(
        body, [(x, ANY)], [(jax.ShapeDtypeStruct((16, 256, 256), BF), ANY)], [], 15, 1, HEAD_AG
    )


def gather_queries(q):
    def body(ins, outs, scr):
        (q_ref,), (o_ref,), (send, recv, loc) = ins, outs, scr
        z, xl, xh, y, c = coords()
        links = Links(send, recv)
        own = o_ref.at[z * 2 + xl]
        keep = pltpu.make_async_copy(q_ref, own, loc.at[0])
        keep.start()
        over_x = links.copy(q_ref, own, place(z, 1 - xl, xh, y, c))
        over_z = [links.copy(q_ref, own, place(ring(z, d), xl, xh, y, c)) for d in (2, 1, 3)]
        yield 0
        over_x.wait_recv()
        far = o_ref.at[z * 2 + 1 - xl]
        over_z += [links.copy(far, far, place(ring(z, d), xl, xh, y, c)) for d in (2, 1, 3)]
        yield 0
        over_x.wait_send()
        for cp in over_z:
            cp.wait()
        keep.wait()

    return Task(
        body, [(q, ANY)], [(jax.ShapeDtypeStruct((8, 256, 256), BF), ANY)], [], 7, 1, TOK_AG
    )


def exchange_tok(*arrays):
    def body(ins, outs, scr):
        send, recv, loc = scr
        z, xl, xh, y, c = coords()
        t = z * 2 + xl
        links = Links(send, recv)
        keep, cps = [], []
        for k, (src, dst) in enumerate(zip(ins, outs)):
            keep.append(pltpu.make_async_copy(src.at[t], dst.at[t], loc.at[k]))
            keep[-1].start()
        for dx, dz in REL8:
            z_, xl_ = ring(z, dz), lax.rem(xl + dx, 2)
            for src, dst in zip(ins, outs):
                cps.append(links.copy(src.at[z_ * 2 + xl_], dst.at[t], place(z_, xl_, xh, y, c)))
        yield 0
        for cp in cps:
            cp.wait()
        for cp in keep:
            cp.wait()

    n = len(arrays)
    return Task(
        body,
        [(a, ANY) for a in arrays],
        [(jax.ShapeDtypeStruct(a.shape, a.dtype), ANY) for a in arrays],
        [],
        7 * n,
        n,
        TOK_ALL,
    )


def unit_rows(v):
    return v * lax.rsqrt(jnp.mean(v * v, axis=-1, keepdims=True) + EPSILON)


def reduce_layer(part, features, attn_gain, final_gain, first, y_first):
    def body(ins, outs, scr):
        part_ref, f_ref, again_ref = ins[:3]
        mine, theirs, came, far, xrow, send, recv, loc = scr
        z, xl, xh, y, c = coords()
        h = xh * 8 + y * 2 + c
        links = Links(send, recv)
        l0 = pltpu.make_async_copy(part_ref.at[:, :, c], mine, loc.at[0])
        l1 = pltpu.make_async_copy(
            f_ref.at[:, pl.ds(pl.multiple_of(h * 16, 16), 16), :], xrow, loc.at[1]
        )
        swap = links.copy(part_ref.at[:, :, 1 - c], theirs, place(z, xl, xh, y, 1 - c))
        l0.start()
        l1.start()
        yield 0
        l0.wait()
        swap.wait_recv()
        cps = []

        def both(xh_, y_):
            return mine[xh_, y_].astype(F32) + theirs[xh_, y_].astype(F32)

        if y_first:
            for dy in (2, 1, 3):
                y_ = ring(y, dy)
                for xh_ in (0, 1):
                    mine[xh_, y_] = both(xh_, y_).astype(BF)
                cps.append(links.copy(mine.at[:, y_], came.at[:, y], place(z, xl, xh, y_, c)))
            total, away = both(xh, y), both(1 - xh, y)
            yield 0
            for cp in cps:
                cp.wait_recv()
            for dy in (1, 3, 2):
                y_ = ring(y, dy)
                away = away + came[1 - xh, y_].astype(F32)
                total = total + came[xh, y_].astype(F32)
            mine[1 - xh, y] = away.astype(BF)
            over = links.copy(mine.at[1 - xh, y], far, place(z, xl, 1 - xh, y, c))
            yield 0
            over.wait()
            total = total + far[...].astype(F32)
            for cp in cps:
                cp.wait_send()
        else:
            for dx, dy in REL8:
                xh_, y_ = lax.rem(xh + dx, 2), ring(y, dy)
                mine[xh_, y_] = both(xh_, y_).astype(BF)
                cps.append(
                    links.copy(mine.at[xh_, y_], came.at[xh, y], place(z, xl, xh_, y_, c))
                )
            total = both(xh, y)
            yield 0
            for cp in cps:
                cp.wait()
            for dx, dy in REL8:
                total = total + came[lax.rem(xh + dx, 2), ring(y, dy)].astype(F32)
        swap.wait_send()
        l1.wait()
        before = jnp.concatenate([xrow[k] for k in range(16)], axis=1).astype(F32)
        states = (before + unit_rows(total) * again_ref[...]).astype(BF)
        if not first:
            outs[0][...] = states
            return
        wide = states.astype(F32)
        squares = jnp.sum(wide * wide, axis=-1, keepdims=True)
        normed = wide * lax.rsqrt(squares * (1.0 / 4096) + EPSILON) * ins[3][...]
        outs[0][...] = normed.astype(BF)
        lane = lax.broadcasted_iota(jnp.int32, (8, 256), 1)
        row = lax.broadcasted_iota(jnp.int32, (8, 256), 0)
        outs[1][...] = jnp.where((lane == z * 2 + xl) & (row == 4), jnp.sum(squares), 0.0)

    ins = [(part, ANY), (features, ANY), (attn_gain, VM)]
    outs = [(jax.ShapeDtypeStruct((16, 4096), BF), VM)]
    if first:
        ins.append((final_gain, VM))
        outs.append((jax.ShapeDtypeStruct((8, 256), F32), VM))
    block = pltpu.VMEM((2, 4, 16, 4096), BF)
    scratch = [block, block, block, pltpu.VMEM((16, 4096), BF), pltpu.VMEM((16, 16, 256), BF)]
    return Task(body, ins, outs, scratch, 8, 2, HEAD_AG if y_first else HEAD_ALL)


def along(axis, d):
    return shift(*{"x": (d, 0, 0, 0), "y": (0, d, 0, 0), "z": (0, 0, d, 0)}[axis])


CHUNKS = ((384, 384, 256), (384, 256, 384), (256, 384, 384), (384, 384, 256))
ORDERS = ("xyz", "yzx", "zxy")


def gather_logits(normed, own_head, other_head):
    vocab = own_head.shape[0]

    def body(ins, outs, scr):
        n_ref, own_ref, other_ref = ins
        (best_ref,) = outs
        bufs = [scr[3 * i : 3 * i + 3] for i in range(4)]
        heads, acc, send, recv, loc = scr[12:]
        z, xl, xh, y, c = coords()
        x = xh * 2 + xl
        links = Links(send, recv)
        full = slice(None)
        loads = [
            pltpu.make_async_copy(src, heads.at[k], loc.at[k])
            for k, src in enumerate((own_ref, other_ref))
        ]

        def block(i, p, known, step=0, half=None):
            last = ORDERS[p][2]
            z_, y_, x_ = z, y, x
            if step:
                if last == "z":
                    z_ = ring(z, step)
                elif last == "y":
                    y_ = ring(y, step)
                else:
                    x_ = ring(x, step)
            at = [
                full if "z" in known else z_,
                full if "x" in known else lax.rem(x_, 2),
                full if "x" in known else x_ // 2,
                full if "y" in known else y_,
            ]
            if half is not None:
                if last == "z":
                    at[1] = half
                else:
                    at[0] = pl.ds(2 * half, 2)
            return bufs[i][p].at[tuple(at)]

        start = 0
        for i in range(4):
            for p in range(3):
                bufs[i][p][z, xl, xh, y] = n_ref[:, start : start + CHUNKS[i][p]]
                start += CHUNKS[i][p]

        everything = []

        def push(i, p, ref, axis, d):
            cp = links.copy(ref, ref, along(axis, d))
            everything.append(cp)
            return cp

        def spread(i, stage, before):
            out = []
            for p in range(3):
                if before is not None:
                    for cp in before[p]:
                        cp.wait_recv()
                ref = block(i, p, ORDERS[p][:stage])
                ds = (2, 1, 3) if stage < 2 else (1, 3)
                out.append([push(i, p, ref, ORDERS[p][stage], d) for d in ds])
            return out

        def relay(i, before):
            out = []
            for p in range(3):
                axis, known = ORDERS[p][2], ORDERS[p][:2]
                before[p][0].wait_recv()
                lower = push(i, p, block(i, p, known, 3, 0), axis, 1)
                before[p][1].wait_recv()
                upper = push(i, p, block(i, p, known, 1, 1), axis, 3)
                out.append([lower, upper])
            return out

        def multiply(i):
            cut = pl.ds(1024 * i, 1024)

            def step(r, carry):
                rows = jnp.concatenate(
                    [bufs[i][p][r].reshape(256, CHUNKS[i][p]) for p in range(3)], axis=1
                )
                top = None
                for k in range(2):
                    part = lax.dot_general(
                        heads[k, :, cut], rows, (((1,), (1,)), ((), ())), preferred_element_type=F32
                    )
                    if i > 0:
                        part = acc[k, r] + part
                    if i < 3:
                        acc[k, r] = part
                    else:
                        m = jnp.max(part, axis=0, keepdims=True)
                        top = m if top is None else jnp.maximum(top, m)
                if i == 3:
                    best_ref[pl.ds(r, 1), :] = top
                return carry

            lax.fori_loop(0, 4, step, 0)

        one = [spread(i, 0, None) for i in range(4)]
        for cp in loads:
            cp.start()
        two = [spread(i, 1, one[i]) for i in range(4)]
        three = {0: spread(0, 2, two[0]), 1: spread(1, 2, two[1])}
        four = {0: relay(0, three[0])}
        for i in range(4):
            if i + 1 < 4:
                four[i + 1] = relay(i + 1, three[i + 1])
            if i + 2 < 4:
                three[i + 2] = spread(i + 2, 2, two[i + 2])
            for pair in four[i]:
                for cp in pair:
                    cp.wait_recv()
            if i == 0:
                for cp in loads:
                    cp.wait()
            multiply(i)
        for cp in everything:
            cp.wait_send()
        yield 0

    scratch = [pltpu.VMEM((4, 2, 2, 4, 16, w), BF) for ws in CHUNKS for w in ws]
    scratch += [pltpu.VMEM((2, vocab, 4096), BF), pltpu.VMEM((2, 4, vocab, 256), F32)]
    return Task(
        body,
        [(normed, VM), (own_head, ANY), (other_head, ANY)],
        [(jax.ShapeDtypeStruct((4, 256), F32), VM)],
        scratch,
        4 * 3 * 10,
        2,
        AXES,
    )


def reduce_best(best, squares):
    def body(ins, outs, scr):
        best_ref, sq_ref = ins
        out_ref, sum_ref = outs
        held, wide, deep, send, recv, loc = scr
        z, xl, xh, y, c = coords()
        links = Links(send, recv)
        held[0] = sq_ref[...]
        held[0, pl.ds(0, 4), :] = best_ref[...]
        top = lax.broadcasted_iota(jnp.int32, (8, 256), 0) < 4

        def join(v, w):
            return jnp.where(top, jnp.maximum(v, w), v + w)

        cps = [links.copy(held.at[0], wide.at[k], shift(*key)) for k, key in enumerate(PLANE)]
        yield 0
        for cp in cps:
            cp.wait()
        mine = held[0]
        for k in range(15):
            mine = join(mine, wide[k])
        held[1] = mine
        cps = [links.copy(held.at[1], deep.at[k], shift(*key)) for k, key in enumerate(DEEP)]
        yield 0
        for cp in cps:
            cp.wait()
        for k in range(3):
            mine = join(mine, deep[k])
        theirs = deep[3]
        for k in range(4, 7):
            theirs = join(theirs, deep[k])
        out_ref[c] = mine
        out_ref[1 - c] = theirs
        sum_ref[...] = mine + theirs

    return Task(
        body,
        [(best, VM), (squares, VM)],
        [
            (jax.ShapeDtypeStruct((2, 8, 256), F32), VM),
            (jax.ShapeDtypeStruct((8, 256), F32), VM),
        ],
        [
            pltpu.VMEM((2, 8, 256), F32),
            pltpu.VMEM((15, 8, 256), F32),
            pltpu.VMEM((7, 8, 256), F32),
        ],
        22,
        1,
        PLANE + DEEP,
    )


def project(x, w_query, w_key, w_value):
    steps = 4
    slots, rows, wide = x.shape
    per = slots // steps
    depth = per * wide

    def kernel(x_ref, a_ref, b_ref, c_ref, q_ref, k_ref, v_ref, acc):
        i = pl.program_id(0)
        xs = jnp.concatenate([x_ref[s] for s in range(per)], axis=1)
        for n, (w_ref, o_ref) in enumerate(((a_ref, q_ref), (b_ref, k_ref), (c_ref, v_ref))):
            part = jnp.dot(xs, w_ref[...], preferred_element_type=F32)

            @pl.when(i == 0)
            def _():
                acc[n] = part

            @pl.when((i > 0) & (i < steps - 1))
            def _():
                acc[n] += part

            @pl.when(i == steps - 1)
            def _():
                o_ref[...] = (acc[n] + part).astype(BF)

    weight = pl.BlockSpec((depth, wide), lambda i: (i, 0))
    out = pl.BlockSpec((rows, wide), lambda i: (0, 0))
    return pl.pallas_call(
        kernel,
        grid=(steps,),
        in_specs=[pl.BlockSpec((per, rows, wide), lambda i: (i, 0, 0)), weight, weight, weight],
        out_specs=[out] * 3,
        out_shape=[jax.ShapeDtypeStruct((rows, wide), BF)] * 3,
        scratch_shapes=[pltpu.VMEM((3, rows, wide), F32)],
        compiler_params=pltpu.CompilerParams(vmem_limit_bytes=24 << 20),
        name="project",
    )(x, w_query, w_key, w_value)


def scores(q, k):
    return lax.dot_general(q, k, (((1,), (1,)), ((), ())), preferred_element_type=F32) * SCALE2


def cached_attention(begins, ends, queries, keys, values):
    rows = queries.shape[1]
    span = 256

    def kernel(lo_ref, hi_ref, q_ref, k_ref, v_ref, o_ref, s_ref, m_sc, l_sc, a_sc):
        r = pl.program_id(0)
        lo, hi = lo_ref[r], hi_ref[r]
        m_sc[...] = jnp.full_like(m_sc, NEG)
        l_sc[...] = jnp.zeros_like(l_sc)
        a_sc[...] = jnp.zeros_like(a_sc)

        @pl.when(hi > lo)
        def _():
            def step(b, carry):
                at = pl.multiple_of(b * span, span)
                pos = at + lax.broadcasted_iota(jnp.int32, (rows, span), 1)
                valid = (pos >= lo) & (pos < hi)
                for g in range(2):
                    cut = slice(g * HEAD_DIM, (g + 1) * HEAD_DIM)
                    s = scores(q_ref[0, :, cut], k_ref[pl.ds(at, span), cut])
                    s = jnp.where(valid, s, NEG)
                    old = m_sc[g, :, 0:1]
                    new = jnp.maximum(old, jnp.max(s, axis=-1, keepdims=True))
                    p = jnp.where(valid, jnp.exp2(s - new), 0.0)
                    f = jnp.exp2(old - new)
                    l_sc[g] = l_sc[g] * f + jnp.sum(p, axis=-1, keepdims=True)
                    a_sc[g] = a_sc[g] * f + jnp.dot(
                        p.astype(BF), v_ref[pl.ds(at, span), cut], preferred_element_type=F32
                    )
                    m_sc[g] = jnp.broadcast_to(new, m_sc.shape[1:])
                return carry

            lax.fori_loop(lo // span, (hi + span - 1) // span, step, 0)

        lane = lax.broadcasted_iota(jnp.int32, (rows, 128), 1)
        stats = jnp.where(lane == 0, m_sc[0], jnp.where(lane == 1, m_sc[1], 0.0))
        stats = jnp.where(lane == 2, l_sc[0], jnp.where(lane == 3, l_sc[1], stats))
        s_ref[0] = jnp.transpose(stats)[:8]
        for g in range(2):
            o_ref[0, :, g * HEAD_DIM : (g + 1) * HEAD_DIM] = a_sc[g].astype(BF)

    whole = pl.BlockSpec(keys.shape, lambda r, a, b: (0, 0))
    per = pl.BlockSpec((1, rows, 256), lambda r, a, b: (r, 0, 0))
    return pl.pallas_call(
        kernel,
        grid_spec=pltpu.PrefetchScalarGridSpec(
            num_scalar_prefetch=2,
            grid=(8,),
            in_specs=[per, whole, whole],
            out_specs=[per, pl.BlockSpec((1, 8, rows), lambda r, a, b: (r, 0, 0))],
            scratch_shapes=[
                pltpu.VMEM((2, rows, 128), F32),
                pltpu.VMEM((2, rows, 128), F32),
                pltpu.VMEM((2, rows, HEAD_DIM), F32),
            ],
        ),
        out_shape=[
            jax.ShapeDtypeStruct((8, rows, 256), BF),
            jax.ShapeDtypeStruct((8, 8, rows), F32),
        ],
        compiler_params=pltpu.CompilerParams(vmem_limit_bytes=32 << 20),
        name="cached",
    )(begins, ends, queries, keys, values)


def combine(parts, stats, q, k, v, w_out):
    steps = 4
    wide = w_out.shape[1] // steps

    def kernel(p_ref, s_ref, q_ref, k_ref, v_ref, w_ref, o_ref, att):
        @pl.when(pl.program_id(0) == 0)
        def _():
            st = jnp.concatenate([s_ref[...].reshape(64, 256), jnp.zeros((64, 256), F32)], axis=0)
            st = jnp.transpose(st)
            for g in range(2):
                cut = slice(g * HEAD_DIM, (g + 1) * HEAD_DIM)
                s = scores(q_ref[:, cut], k_ref[:, cut])
                top = jnp.max(s, axis=-1, keepdims=True)
                for i in range(8):
                    top = jnp.maximum(top, st[:, i * 8 + g : i * 8 + g + 1])
                p = jnp.exp2(s - top)
                mass = jnp.sum(p, axis=-1, keepdims=True)
                acc = jnp.dot(p.astype(BF), v_ref[:, cut], preferred_element_type=F32)
                for i in range(8):
                    f = jnp.exp2(st[:, i * 8 + g : i * 8 + g + 1] - top)
                    mass = mass + f * st[:, i * 8 + g + 2 : i * 8 + g + 3]
                    acc = acc + f * p_ref[i, :, cut].astype(F32)
                att[:, cut] = (acc / mass).astype(BF)

        o = jnp.dot(att[...], w_ref[...], preferred_element_type=F32).astype(BF)
        o_ref[...] = o.reshape(o_ref.shape)

    def whole(a):
        return pl.BlockSpec(a.shape, lambda i: (0,) * a.ndim)

    return pl.pallas_call(
        kernel,
        grid=(steps,),
        in_specs=[whole(a) for a in (parts, stats, q, k, v)]
        + [pl.BlockSpec((256, wide), lambda i: (0, i))],
        out_specs=pl.BlockSpec((2, 4, 2, 16, wide), lambda i: (0, 0, 0, 0, i)),
        out_shape=jax.ShapeDtypeStruct((2, 4, 2, 16, w_out.shape[1]), BF),
        scratch_shapes=[pltpu.VMEM((256, 256), BF)],
        compiler_params=pltpu.CompilerParams(vmem_limit_bytes=32 << 20),
        name="combine",
    )(parts, stats, q, k, v, w_out)


def shards(
    block_states,
    token_ids,
    accept,
    cache_lengths,
    cache_keys,
    cache_values,
    w_query,
    w_key,
    w_value,
    w_out,
    attn_gain,
    final_gain,
    embed,
    lm_head,
):
    tok = lax.axis_index("tok")
    other_head = lax.ppermute(lm_head, "head", [(i, i ^ 1) for i in range(16)])
    cache_here = cache_keys.shape[0]
    offsets = jnp.cumsum(cache_lengths) - cache_lengths - tok * cache_here
    begins = jnp.clip(offsets, 0, cache_here)
    ends = jnp.clip(offsets + cache_lengths, 0, cache_here)
    attn_gain = attn_gain.reshape(1, -1)
    final_gain = final_gain.reshape(1, -1)

    vocab_here = embed.shape[0]
    local_ids = token_ids - tok * vocab_here
    inside = (local_ids >= 0) & (local_ids < vocab_here)
    looked_up = jnp.take(embed, jnp.clip(local_ids, 0, vocab_here - 1), axis=0)
    looked_up = jnp.where(inside[:, None], looked_up, jnp.zeros_like(looked_up))

    (feat1,), (came,) = comm(
        [gather_features(block_states), exchange_tok(looked_up.reshape(8, 256, 256))], 0, "comm_a"
    )
    q1, k1, v1 = project(feat1, w_query, w_key, w_value)
    embedded = jnp.sum(came.astype(F32), axis=0).astype(BF)
    swapped = jnp.where((accept == 1)[:, None], embedded, block_states)

    (qs1,), (feat2,) = comm([gather_queries(q1), gather_features(swapped)], 1, "comm_b")
    part1, stat1 = cached_attention(begins, ends, qs1, cache_keys, cache_values)
    q2, k2, v2 = project(feat2, w_query, w_key, w_value)

    (part1, stat1), (qs2,) = comm([exchange_tok(part1, stat1), gather_queries(q2)], 2, "comm_c")
    sum1 = combine(part1, stat1, q1, k1, v1, w_out)
    part2, stat2 = cached_attention(begins, ends, qs2, cache_keys, cache_values)

    (normed, squares), (part2, stat2) = comm(
        [
            reduce_layer(sum1, feat1, attn_gain, final_gain, True, True),
            exchange_tok(part2, stat2),
        ],
        3,
        "comm_d",
        12,
    )
    sum2 = combine(part2, stat2, q2, k2, v2, w_out)

    ((best,),) = comm([gather_logits(normed, lm_head, other_head)], 4, "comm_e", 48)
    (top, sums), (hiddens,) = comm(
        [reduce_best(best, squares), reduce_layer(sum2, feat2, attn_gain, None, False, False)],
        5,
        "comm_f",
        12,
    )
    top_logits = top[:, :4].reshape(2, 64, 16).transpose(1, 0, 2).reshape(-1)
    request_norms = jnp.sqrt(sums[4, :8] / (256 * 4096))
    return (hiddens, request_norms, top_logits)


def solution(mesh):
    placed = (
        P("tok", "head"),
        P(),
        P("tok"),
        P(),
        P("tok", "head"),
        P("tok", "head"),
        P(None, "head"),
        P(None, "head"),
        P(None, "head"),
        P("head", None),
        P(),
        P(),
        P("tok", "head"),
        P(("tok", "head"), None),
    )
    return jax.shard_map(
        shards,
        mesh=mesh,
        in_specs=placed,
        out_specs=(P(("tok", "head"), None), P(), P()),
        check_vma=False,
    )
```

```python
import math

import jax
import jax.numpy as jnp
from jax import lax
from jax.experimental import pallas as pl
from jax.experimental.pallas import tpu as pltpu
from jax.sharding import PartitionSpec as P

HEAD_DIM = 128
EPSILON = 1e-06
NEG = -1e30
SCALE2 = (1.0 / math.sqrt(HEAD_DIM)) * math.log2(math.e)
MESH = pl.DeviceIdType.MESH
BF = jnp.bfloat16
F32 = jnp.float32
ANY = pl.BlockSpec(memory_space=pltpu.HBM)
VM = pl.BlockSpec(memory_space=pltpu.VMEM)
REL8 = ((0, 2), (1, 2), (1, 1), (1, 3), (0, 1), (0, 3), (1, 0))


def coords():
    t = lax.axis_index("tok")
    h = lax.axis_index("head")
    return t // 2, lax.rem(t, 2), h // 8, lax.rem(h // 2, 4), lax.rem(h, 2)


def place(z, xl, xh, y, c):
    return (z * 2 + xl, xh * 8 + y * 2 + c)


def ring(v, d):
    return lax.rem(v + d, 4)


class Links:
    def __init__(self, send, recv):
        self.send, self.recv, self.used = send, recv, 0

    def copy(self, src, dst, device):
        k = self.used
        self.used += 1
        cp = pltpu.make_async_remote_copy(
            src_ref=src,
            dst_ref=dst,
            send_sem=self.send.at[k],
            recv_sem=self.recv.at[k],
            device_id=device,
            device_id_type=MESH,
        )
        cp.start()
        return cp


class Task:
    def __init__(self, body, ins, outs, scratch, copies, local, peers):
        self.body, self.ins, self.outs = body, ins, outs
        self.scratch = list(scratch) + [
            pltpu.SemaphoreType.DMA((copies,)),
            pltpu.SemaphoreType.DMA((copies,)),
            pltpu.SemaphoreType.DMA((max(local, 1),)),
        ]
        self.peers = peers


def shift(dx, dy, dz, dc):
    z, xl, xh, y, c = coords()
    c_ = lax.rem(c + dc, 2)
    if dx == "s":
        return place(ring(z, dz), 1 - xl, xh, ring(y, dy), c_)
    x_ = ring(xh * 2 + xl, dx)
    return place(ring(z, dz), lax.rem(x_, 2), x_ // 2, ring(y, dy), c_)


HEAD_AG = [(0, 0, 0, 1), (2, 0, 0, 0), (0, 1, 0, 0), (0, 2, 0, 0), (0, 3, 0, 0)]
HEAD_ALL = [(0, 0, 0, 1)] + [(2 * dx, dy, 0, 0) for dx, dy in REL8]
TOK_AG = [("s", 0, 0, 0), (0, 0, 1, 0), (0, 0, 2, 0), (0, 0, 3, 0)]
TOK_ALL = [("s" if dx else 0, 0, dz, 0) for dx, dz in REL8]
AXES = [(d, 0, 0, 0) for d in (1, 2, 3)] + [(0, d, 0, 0) for d in (1, 2, 3)]
AXES += [(0, 0, d, 0) for d in (1, 2, 3)]
PLANE = [(k // 4, k % 4, 0, 0) for k in range(1, 16)]
DEEP = [(0, 0, k % 4, k // 4) for k in range(1, 8)]


def comm(tasks, cid, name, vmem=4):
    n_in = [len(t.ins) for t in tasks]
    n_out = [len(t.outs) for t in tasks]
    n_scr = [len(t.scratch) for t in tasks]

    def kernel(*refs):
        ins, rest = refs[: sum(n_in)], refs[sum(n_in) :]
        outs, scr = rest[: sum(n_out)], rest[sum(n_out) :]
        peers = {}
        for t in tasks:
            for key in t.peers:
                peers.setdefault(key, shift(*key))
        barrier = pltpu.get_barrier_semaphore()
        for device in peers.values():
            pl.semaphore_signal(barrier, inc=1, device_id=device, device_id_type=MESH)
        pl.semaphore_wait(barrier, len(peers))
        running, a, b, c = [], 0, 0, 0
        for k, t in enumerate(tasks):
            running.append(
                t.body(
                    ins[a : a + n_in[k]], outs[b : b + n_out[k]], scr[c : c + n_scr[k]]
                )
            )
            a, b, c = a + n_in[k], b + n_out[k], c + n_scr[k]
        while running:
            again = []
            for g in running:
                if next(g, StopIteration) is not StopIteration:
                    again.append(g)
            running = again

    flat = pl.pallas_call(
        kernel,
        out_shape=[o[0] for t in tasks for o in t.outs],
        in_specs=[i[1] for t in tasks for i in t.ins],
        out_specs=[o[1] for t in tasks for o in t.outs],
        scratch_shapes=[s for t in tasks for s in t.scratch],
        compiler_params=pltpu.CompilerParams(
            collective_id=cid, has_side_effects=True, vmem_limit_bytes=vmem << 20
        ),
        name=name,
    )(*[i[0] for t in tasks for i in t.ins])
    res, b = [], 0
    for n in n_out:
        res.append(flat[b : b + n])
        b += n
    return res


def gather_project(x, weights):
    rows, wide = x.shape

    def body(ins, outs, scr):
        x_ref, w_refs = ins[0], ins[1:]
        own_rows, outs = outs[0], outs[1:]
        f_ref, w_ref, acc, send, recv, loc = scr
        z, xl, xh, y, c = coords()
        links = Links(send, recv)

        def index(xh_, y_, c_):
            return xh_ * 8 + y_ * 2 + c_

        def slot(*at):
            return f_ref.at[index(*at)]

        def absorb(*at):
            k = index(*at)
            v = f_ref[k]
            for n in range(3):
                w = w_ref[n, pl.ds(pl.multiple_of(k * wide, wide), wide), :]
                acc[n] += jnp.dot(v, w, preferred_element_type=F32)

        core = place(z, xl, xh, y, 1 - c)
        own = slot(xh, y, c)
        keep = pltpu.make_async_copy(x_ref, own, loc.at[0])
        keep.start()
        landed = []
        over_x = links.copy(x_ref, own, place(z, xl, 1 - xh, y, c))
        over_y = {d: links.copy(x_ref, own, place(z, xl, xh, ring(y, d), c)) for d in (2, 1, 3)}
        landed.append(links.copy(x_ref, own, core))
        loads = [pltpu.make_async_copy(w_refs[n], w_ref.at[n], loc.at[1 + n]) for n in range(3)]
        for cp in loads:
            cp.start()
        acc[...] = jnp.zeros_like(acc)
        yield 0
        over_x.wait_recv()
        far = slot(1 - xh, y, c)
        far_y = {d: links.copy(far, far, place(z, xl, xh, ring(y, d), c)) for d in (2, 1, 3)}
        landed.append(links.copy(far, far, core))
        yield 0
        keep.wait()
        for cp in loads:
            cp.wait()
        absorb(xh, y, c)
        absorb(1 - xh, y, c)
        for k, xh_ in enumerate((xh, 1 - xh)):
            landed[k].wait_recv()
            absorb(xh_, y, 1 - c)
        yield 0
        for xh_, arrive in ((xh, over_y), (1 - xh, far_y)):
            for d in (1, 3, 2):
                y_ = ring(y, 4 - d)
                arrive[d].wait_recv()
                got = slot(xh_, y_, c)
                landed.append(links.copy(got, got, core))
                absorb(xh_, y_, c)
            for k, d in enumerate((1, 3, 2)):
                landed[k - 3].wait_recv()
                absorb(xh_, ring(y, 4 - d), 1 - c)
            yield 0
        h = pl.multiple_of(index(xh, y, c) * 16, 16)
        for k in range(16):
            own_rows[:, k * wide : (k + 1) * wide] = f_ref[k, pl.ds(h, 16), :]
        for n in range(3):
            outs[n][...] = acc[n].astype(BF)
        for cp in [over_x] + list(over_y.values()) + list(far_y.values()) + landed:
            cp.wait_send()

    return Task(
        body,
        [(x, ANY)] + [(w, ANY) for w in weights],
        [(jax.ShapeDtypeStruct((16, 16 * wide), BF), VM)]
        + [(jax.ShapeDtypeStruct((rows, wide), BF), VM)] * 3,
        [
            pltpu.VMEM((16, rows, wide), BF),
            pltpu.VMEM((3, 16 * wide, wide), BF),
            pltpu.VMEM((3, rows, wide), F32),
        ],
        15,
        4,
        HEAD_AG,
    )


def gather_queries(q):
    def body(ins, outs, scr):
        (q_ref,), (o_ref,), (send, recv, loc) = ins, outs, scr
        z, xl, xh, y, c = coords()
        links = Links(send, recv)
        own = o_ref.at[z * 2 + xl]
        keep = pltpu.make_async_copy(q_ref, own, loc.at[0])
        keep.start()
        over_x = links.copy(q_ref, own, place(z, 1 - xl, xh, y, c))
        over_z = [links.copy(q_ref, own, place(ring(z, d), xl, xh, y, c)) for d in (2, 1, 3)]
        yield 0
        over_x.wait_recv()
        far = o_ref.at[z * 2 + 1 - xl]
        over_z += [links.copy(far, far, place(ring(z, d), xl, xh, y, c)) for d in (2, 1, 3)]
        yield 0
        over_x.wait_send()
        for cp in over_z:
            cp.wait()
        keep.wait()

    return Task(
        body, [(q, ANY)], [(jax.ShapeDtypeStruct((8, 256, 256), BF), ANY)], [], 7, 1, TOK_AG
    )


def exchange_tok(*arrays):
    def body(ins, outs, scr):
        send, recv, loc = scr
        z, xl, xh, y, c = coords()
        t = z * 2 + xl
        links = Links(send, recv)
        keep, cps = [], []
        for k, (src, dst) in enumerate(zip(ins, outs)):
            keep.append(pltpu.make_async_copy(src.at[t], dst.at[t], loc.at[k]))
            keep[-1].start()
        for dx, dz in REL8:
            z_, xl_ = ring(z, dz), lax.rem(xl + dx, 2)
            for src, dst in zip(ins, outs):
                cps.append(links.copy(src.at[z_ * 2 + xl_], dst.at[t], place(z_, xl_, xh, y, c)))
        yield 0
        for cp in cps:
            cp.wait()
        for cp in keep:
            cp.wait()

    n = len(arrays)
    return Task(
        body,
        [(a, ANY) for a in arrays],
        [(jax.ShapeDtypeStruct(a.shape, a.dtype), ANY) for a in arrays],
        [],
        7 * n,
        n,
        TOK_ALL,
    )


def unit_rows(v):
    return v * lax.rsqrt(jnp.mean(v * v, axis=-1, keepdims=True) + EPSILON)


def reduce_layer(part, states_in, attn_gain, final_gain):
    first = final_gain is not None

    def body(ins, outs, scr):
        part_ref, x_ref, again_ref = ins[:3]
        mine, theirs, came, far, send, recv, loc = scr
        z, xl, xh, y, c = coords()
        links = Links(send, recv)
        cps = []
        if first:
            l0 = pltpu.make_async_copy(part_ref.at[:, :, c], mine, loc.at[0])
            l0.start()
            swap = links.copy(part_ref.at[:, :, 1 - c], theirs, place(z, xl, xh, y, 1 - c))
            yield 0
            l0.wait()
            swap.wait_recv()

            def both(xh_, y_):
                return mine[xh_, y_].astype(F32) + theirs[xh_, y_].astype(F32)

            for dy in (2, 1, 3):
                y_ = ring(y, dy)
                for xh_ in (0, 1):
                    mine[xh_, y_] = both(xh_, y_).astype(BF)
                cps.append(links.copy(mine.at[:, y_], came.at[:, y], place(z, xl, xh, y_, c)))
            total, away = both(xh, y), both(1 - xh, y)
            yield 0
            for cp in cps:
                cp.wait_recv()
            for dy in (1, 3, 2):
                y_ = ring(y, dy)
                away = away + came[1 - xh, y_].astype(F32)
                total = total + came[xh, y_].astype(F32)
            mine[1 - xh, y] = away.astype(BF)
            over = links.copy(mine.at[1 - xh, y], far, place(z, xl, 1 - xh, y, c))
            yield 0
            over.wait()
            total = total + far[...].astype(F32)
            for cp in cps:
                cp.wait_send()
            swap.wait_send()
        else:
            l0 = pltpu.make_async_copy(part_ref.at[xh, y], far, loc.at[0])
            l0.start()
            for dx, dy in REL8:
                xh_, y_ = lax.rem(xh + dx, 2), ring(y, dy)
                cps.append(
                    links.copy(part_ref.at[xh_, y_], came.at[xh, y], place(z, xl, xh_, y_, c))
                )
            yield 0
            yield 0
            l0.wait()
            total = far[...].astype(F32)
            for cp in cps:
                cp.wait()
            for dx, dy in REL8:
                total = total + came[lax.rem(xh + dx, 2), ring(y, dy)].astype(F32)
        states = (x_ref[...].astype(F32) + unit_rows(total) * again_ref[...]).astype(BF)
        if not first:
            outs[0][...] = states
            return
        wide = states.astype(F32)
        squares = jnp.sum(wide * wide, axis=-1, keepdims=True)
        normed = wide * lax.rsqrt(squares * (1.0 / 4096) + EPSILON) * ins[3][...]
        outs[0][...] = normed.astype(BF)
        lane = lax.broadcasted_iota(jnp.int32, (8, 256), 1)
        row = lax.broadcasted_iota(jnp.int32, (8, 256), 0)
        outs[1][...] = jnp.where((lane == z * 2 + xl) & (row == 4), jnp.sum(squares), 0.0)

    ins = [(part, ANY), (states_in, VM), (attn_gain, VM)]
    outs = [(jax.ShapeDtypeStruct((16, 4096), BF), VM)]
    if first:
        ins.append((final_gain, VM))
        outs.append((jax.ShapeDtypeStruct((8, 256), F32), VM))
    block = pltpu.VMEM((2, 4, 16, 4096), BF)
    scratch = [block, block, block, pltpu.VMEM((16, 4096), BF)]
    return Task(body, ins, outs, scratch, 8, 1, HEAD_AG if first else HEAD_ALL[1:])


def along(axis, d):
    return shift(*{"x": (d, 0, 0, 0), "y": (0, d, 0, 0), "z": (0, 0, d, 0)}[axis])


CHUNKS = ((384, 384, 256), (384, 256, 384), (256, 384, 384), (384, 384, 256))
ORDERS = ("xyz", "yzx", "zxy")


def gather_logits(normed, own_head, other_head, second):
    vocab = own_head.shape[0]

    def body(ins, outs, scr):
        n_ref, own_ref, other_ref = ins[:3]
        best_ref, sums_ref = outs
        bufs = [scr[3 * i : 3 * i + 3] for i in range(4)]
        heads, acc = scr[12:14]
        held = scr[14:20]
        att, out, theirs, sums, send, recv, loc = scr[20:]
        z, xl, xh, y, c = coords()
        x = xh * 2 + xl
        links = Links(send, recv)
        full = slice(None)
        loads = [
            pltpu.make_async_copy(src, heads.at[k], loc.at[k])
            for k, src in enumerate((own_ref, other_ref))
        ]

        def block(i, p, known, step=0, half=None):
            last = ORDERS[p][2]
            z_, y_, x_ = z, y, x
            if step:
                if last == "z":
                    z_ = ring(z, step)
                elif last == "y":
                    y_ = ring(y, step)
                else:
                    x_ = ring(x, step)
            at = [
                full if "z" in known else z_,
                full if "x" in known else lax.rem(x_, 2),
                full if "x" in known else x_ // 2,
                full if "y" in known else y_,
            ]
            if half is not None:
                if last == "z":
                    at[1] = half
                else:
                    at[0] = pl.ds(2 * half, 2)
            return bufs[i][p].at[tuple(at)]

        start = 0
        for i in range(4):
            for p in range(3):
                bufs[i][p][z, xl, xh, y] = n_ref[:, start : start + CHUNKS[i][p]]
                start += CHUNKS[i][p]

        everything = []

        def push(i, p, ref, axis, d):
            cp = links.copy(ref, ref, along(axis, d))
            everything.append(cp)
            return cp

        def spread(i, stage, before):
            out = []
            for p in range(3):
                if before is not None:
                    for cp in before[p]:
                        cp.wait_recv()
                ref = block(i, p, ORDERS[p][:stage])
                ds = (2, 1, 3) if stage < 2 else (1, 3)
                out.append([push(i, p, ref, ORDERS[p][stage], d) for d in ds])
            return out

        def relay(i, before):
            out = []
            for p in range(3):
                axis, known = ORDERS[p][2], ORDERS[p][:2]
                before[p][0].wait_recv()
                lower = push(i, p, block(i, p, known, 3, 0), axis, 1)
                before[p][1].wait_recv()
                upper = push(i, p, block(i, p, known, 1, 1), axis, 3)
                out.append([lower, upper])
            return out

        def multiply(i):
            cut = pl.ds(1024 * i, 1024)

            def step(r, carry):
                rows = jnp.concatenate(
                    [bufs[i][p][r].reshape(256, CHUNKS[i][p]) for p in range(3)], axis=1
                )
                top = None
                for k in range(2):
                    part = lax.dot_general(
                        heads[k, :, cut], rows, (((1,), (1,)), ((), ())), preferred_element_type=F32
                    )
                    if i > 0:
                        part = acc[k, r] + part
                    if i < 3:
                        acc[k, r] = part
                    else:
                        m = jnp.max(part, axis=0, keepdims=True)
                        top = m if top is None else jnp.maximum(top, m)
                if i == 3:
                    best_ref[pl.ds(r, 1), :] = top
                return carry

            lax.fori_loop(0, 4, step, 0)

        fetch = [
            pltpu.make_async_copy(src, dst, loc.at[2 + k])
            for k, (src, dst) in enumerate(zip(ins[3:], held))
        ]
        one = [spread(i, 0, None) for i in range(4)]
        for cp in fetch + loads:
            cp.start()
        two = [spread(i, 1, one[i]) for i in range(4)]
        three = {0: spread(0, 2, two[0]), 1: spread(1, 2, two[1])}
        for cp in fetch:
            cp.wait()
        attend(*held[:5], att)

        def times_out(k, carry):
            cut = pl.ds(pl.multiple_of(k * 1024, 1024), 1024)
            o = jnp.dot(att[...], held[5][:, cut], preferred_element_type=F32).astype(BF)
            out[:, :, :, :, cut] = o.reshape(2, 4, 2, 16, 1024)
            return carry

        lax.fori_loop(0, 4, times_out, 0)
        swap = links.copy(out.at[:, :, 1 - c], theirs, shift(0, 0, 0, 1))
        four = {0: relay(0, three[0])}
        for i in range(4):
            if i + 1 < 4:
                four[i + 1] = relay(i + 1, three[i + 1])
            if i + 2 < 4:
                three[i + 2] = spread(i + 2, 2, two[i + 2])
            for pair in four[i]:
                for cp in pair:
                    cp.wait_recv()
            if i == 0:
                for cp in loads:
                    cp.wait()
            multiply(i)
            if i == 0:
                swap.wait()
                for xh_ in range(2):
                    for y_ in range(4):
                        v = out[xh_, y_, c].astype(F32) + theirs[xh_, y_].astype(F32)
                        sums[xh_, y_] = v.astype(BF)
                keep = pltpu.make_async_copy(sums, sums_ref, loc.at[8])
                keep.start()
        keep.wait()
        for cp in everything:
            cp.wait_send()
        yield 0

    scratch = [pltpu.VMEM((4, 2, 2, 4, 16, w), BF) for ws in CHUNKS for w in ws]
    scratch += [pltpu.VMEM((2, vocab, 4096), BF), pltpu.VMEM((2, 4, vocab, 256), F32)]
    scratch += [pltpu.VMEM(a.shape, a.dtype) for a in second]
    scratch += [
        pltpu.VMEM((256, 256), BF),
        pltpu.VMEM((2, 4, 2, 16, 4096), BF),
        pltpu.VMEM((2, 4, 16, 4096), BF),
        pltpu.VMEM((2, 4, 16, 4096), BF),
    ]
    return Task(
        body,
        [(normed, VM), (own_head, ANY), (other_head, ANY)] + [(a, ANY) for a in second],
        [
            (jax.ShapeDtypeStruct((4, 256), F32), VM),
            (jax.ShapeDtypeStruct((2, 4, 16, 4096), BF), ANY),
        ],
        scratch,
        4 * 3 * 10 + 1,
        9,
        AXES + [(0, 0, 0, 1)],
    )


def reduce_best(best, squares):
    def body(ins, outs, scr):
        best_ref, sq_ref = ins
        out_ref, sum_ref = outs
        held, wide, deep, send, recv, loc = scr
        z, xl, xh, y, c = coords()
        links = Links(send, recv)
        held[0] = sq_ref[...]
        held[0, pl.ds(0, 4), :] = best_ref[...]
        top = lax.broadcasted_iota(jnp.int32, (8, 256), 0) < 4

        def join(v, w):
            return jnp.where(top, jnp.maximum(v, w), v + w)

        cps = [links.copy(held.at[0], wide.at[k], shift(*key)) for k, key in enumerate(PLANE)]
        yield 0
        for cp in cps:
            cp.wait()
        mine = held[0]
        for k in range(15):
            mine = join(mine, wide[k])
        held[1] = mine
        cps = [links.copy(held.at[1], deep.at[k], shift(*key)) for k, key in enumerate(DEEP)]
        yield 0
        for cp in cps:
            cp.wait()
        for k in range(3):
            mine = join(mine, deep[k])
        theirs = deep[3]
        for k in range(4, 7):
            theirs = join(theirs, deep[k])
        out_ref[c] = mine
        out_ref[1 - c] = theirs
        sum_ref[...] = mine + theirs

    return Task(
        body,
        [(best, VM), (squares, VM)],
        [
            (jax.ShapeDtypeStruct((2, 8, 256), F32), VM),
            (jax.ShapeDtypeStruct((8, 256), F32), VM),
        ],
        [
            pltpu.VMEM((2, 8, 256), F32),
            pltpu.VMEM((15, 8, 256), F32),
            pltpu.VMEM((7, 8, 256), F32),
        ],
        22,
        1,
        PLANE + DEEP,
    )


def scores(q, k):
    return lax.dot_general(q, k, (((1,), (1,)), ((), ())), preferred_element_type=F32) * SCALE2


def cached_attention(begins, ends, queries, keys, values):
    rows = queries.shape[1]
    span = 256

    def kernel(lo_ref, hi_ref, q_ref, k_ref, v_ref, o_ref, s_ref, m_sc, l_sc, a_sc):
        r = pl.program_id(0)
        lo, hi = lo_ref[r], hi_ref[r]
        m_sc[...] = jnp.full_like(m_sc, NEG)
        l_sc[...] = jnp.zeros_like(l_sc)
        a_sc[...] = jnp.zeros_like(a_sc)

        @pl.when(hi > lo)
        def _():
            def step(b, carry):
                at = pl.multiple_of(b * span, span)
                pos = at + lax.broadcasted_iota(jnp.int32, (rows, span), 1)
                valid = (pos >= lo) & (pos < hi)
                for g in range(2):
                    cut = slice(g * HEAD_DIM, (g + 1) * HEAD_DIM)
                    s = scores(q_ref[0, :, cut], k_ref[pl.ds(at, span), cut])
                    s = jnp.where(valid, s, NEG)
                    old = m_sc[g, :, 0:1]
                    new = jnp.maximum(old, jnp.max(s, axis=-1, keepdims=True))
                    p = jnp.where(valid, jnp.exp2(s - new), 0.0)
                    f = jnp.exp2(old - new)
                    l_sc[g] = l_sc[g] * f + jnp.sum(p, axis=-1, keepdims=True)
                    a_sc[g] = a_sc[g] * f + jnp.dot(
                        p.astype(BF), v_ref[pl.ds(at, span), cut], preferred_element_type=F32
                    )
                    m_sc[g] = jnp.broadcast_to(new, m_sc.shape[1:])
                return carry

            lax.fori_loop(lo // span, (hi + span - 1) // span, step, 0)

        lane = lax.broadcasted_iota(jnp.int32, (rows, 128), 1)
        stats = jnp.where(lane == 0, m_sc[0], jnp.where(lane == 1, m_sc[1], 0.0))
        stats = jnp.where(lane == 2, l_sc[0], jnp.where(lane == 3, l_sc[1], stats))
        s_ref[0] = jnp.transpose(stats)[:8]
        for g in range(2):
            o_ref[0, :, g * HEAD_DIM : (g + 1) * HEAD_DIM] = a_sc[g].astype(BF)

    whole = pl.BlockSpec(keys.shape, lambda r, a, b: (0, 0))
    per = pl.BlockSpec((1, rows, 256), lambda r, a, b: (r, 0, 0))
    return pl.pallas_call(
        kernel,
        grid_spec=pltpu.PrefetchScalarGridSpec(
            num_scalar_prefetch=2,
            grid=(8,),
            in_specs=[per, whole, whole],
            out_specs=[per, pl.BlockSpec((1, 8, rows), lambda r, a, b: (r, 0, 0))],
            scratch_shapes=[
                pltpu.VMEM((2, rows, 128), F32),
                pltpu.VMEM((2, rows, 128), F32),
                pltpu.VMEM((2, rows, HEAD_DIM), F32),
            ],
        ),
        out_shape=[
            jax.ShapeDtypeStruct((8, rows, 256), BF),
            jax.ShapeDtypeStruct((8, 8, rows), F32),
        ],
        compiler_params=pltpu.CompilerParams(vmem_limit_bytes=32 << 20),
        name="cached",
    )(begins, ends, queries, keys, values)


def attend(p_ref, s_ref, q_ref, k_ref, v_ref, att):
    st = jnp.concatenate([s_ref[...].reshape(64, 256), jnp.zeros((64, 256), F32)], axis=0)
    st = jnp.transpose(st)
    for g in range(2):
        cut = slice(g * HEAD_DIM, (g + 1) * HEAD_DIM)
        s = scores(q_ref[:, cut], k_ref[:, cut])
        top = jnp.max(s, axis=-1, keepdims=True)
        for i in range(8):
            top = jnp.maximum(top, st[:, i * 8 + g : i * 8 + g + 1])
        p = jnp.exp2(s - top)
        mass = jnp.sum(p, axis=-1, keepdims=True)
        acc = jnp.dot(p.astype(BF), v_ref[:, cut], preferred_element_type=F32)
        for i in range(8):
            f = jnp.exp2(st[:, i * 8 + g : i * 8 + g + 1] - top)
            mass = mass + f * st[:, i * 8 + g + 2 : i * 8 + g + 3]
            acc = acc + f * p_ref[i, :, cut].astype(F32)
        att[:, cut] = (acc / mass).astype(BF)


def combine(parts, stats, q, k, v, w_out):
    steps = 4
    wide = w_out.shape[1] // steps

    def kernel(p_ref, s_ref, q_ref, k_ref, v_ref, w_ref, o_ref, att):
        @pl.when(pl.program_id(0) == 0)
        def _():
            attend(p_ref, s_ref, q_ref, k_ref, v_ref, att)

        o = jnp.dot(att[...], w_ref[...], preferred_element_type=F32).astype(BF)
        o_ref[...] = o.reshape(o_ref.shape)

    def whole(a):
        return pl.BlockSpec(a.shape, lambda i: (0,) * a.ndim)

    return pl.pallas_call(
        kernel,
        grid=(steps,),
        in_specs=[whole(a) for a in (parts, stats, q, k, v)]
        + [pl.BlockSpec((256, wide), lambda i: (0, i))],
        out_specs=pl.BlockSpec((2, 4, 2, 16, wide), lambda i: (0, 0, 0, 0, i)),
        out_shape=jax.ShapeDtypeStruct((2, 4, 2, 16, w_out.shape[1]), BF),
        scratch_shapes=[pltpu.VMEM((256, 256), BF)],
        compiler_params=pltpu.CompilerParams(vmem_limit_bytes=16 << 20),
        name="combine",
    )(parts, stats, q, k, v, w_out)


def shards(
    block_states,
    token_ids,
    accept,
    cache_lengths,
    cache_keys,
    cache_values,
    w_query,
    w_key,
    w_value,
    w_out,
    attn_gain,
    final_gain,
    embed,
    lm_head,
):
    tok = lax.axis_index("tok")
    other_head = lax.ppermute(lm_head, "head", [(i, i ^ 1) for i in range(16)])
    cache_here = cache_keys.shape[0]
    offsets = jnp.cumsum(cache_lengths) - cache_lengths - tok * cache_here
    begins = jnp.clip(offsets, 0, cache_here)
    ends = jnp.clip(offsets + cache_lengths, 0, cache_here)
    attn_gain = attn_gain.reshape(1, -1)
    final_gain = final_gain.reshape(1, -1)

    vocab_here = embed.shape[0]
    local_ids = token_ids - tok * vocab_here
    inside = (local_ids >= 0) & (local_ids < vocab_here)
    looked_up = jnp.take(embed, jnp.clip(local_ids, 0, vocab_here - 1), axis=0)
    looked_up = jnp.where(inside[:, None], looked_up, jnp.zeros_like(looked_up))

    weights = (w_query, w_key, w_value)
    (rows1, q1, k1, v1), (came,) = comm(
        [
            gather_project(block_states, weights),
            exchange_tok(looked_up.reshape(8, 256, 256)),
        ],
        0,
        "comm_a",
        16,
    )
    embedded = jnp.sum(came.astype(F32), axis=0).astype(BF)
    swapped = jnp.where((accept == 1)[:, None], embedded, block_states)

    (qs1,), (rows2, q2, k2, v2) = comm(
        [gather_queries(q1), gather_project(swapped, weights)], 1, "comm_b", 16
    )
    part1, stat1 = cached_attention(begins, ends, qs1, cache_keys, cache_values)

    (part1, stat1), (qs2,) = comm([exchange_tok(part1, stat1), gather_queries(q2)], 2, "comm_c")
    sum1 = combine(part1, stat1, q1, k1, v1, w_out)
    part2, stat2 = cached_attention(begins, ends, qs2, cache_keys, cache_values)

    (normed, squares), (part2, stat2) = comm(
        [reduce_layer(sum1, rows1, attn_gain, final_gain), exchange_tok(part2, stat2)],
        3,
        "comm_d",
        12,
    )
    second = (part2, stat2, q2, k2, v2, w_out)
    ((best, sum2),) = comm([gather_logits(normed, lm_head, other_head, second)], 4, "comm_e", 52)
    (top, sums), (hiddens,) = comm(
        [reduce_best(best, squares), reduce_layer(sum2, rows2, attn_gain, None)],
        5,
        "comm_f",
        12,
    )
    top_logits = top[:, :4].reshape(2, 64, 16).transpose(1, 0, 2).reshape(-1)
    request_norms = jnp.sqrt(sums[4, :8] / (256 * 4096))
    return (hiddens, request_norms, top_logits)


def solution(mesh):
    placed = (
        P("tok", "head"),
        P(),
        P("tok"),
        P(),
        P("tok", "head"),
        P("tok", "head"),
        P(None, "head"),
        P(None, "head"),
        P(None, "head"),
        P("head", None),
        P(),
        P(),
        P("tok", "head"),
        P(("tok", "head"), None),
    )
    return jax.shard_map(
        shards,
        mesh=mesh,
        in_specs=placed,
        out_specs=(P(("tok", "head"), None), P(), P()),
        check_vma=False,
    )
```

```python
import math

import jax
import jax.numpy as jnp
from jax import lax
from jax.experimental import pallas as pl
from jax.experimental.pallas import tpu as pltpu
from jax.sharding import PartitionSpec as P

HEAD_DIM = 128
EPSILON = 1e-06
NEG = -1e30
SCALE2 = (1.0 / math.sqrt(HEAD_DIM)) * math.log2(math.e)
MESH = pl.DeviceIdType.MESH
BF = jnp.bfloat16
F32 = jnp.float32
ANY = pl.BlockSpec(memory_space=pltpu.HBM)
VM = pl.BlockSpec(memory_space=pltpu.VMEM)
REL8 = ((0, 2), (1, 2), (1, 1), (1, 3), (0, 1), (0, 3), (1, 0))


def coords():
    t = lax.axis_index("tok")
    h = lax.axis_index("head")
    return t // 2, lax.rem(t, 2), h // 8, lax.rem(h // 2, 4), lax.rem(h, 2)


def place(z, xl, xh, y, c):
    return (z * 2 + xl, xh * 8 + y * 2 + c)


def ring(v, d):
    return lax.rem(v + d, 4)


class Links:
    def __init__(self, send, recv):
        self.send, self.recv, self.used = send, recv, 0

    def copy(self, src, dst, device):
        k = self.used
        self.used += 1
        cp = pltpu.make_async_remote_copy(
            src_ref=src,
            dst_ref=dst,
            send_sem=self.send.at[k],
            recv_sem=self.recv.at[k],
            device_id=device,
            device_id_type=MESH,
        )
        cp.start()
        return cp


class Task:
    def __init__(self, body, ins, outs, scratch, copies, local, peers):
        self.body, self.ins, self.outs = body, ins, outs
        self.scratch = list(scratch) + [
            pltpu.SemaphoreType.DMA((copies,)),
            pltpu.SemaphoreType.DMA((copies,)),
            pltpu.SemaphoreType.DMA((max(local, 1),)),
        ]
        self.peers = peers


def shift(dx, dy, dz, dc):
    z, xl, xh, y, c = coords()
    c_ = lax.rem(c + dc, 2)
    if dx == "s":
        return place(ring(z, dz), 1 - xl, xh, ring(y, dy), c_)
    x_ = ring(xh * 2 + xl, dx)
    return place(ring(z, dz), lax.rem(x_, 2), x_ // 2, ring(y, dy), c_)


HEAD_AG = [(0, 0, 0, 1), (2, 0, 0, 0), (0, 1, 0, 0), (0, 2, 0, 0), (0, 3, 0, 0)]
HEAD_ALL = [(0, 0, 0, 1)] + [(2 * dx, dy, 0, 0) for dx, dy in REL8]
TOK_AG = [("s", 0, 0, 0), (0, 0, 1, 0), (0, 0, 2, 0), (0, 0, 3, 0)]
TOK_ALL = [("s" if dx else 0, 0, dz, 0) for dx, dz in REL8]
AXES = [(d, 0, 0, 0) for d in (1, 2, 3)] + [(0, d, 0, 0) for d in (1, 2, 3)]
AXES += [(0, 0, d, 0) for d in (1, 2, 3)]
PLANE = [(k // 4, k % 4, 0, 0) for k in range(1, 16)]
DEEP = [(0, 0, k % 4, k // 4) for k in range(1, 8)]


def comm(tasks, cid, name, vmem=4):
    n_in = [len(t.ins) for t in tasks]
    n_out = [len(t.outs) for t in tasks]
    n_scr = [len(t.scratch) for t in tasks]

    def kernel(*refs):
        ins, rest = refs[: sum(n_in)], refs[sum(n_in) :]
        outs, scr = rest[: sum(n_out)], rest[sum(n_out) :]
        peers = {}
        for t in tasks:
            for key in t.peers:
                peers.setdefault(key, shift(*key))
        barrier = pltpu.get_barrier_semaphore()
        for device in peers.values():
            pl.semaphore_signal(barrier, inc=1, device_id=device, device_id_type=MESH)
        pl.semaphore_wait(barrier, len(peers))
        running, a, b, c = [], 0, 0, 0
        for k, t in enumerate(tasks):
            running.append(
                t.body(
                    ins[a : a + n_in[k]], outs[b : b + n_out[k]], scr[c : c + n_scr[k]]
                )
            )
            a, b, c = a + n_in[k], b + n_out[k], c + n_scr[k]
        while running:
            again = []
            for g in running:
                if next(g, StopIteration) is not StopIteration:
                    again.append(g)
            running = again

    flat = pl.pallas_call(
        kernel,
        out_shape=[o[0] for t in tasks for o in t.outs],
        in_specs=[i[1] for t in tasks for i in t.ins],
        out_specs=[o[1] for t in tasks for o in t.outs],
        scratch_shapes=[s for t in tasks for s in t.scratch],
        compiler_params=pltpu.CompilerParams(
            collective_id=cid, has_side_effects=True, vmem_limit_bytes=vmem << 20
        ),
        name=name,
    )(*[i[0] for t in tasks for i in t.ins])
    res, b = [], 0
    for n in n_out:
        res.append(flat[b : b + n])
        b += n
    return res


def gather_project(x, weights):
    rows, wide = x.shape

    def body(ins, outs, scr):
        x_ref, w_refs = ins[0], ins[1:]
        own_rows, outs = outs[0], outs[1:]
        f_ref, w_ref, acc, send, recv, loc = scr
        z, xl, xh, y, c = coords()
        links = Links(send, recv)

        def index(xh_, y_, c_):
            return xh_ * 8 + y_ * 2 + c_

        def slot(*at):
            return f_ref.at[index(*at)]

        def absorb(*at):
            k = index(*at)
            v = f_ref[k]
            for n in range(3):
                w = w_ref[n, pl.ds(pl.multiple_of(k * wide, wide), wide), :]
                acc[n] += jnp.dot(v, w, preferred_element_type=F32)

        core = place(z, xl, xh, y, 1 - c)
        own = slot(xh, y, c)
        keep = pltpu.make_async_copy(x_ref, own, loc.at[0])
        keep.start()
        landed = []
        over_x = links.copy(x_ref, own, place(z, xl, 1 - xh, y, c))
        over_y = {d: links.copy(x_ref, own, place(z, xl, xh, ring(y, d), c)) for d in (2, 1, 3)}
        landed.append(links.copy(x_ref, own, core))
        loads = [pltpu.make_async_copy(w_refs[n], w_ref.at[n], loc.at[1 + n]) for n in range(3)]
        for cp in loads:
            cp.start()
        acc[...] = jnp.zeros_like(acc)
        yield 0
        over_x.wait_recv()
        far = slot(1 - xh, y, c)
        far_y = {d: links.copy(far, far, place(z, xl, xh, ring(y, d), c)) for d in (2, 1, 3)}
        landed.append(links.copy(far, far, core))
        yield 0
        keep.wait()
        for cp in loads:
            cp.wait()
        absorb(xh, y, c)
        absorb(1 - xh, y, c)
        for k, xh_ in enumerate((xh, 1 - xh)):
            landed[k].wait_recv()
            absorb(xh_, y, 1 - c)
        yield 0
        for xh_, arrive in ((xh, over_y), (1 - xh, far_y)):
            for d in (1, 3, 2):
                y_ = ring(y, 4 - d)
                arrive[d].wait_recv()
                got = slot(xh_, y_, c)
                landed.append(links.copy(got, got, core))
                absorb(xh_, y_, c)
            for k, d in enumerate((1, 3, 2)):
                landed[k - 3].wait_recv()
                absorb(xh_, ring(y, 4 - d), 1 - c)
            yield 0
        h = pl.multiple_of(index(xh, y, c) * 16, 16)
        for k in range(16):
            own_rows[:, k * wide : (k + 1) * wide] = f_ref[k, pl.ds(h, 16), :]
        for n in range(3):
            outs[n][...] = acc[n].astype(BF)
        for cp in [over_x] + list(over_y.values()) + list(far_y.values()) + landed:
            cp.wait_send()

    return Task(
        body,
        [(x, ANY)] + [(w, ANY) for w in weights],
        [(jax.ShapeDtypeStruct((16, 16 * wide), BF), VM)]
        + [(jax.ShapeDtypeStruct((rows, wide), BF), VM)] * 3,
        [
            pltpu.VMEM((16, rows, wide), BF),
            pltpu.VMEM((3, 16 * wide, wide), BF),
            pltpu.VMEM((3, rows, wide), F32),
        ],
        15,
        4,
        HEAD_AG,
    )


def gather_queries(q):
    def body(ins, outs, scr):
        (q_ref,), (o_ref,), (send, recv, loc) = ins, outs, scr
        z, xl, xh, y, c = coords()
        links = Links(send, recv)
        own = o_ref.at[z * 2 + xl]
        keep = pltpu.make_async_copy(q_ref, own, loc.at[0])
        keep.start()
        side = place(z, 1 - xl, xh, y, c)
        over_x = [links.copy(q_ref, own, side)]
        over_z = {d: links.copy(q_ref, own, place(ring(z, d), xl, xh, y, c)) for d in (2, 1, 3)}
        yield 0
        over_x[0].wait_recv()
        far = o_ref.at[z * 2 + 1 - xl, pl.ds(0, 128)]
        more = [links.copy(far, far, place(ring(z, d), xl, xh, y, c)) for d in (2, 1, 3)]
        yield 0
        for d in (1, 3, 2):
            over_z[d].wait_recv()
            got = o_ref.at[ring(z, 4 - d) * 2 + xl, pl.ds(128, 128)]
            over_x.append(links.copy(got, got, side))
        yield 0
        for cp in over_x[1:] + more:
            cp.wait_recv()
        for cp in over_x + more + list(over_z.values()):
            cp.wait_send()
        keep.wait()

    return Task(
        body, [(q, ANY)], [(jax.ShapeDtypeStruct((8, 256, 256), BF), ANY)], [], 10, 1, TOK_AG
    )


def exchange_tok(*arrays):
    def body(ins, outs, scr):
        send, recv, loc = scr
        z, xl, xh, y, c = coords()
        t = z * 2 + xl
        links = Links(send, recv)
        keep, cps = [], []
        for k, (src, dst) in enumerate(zip(ins, outs)):
            keep.append(pltpu.make_async_copy(src.at[t], dst.at[t], loc.at[k]))
            keep[-1].start()
        for dx, dz in REL8:
            z_, xl_ = ring(z, dz), lax.rem(xl + dx, 2)
            for src, dst in zip(ins, outs):
                cps.append(links.copy(src.at[z_ * 2 + xl_], dst.at[t], place(z_, xl_, xh, y, c)))
        yield 0
        for cp in cps:
            cp.wait()
        for cp in keep:
            cp.wait()

    n = len(arrays)
    return Task(
        body,
        [(a, ANY) for a in arrays],
        [(jax.ShapeDtypeStruct(a.shape, a.dtype), ANY) for a in arrays],
        [],
        7 * n,
        n,
        TOK_ALL,
    )


def unit_rows(v):
    return v * lax.rsqrt(jnp.mean(v * v, axis=-1, keepdims=True) + EPSILON)


def layer_end(before, total, gain):
    return (before.astype(F32) + unit_rows(total) * gain).astype(BF)


def reduce_layer(part, states_in, attn_gain, final_gain):
    def body(ins, outs, scr):
        part_ref, x_ref, again_ref, fgain_ref = ins
        mine, theirs, came, far, send, recv, loc = scr
        z, xl, xh, y, c = coords()
        links = Links(send, recv)
        cps = []
        l0 = pltpu.make_async_copy(part_ref.at[:, :, c], mine, loc.at[0])
        l0.start()
        swap = links.copy(part_ref.at[:, :, 1 - c], theirs, place(z, xl, xh, y, 1 - c))
        yield 0
        l0.wait()
        swap.wait_recv()

        def both(xh_, y_):
            return mine[xh_, y_].astype(F32) + theirs[xh_, y_].astype(F32)

        for dy in (2, 1, 3):
            y_ = ring(y, dy)
            for xh_ in (0, 1):
                mine[xh_, y_] = both(xh_, y_).astype(BF)
            cps.append(links.copy(mine.at[:, y_], came.at[:, y], place(z, xl, xh, y_, c)))
        total, away = both(xh, y), both(1 - xh, y)
        yield 0
        for cp in cps:
            cp.wait_recv()
        for dy in (1, 3, 2):
            y_ = ring(y, dy)
            away = away + came[1 - xh, y_].astype(F32)
            total = total + came[xh, y_].astype(F32)
        mine[1 - xh, y] = away.astype(BF)
        over = links.copy(mine.at[1 - xh, y], far, place(z, xl, 1 - xh, y, c))
        yield 0
        over.wait()
        total = total + far[...].astype(F32)
        for cp in cps:
            cp.wait_send()
        swap.wait_send()
        wide = layer_end(x_ref[...], total, again_ref[...]).astype(F32)
        squares = jnp.sum(wide * wide, axis=-1, keepdims=True)
        normed = wide * lax.rsqrt(squares * (1.0 / 4096) + EPSILON) * fgain_ref[...]
        outs[0][...] = normed.astype(BF)
        lane = lax.broadcasted_iota(jnp.int32, (8, 256), 1)
        row = lax.broadcasted_iota(jnp.int32, (8, 256), 0)
        outs[1][...] = jnp.where((lane == z * 2 + xl) & (row == 4), jnp.sum(squares), 0.0)

    block = pltpu.VMEM((2, 4, 16, 4096), BF)
    return Task(
        body,
        [(part, ANY), (states_in, VM), (attn_gain, VM), (final_gain, VM)],
        [(jax.ShapeDtypeStruct((16, 4096), BF), VM), (jax.ShapeDtypeStruct((8, 256), F32), VM)],
        [block, block, block, pltpu.VMEM((16, 4096), BF)],
        8,
        1,
        HEAD_AG,
    )


def along(axis, d):
    return shift(*{"x": (d, 0, 0, 0), "y": (0, d, 0, 0), "z": (0, 0, d, 0)}[axis])


CHUNKS = ((384, 384, 256), (384, 384, 256), (384, 384, 256), (512, 384, 128))
ORDERS = ("xyz", "yzx", "zxy")


def gather_logits(normed, squares, own_head, other_head, second, states_in, attn_gain):
    vocab = own_head.shape[0]

    def body(ins, outs, scr):
        n_ref, sq_ref, x_ref, again_ref, own_ref, other_ref = ins[:6]
        top_ref, sum_ref, hid_ref = outs
        bufs = [scr[3 * i : 3 * i + 3] for i in range(4)]
        heads, acc = scr[12:14]
        held = scr[14:20]
        att, out, theirs, came, far, maxima, wide, deep, send, recv, loc = scr[20:]
        z, xl, xh, y, c = coords()
        x = xh * 2 + xl
        links = Links(send, recv)
        full = slice(None)
        loads = [
            pltpu.make_async_copy(src, heads.at[k], loc.at[k])
            for k, src in enumerate((own_ref, other_ref))
        ]

        def block(i, p, known, step=0, half=None):
            last = ORDERS[p][2]
            z_, y_, x_ = z, y, x
            if step:
                if last == "z":
                    z_ = ring(z, step)
                elif last == "y":
                    y_ = ring(y, step)
                else:
                    x_ = ring(x, step)
            at = [
                full if "z" in known else z_,
                full if "x" in known else lax.rem(x_, 2),
                full if "x" in known else x_ // 2,
                full if "y" in known else y_,
            ]
            if half is not None:
                if last == "z":
                    at[1] = half
                else:
                    at[0] = pl.ds(2 * half, 2)
            return bufs[i][p].at[tuple(at)]

        start = 0
        for i in range(4):
            for p in range(3):
                bufs[i][p][z, xl, xh, y] = n_ref[:, start : start + CHUNKS[i][p]]
                start += CHUNKS[i][p]

        everything = []

        def push(i, p, ref, axis, d):
            cp = links.copy(ref, ref, along(axis, d))
            everything.append(cp)
            return cp

        def spread(i, stage, before):
            out = []
            for p in range(3):
                if before is not None:
                    for cp in before[p]:
                        cp.wait_recv()
                ref = block(i, p, ORDERS[p][:stage])
                ds = (2, 1, 3) if stage < 2 else (1, 3)
                out.append([push(i, p, ref, ORDERS[p][stage], d) for d in ds])
            return out

        def relay(i, before):
            out = []
            for p in range(3):
                axis, known = ORDERS[p][2], ORDERS[p][:2]
                before[p][0].wait_recv()
                lower = push(i, p, block(i, p, known, 3, 0), axis, 1)
                before[p][1].wait_recv()
                upper = push(i, p, block(i, p, known, 1, 1), axis, 3)
                out.append([lower, upper])
            return out

        def multiply(i):
            cut = pl.ds(1024 * i, 1024)

            def step(r, carry):
                rows = jnp.concatenate(
                    [bufs[i][p][r].reshape(256, CHUNKS[i][p]) for p in range(3)], axis=1
                )
                top = None
                for k in range(2):
                    part = lax.dot_general(
                        heads[k, :, cut], rows, (((1,), (1,)), ((), ())), preferred_element_type=F32
                    )
                    if i > 0:
                        part = acc[k, r] + part
                    if i < 3:
                        acc[k, r] = part
                    else:
                        m = jnp.max(part, axis=0, keepdims=True)
                        top = m if top is None else jnp.maximum(top, m)
                if i == 3:
                    maxima[0, pl.ds(r, 1), :] = top
                return carry

            lax.fori_loop(0, 4, step, 0)

        fetch = [
            pltpu.make_async_copy(src, dst, loc.at[2 + k])
            for k, (src, dst) in enumerate(zip(ins[6:], held))
        ]
        one = [spread(i, 0, None) for i in range(4)]
        for cp in fetch + loads:
            cp.start()
        two = [spread(i, 1, one[i]) for i in range(4)]
        three = {0: spread(0, 2, two[0]), 1: spread(1, 2, two[1])}
        for cp in fetch:
            cp.wait()
        attend(*held[:5], att)

        def times_out(k, carry):
            cut = pl.ds(pl.multiple_of(k * 1024, 1024), 1024)
            o = jnp.dot(att[...], held[5][:, cut], preferred_element_type=F32).astype(BF)
            out[:, :, :, :, cut] = o.reshape(2, 4, 2, 16, 1024)
            return carry

        lax.fori_loop(0, 4, times_out, 0)
        swap = links.copy(out.at[:, :, 1 - c], theirs, shift(0, 0, 0, 1))
        over_y = []
        four = {0: relay(0, three[0])}
        for i in range(4):
            if i + 1 < 4:
                four[i + 1] = relay(i + 1, three[i + 1])
            if i + 2 < 4:
                three[i + 2] = spread(i + 2, 2, two[i + 2])
            for pair in four[i]:
                for cp in pair:
                    cp.wait_recv()
            if i == 0:
                for cp in loads:
                    cp.wait()
            if i == 3:
                maxima[0] = sq_ref[...]
            multiply(i)
            if i == 0:
                swap.wait()
                for dy in (2, 1, 3, 0):
                    y_ = ring(y, dy)
                    for xh_ in (0, 1):
                        v = out[xh_, y_, c].astype(F32) + theirs[xh_, y_].astype(F32)
                        theirs[xh_, y_] = v.astype(BF)
                    if dy:
                        over_y.append(
                            links.copy(
                                theirs.at[:, y_], came.at[:, y], place(z, xl, xh, y_, c)
                            )
                        )
            if i == 2:
                for cp in over_y:
                    cp.wait_recv()
                for xh_ in (0, 1):
                    v = theirs[xh_, y].astype(F32)
                    for dy in (1, 3, 2):
                        v = v + came[xh_, ring(y, dy)].astype(F32)
                    theirs[xh_, y] = v.astype(BF)
                over_x = links.copy(
                    theirs.at[1 - xh, y], far, place(z, xl, 1 - xh, y, c)
                )
        top = lax.broadcasted_iota(jnp.int32, (8, 256), 0) < 4

        def join(v, w):
            return jnp.where(top, jnp.maximum(v, w), v + w)

        cps = [links.copy(maxima.at[0], wide.at[k], shift(*key)) for k, key in enumerate(PLANE)]
        over_x.wait_recv()
        total = theirs[xh, y].astype(F32) + far[...].astype(F32)
        hid_ref[...] = layer_end(x_ref[...], total, again_ref[...])
        everything += over_y + [over_x]
        for cp in cps:
            cp.wait()
        mine = maxima[0]
        for k in range(15):
            mine = join(mine, wide[k])
        maxima[1] = mine
        cps = [links.copy(maxima.at[1], deep.at[k], shift(*key)) for k, key in enumerate(DEEP)]
        for cp in cps:
            cp.wait()
        for k in range(3):
            mine = join(mine, deep[k])
        other = deep[3]
        for k in range(4, 7):
            other = join(other, deep[k])
        top_ref[c] = mine
        top_ref[1 - c] = other
        sum_ref[...] = mine + other
        for cp in everything:
            cp.wait_send()
        yield 0

    scratch = [pltpu.VMEM((4, 2, 2, 4, 16, w), BF) for ws in CHUNKS for w in ws]
    scratch += [pltpu.VMEM((2, vocab, 4096), BF), pltpu.VMEM((2, 4, vocab, 256), F32)]
    scratch += [pltpu.VMEM(a.shape, a.dtype) for a in second]
    scratch += [
        pltpu.VMEM((256, 256), BF),
        pltpu.VMEM((2, 4, 2, 16, 4096), BF),
        pltpu.VMEM((2, 4, 16, 4096), BF),
        pltpu.VMEM((2, 4, 16, 4096), BF),
        pltpu.VMEM((16, 4096), BF),
        pltpu.VMEM((2, 8, 256), F32),
        pltpu.VMEM((15, 8, 256), F32),
        pltpu.VMEM((7, 8, 256), F32),
    ]
    return Task(
        body,
        [(normed, VM), (squares, VM), (states_in, VM), (attn_gain, VM)]
        + [(a, ANY) for a in (own_head, other_head) + second],
        [
            (jax.ShapeDtypeStruct((2, 8, 256), F32), VM),
            (jax.ShapeDtypeStruct((8, 256), F32), VM),
            (jax.ShapeDtypeStruct((16, 4096), BF), VM),
        ],
        scratch,
        4 * 3 * 10 + 5 + 22,
        8,
        AXES + PLANE + DEEP,
    )


def scores(q, k):
    return lax.dot_general(q, k, (((1,), (1,)), ((), ())), preferred_element_type=F32) * SCALE2


def cached_attention(begins, ends, queries, keys, values):
    rows = queries.shape[1]
    span = 256

    def kernel(lo_ref, hi_ref, q_ref, k_ref, v_ref, o_ref, s_ref, v_sc, m_sc, a_sc):
        for g in range(2):
            v_sc[g, :, :HEAD_DIM] = v_ref[:, g * HEAD_DIM : (g + 1) * HEAD_DIM]
            v_sc[g, :, HEAD_DIM:] = jnp.ones((v_ref.shape[0], HEAD_DIM), BF)
        lane = lax.broadcasted_iota(jnp.int32, (rows, 128), 1)
        sub = lax.broadcasted_iota(jnp.int32, (8, rows), 0)

        def request(r, carry):
            lo, hi = lo_ref[r], hi_ref[r]

            @pl.when(hi <= lo)
            def _():
                o_ref[r] = jnp.zeros(o_ref.shape[1:], BF)
                s_ref[r] = jnp.where(sub < 2, NEG, 0.0)

            @pl.when(hi > lo)
            def _():
                m_sc[...] = jnp.full_like(m_sc, NEG)
                a_sc[...] = jnp.zeros_like(a_sc)

                def step(b, carry):
                    at = pl.multiple_of(b * span, span)
                    pos = at + lax.broadcasted_iota(jnp.int32, (1, span), 1)
                    bias = jnp.where((pos >= lo) & (pos < hi), 0.0, NEG)
                    for g in range(2):
                        cut = slice(g * HEAD_DIM, (g + 1) * HEAD_DIM)
                        s = scores(q_ref[r, :, cut], k_ref[pl.ds(at, span), cut]) + bias
                        old = m_sc[g]
                        new = jnp.maximum(old, jnp.max(s, axis=-1, keepdims=True))
                        p = jnp.exp2(s - new[:, 0:1]).astype(BF)
                        f = jnp.exp2(old - new)
                        a_sc[g] = a_sc[g] * jnp.concatenate([f, f], axis=1) + jnp.dot(
                            p, v_sc[g, pl.ds(at, span), :], preferred_element_type=F32
                        )
                        m_sc[g] = new
                    return carry

                lax.fori_loop(lo // span, (hi + span - 1) // span, step, 0)
                stats = jnp.where(lane == 0, m_sc[0], m_sc[1])
                stats = jnp.where(lane == 2, a_sc[0, :, HEAD_DIM:], stats)
                stats = jnp.where(lane == 3, a_sc[1, :, HEAD_DIM:], stats)
                s_ref[r] = jnp.transpose(stats)[:8]
                for g in range(2):
                    o_ref[r, :, g * HEAD_DIM : (g + 1) * HEAD_DIM] = a_sc[g, :, :HEAD_DIM].astype(BF)

            return carry

        lax.fori_loop(0, 8, request, 0)

    smem = pl.BlockSpec(memory_space=pltpu.SMEM)
    return pl.pallas_call(
        kernel,
        in_specs=[smem, smem, VM, VM, VM],
        out_specs=[VM, VM],
        scratch_shapes=[
            pltpu.VMEM((2, values.shape[0], 256), BF),
            pltpu.VMEM((2, rows, 128), F32),
            pltpu.VMEM((2, rows, 256), F32),
        ],
        out_shape=[
            jax.ShapeDtypeStruct((8, rows, 256), BF),
            jax.ShapeDtypeStruct((8, 8, rows), F32),
        ],
        compiler_params=pltpu.CompilerParams(vmem_limit_bytes=16 << 20),
        name="cached",
    )(begins, ends, queries, keys, values)


def attend(p_ref, s_ref, q_ref, k_ref, v_ref, att):
    st = jnp.concatenate([s_ref[...].reshape(64, 256), jnp.zeros((64, 256), F32)], axis=0)
    st = jnp.transpose(st)
    for g in range(2):
        cut = slice(g * HEAD_DIM, (g + 1) * HEAD_DIM)
        s = scores(q_ref[:, cut], k_ref[:, cut])
        top = jnp.max(s, axis=-1, keepdims=True)
        for i in range(8):
            top = jnp.maximum(top, st[:, i * 8 + g : i * 8 + g + 1])
        p = jnp.exp2(s - top)
        mass = jnp.sum(p, axis=-1, keepdims=True)
        acc = jnp.dot(p.astype(BF), v_ref[:, cut], preferred_element_type=F32)
        for i in range(8):
            f = jnp.exp2(st[:, i * 8 + g : i * 8 + g + 1] - top)
            mass = mass + f * st[:, i * 8 + g + 2 : i * 8 + g + 3]
            acc = acc + f * p_ref[i, :, cut].astype(F32)
        att[:, cut] = (acc / mass).astype(BF)


def combine(parts, stats, q, k, v, w_out):
    steps = 4
    wide = w_out.shape[1] // steps

    def kernel(p_ref, s_ref, q_ref, k_ref, v_ref, w_ref, o_ref, att):
        @pl.when(pl.program_id(0) == 0)
        def _():
            attend(p_ref, s_ref, q_ref, k_ref, v_ref, att)

        o = jnp.dot(att[...], w_ref[...], preferred_element_type=F32).astype(BF)
        o_ref[...] = o.reshape(o_ref.shape)

    def whole(a):
        return pl.BlockSpec(a.shape, lambda i: (0,) * a.ndim)

    return pl.pallas_call(
        kernel,
        grid=(steps,),
        in_specs=[whole(a) for a in (parts, stats, q, k, v)]
        + [pl.BlockSpec((256, wide), lambda i: (0, i))],
        out_specs=pl.BlockSpec((2, 4, 2, 16, wide), lambda i: (0, 0, 0, 0, i)),
        out_shape=jax.ShapeDtypeStruct((2, 4, 2, 16, w_out.shape[1]), BF),
        scratch_shapes=[pltpu.VMEM((256, 256), BF)],
        compiler_params=pltpu.CompilerParams(vmem_limit_bytes=16 << 20),
        name="combine",
    )(parts, stats, q, k, v, w_out)


def shards(
    block_states,
    token_ids,
    accept,
    cache_lengths,
    cache_keys,
    cache_values,
    w_query,
    w_key,
    w_value,
    w_out,
    attn_gain,
    final_gain,
    embed,
    lm_head,
):
    tok = lax.axis_index("tok")
    other_head = lax.ppermute(lm_head, "head", [(i, i ^ 1) for i in range(16)])
    cache_here = cache_keys.shape[0]
    offsets = jnp.cumsum(cache_lengths) - cache_lengths - tok * cache_here
    begins = jnp.clip(offsets, 0, cache_here)
    ends = jnp.clip(offsets + cache_lengths, 0, cache_here)
    attn_gain = attn_gain.reshape(1, -1)
    final_gain = final_gain.reshape(1, -1)

    vocab_here = embed.shape[0]
    local_ids = token_ids - tok * vocab_here
    inside = (local_ids >= 0) & (local_ids < vocab_here)
    looked_up = jnp.take(embed, jnp.clip(local_ids, 0, vocab_here - 1), axis=0)
    looked_up = jnp.where(inside[:, None], looked_up, jnp.zeros_like(looked_up))

    weights = (w_query, w_key, w_value)
    (rows1, q1, k1, v1), (came,) = comm(
        [
            gather_project(block_states, weights),
            exchange_tok(looked_up.reshape(8, 256, 256)),
        ],
        0,
        "comm_a",
        60,
    )
    embedded = jnp.sum(came.astype(F32), axis=0).astype(BF)
    swapped = jnp.where((accept == 1)[:, None], embedded, block_states)

    (qs1,), (rows2, q2, k2, v2) = comm(
        [gather_queries(q1), gather_project(swapped, weights)], 1, "comm_b", 60
    )
    part1, stat1 = cached_attention(begins, ends, qs1, cache_keys, cache_values)

    (part1, stat1), (qs2,) = comm([exchange_tok(part1, stat1), gather_queries(q2)], 2, "comm_c")
    sum1 = combine(part1, stat1, q1, k1, v1, w_out)
    part2, stat2 = cached_attention(begins, ends, qs2, cache_keys, cache_values)

    (normed, squares), (part2, stat2) = comm(
        [reduce_layer(sum1, rows1, attn_gain, final_gain), exchange_tok(part2, stat2)],
        3,
        "comm_d",
        12,
    )
    second = (part2, stat2, q2, k2, v2, w_out)
    ((top, sums, hiddens),) = comm(
        [gather_logits(normed, squares, lm_head, other_head, second, rows2, attn_gain)],
        4,
        "comm_e",
        56,
    )
    top_logits = top[:, :4].reshape(2, 64, 16).transpose(1, 0, 2).reshape(-1)
    request_norms = jnp.sqrt(sums[4, :8] / (256 * 4096))
    return (hiddens, request_norms, top_logits)


def solution(mesh):
    placed = (
        P("tok", "head"),
        P(),
        P("tok"),
        P(),
        P("tok", "head"),
        P("tok", "head"),
        P(None, "head"),
        P(None, "head"),
        P(None, "head"),
        P("head", None),
        P(),
        P(),
        P("tok", "head"),
        P(("tok", "head"), None),
    )
    return jax.shard_map(
        shards,
        mesh=mesh,
        in_specs=placed,
        out_specs=(P(("tok", "head"), None), P(), P()),
        check_vma=False,
    )
```

```python
import math

import jax
import jax.numpy as jnp
from jax import lax
from jax.experimental import pallas as pl
from jax.experimental.pallas import tpu as pltpu
from jax.sharding import PartitionSpec as P

HEAD_DIM = 128
EPSILON = 1e-06
NEG = -1e30
SCALE2 = (1.0 / math.sqrt(HEAD_DIM)) * math.log2(math.e)
MESH = pl.DeviceIdType.MESH
BF = jnp.bfloat16
F32 = jnp.float32
ANY = pl.BlockSpec(memory_space=pltpu.HBM)
VM = pl.BlockSpec(memory_space=pltpu.VMEM)
REL8 = ((0, 2), (1, 2), (1, 1), (1, 3), (0, 1), (0, 3), (1, 0))


def coords():
    t = lax.axis_index("tok")
    h = lax.axis_index("head")
    return t // 2, lax.rem(t, 2), h // 8, lax.rem(h // 2, 4), lax.rem(h, 2)


def place(z, xl, xh, y, c):
    return (z * 2 + xl, xh * 8 + y * 2 + c)


def ring(v, d):
    return lax.rem(v + d, 4)


class Links:
    def __init__(self, send, recv):
        self.send, self.recv, self.used = send, recv, 0

    def copy(self, src, dst, device):
        k = self.used
        self.used += 1
        cp = pltpu.make_async_remote_copy(
            src_ref=src,
            dst_ref=dst,
            send_sem=self.send.at[k],
            recv_sem=self.recv.at[k],
            device_id=device,
            device_id_type=MESH,
        )
        cp.start()
        return cp


class Task:
    def __init__(self, body, ins, outs, scratch, copies, local, peers):
        self.body, self.ins, self.outs = body, ins, outs
        self.scratch = list(scratch) + [
            pltpu.SemaphoreType.DMA((copies,)),
            pltpu.SemaphoreType.DMA((copies,)),
            pltpu.SemaphoreType.DMA((max(local, 1),)),
        ]
        self.peers = peers


def shift(dx, dy, dz, dc):
    z, xl, xh, y, c = coords()
    c_ = lax.rem(c + dc, 2)
    if dx == "s":
        return place(ring(z, dz), 1 - xl, xh, ring(y, dy), c_)
    x_ = ring(xh * 2 + xl, dx)
    return place(ring(z, dz), lax.rem(x_, 2), x_ // 2, ring(y, dy), c_)


HEAD_AG = [(0, 0, 0, 1), (2, 0, 0, 0), (0, 1, 0, 0), (0, 2, 0, 0), (0, 3, 0, 0)]
HEAD_ALL = [(0, 0, 0, 1)] + [(2 * dx, dy, 0, 0) for dx, dy in REL8]
TOK_AG = [("s", 0, 0, 0), (0, 0, 1, 0), (0, 0, 2, 0), (0, 0, 3, 0)]
TOK_ALL = [("s" if dx else 0, 0, dz, 0) for dx, dz in REL8]
AXES = [(d, 0, 0, 0) for d in (1, 2, 3)] + [(0, d, 0, 0) for d in (1, 2, 3)]
AXES += [(0, 0, d, 0) for d in (1, 2, 3)]
PLANE = [(k // 4, k % 4, 0, 0) for k in range(1, 16)]
DEEP = [(0, 0, k % 4, k // 4) for k in range(1, 8)]


def comm(tasks, cid, name, vmem=4):
    n_in = [len(t.ins) for t in tasks]
    n_out = [len(t.outs) for t in tasks]
    n_scr = [len(t.scratch) for t in tasks]

    def kernel(*refs):
        ins, rest = refs[: sum(n_in)], refs[sum(n_in) :]
        outs, scr = rest[: sum(n_out)], rest[sum(n_out) :]
        peers = {}
        for t in tasks:
            for key in t.peers:
                peers.setdefault(key, shift(*key))
        barrier = pltpu.get_barrier_semaphore()
        for device in peers.values():
            pl.semaphore_signal(barrier, inc=1, device_id=device, device_id_type=MESH)
        pl.semaphore_wait(barrier, len(peers))
        running, a, b, c = [], 0, 0, 0
        for k, t in enumerate(tasks):
            running.append(
                t.body(
                    ins[a : a + n_in[k]], outs[b : b + n_out[k]], scr[c : c + n_scr[k]]
                )
            )
            a, b, c = a + n_in[k], b + n_out[k], c + n_scr[k]
        while running:
            again = []
            for g in running:
                if next(g, StopIteration) is not StopIteration:
                    again.append(g)
            running = again

    flat = pl.pallas_call(
        kernel,
        out_shape=[o[0] for t in tasks for o in t.outs],
        in_specs=[i[1] for t in tasks for i in t.ins],
        out_specs=[o[1] for t in tasks for o in t.outs],
        scratch_shapes=[s for t in tasks for s in t.scratch],
        compiler_params=pltpu.CompilerParams(
            collective_id=cid, has_side_effects=True, vmem_limit_bytes=vmem << 20
        ),
        name=name,
    )(*[i[0] for t in tasks for i in t.ins])
    res, b = [], 0
    for n in n_out:
        res.append(flat[b : b + n])
        b += n
    return res


def gather_project(x, weights):
    rows, wide = x.shape

    def body(ins, outs, scr):
        x_ref, w_refs = ins[0], ins[1:]
        own_rows, outs = outs[0], outs[1:]
        f_ref, w_ref, acc, send, recv, loc = scr
        z, xl, xh, y, c = coords()
        links = Links(send, recv)

        def index(xh_, y_, c_):
            return xh_ * 8 + y_ * 2 + c_

        def slot(*at):
            return f_ref.at[index(*at)]

        def absorb(*at):
            k = index(*at)
            v = f_ref[k]
            for n in range(3):
                w = w_ref[n, pl.ds(pl.multiple_of(k * wide, wide), wide), :]
                acc[n] += jnp.dot(v, w, preferred_element_type=F32)

        core = place(z, xl, xh, y, 1 - c)
        own = slot(xh, y, c)
        keep = pltpu.make_async_copy(x_ref, own, loc.at[0])
        keep.start()
        landed = []
        over_x = links.copy(x_ref, own, place(z, xl, 1 - xh, y, c))
        over_y = {d: links.copy(x_ref, own, place(z, xl, xh, ring(y, d), c)) for d in (2, 1, 3)}
        landed.append(links.copy(x_ref, own, core))
        loads = [pltpu.make_async_copy(w_refs[n], w_ref.at[n], loc.at[1 + n]) for n in range(3)]
        for cp in loads:
            cp.start()
        acc[...] = jnp.zeros_like(acc)
        yield 0
        over_x.wait_recv()
        far = slot(1 - xh, y, c)
        far_y = {d: links.copy(far, far, place(z, xl, xh, ring(y, d), c)) for d in (2, 1, 3)}
        landed.append(links.copy(far, far, core))
        yield 0
        keep.wait()
        for cp in loads:
            cp.wait()
        absorb(xh, y, c)
        absorb(1 - xh, y, c)
        for k, xh_ in enumerate((xh, 1 - xh)):
            landed[k].wait_recv()
            absorb(xh_, y, 1 - c)
        yield 0
        for xh_, arrive in ((xh, over_y), (1 - xh, far_y)):
            for d in (1, 3, 2):
                y_ = ring(y, 4 - d)
                arrive[d].wait_recv()
                got = slot(xh_, y_, c)
                landed.append(links.copy(got, got, core))
                absorb(xh_, y_, c)
            for k, d in enumerate((1, 3, 2)):
                landed[k - 3].wait_recv()
                absorb(xh_, ring(y, 4 - d), 1 - c)
            yield 0
        h = pl.multiple_of(index(xh, y, c) * 16, 16)
        for k in range(16):
            own_rows[:, k * wide : (k + 1) * wide] = f_ref[k, pl.ds(h, 16), :]
        for n in range(3):
            outs[n][...] = acc[n].astype(BF)
        for cp in [over_x] + list(over_y.values()) + list(far_y.values()) + landed:
            cp.wait_send()

    return Task(
        body,
        [(x, ANY)] + [(w, ANY) for w in weights],
        [(jax.ShapeDtypeStruct((16, 16 * wide), BF), VM)]
        + [(jax.ShapeDtypeStruct((rows, wide), BF), VM)] * 3,
        [
            pltpu.VMEM((16, rows, wide), BF),
            pltpu.VMEM((3, 16 * wide, wide), BF),
            pltpu.VMEM((3, rows, wide), F32),
        ],
        15,
        4,
        HEAD_AG,
    )


def gather_queries(q):
    def body(ins, outs, scr):
        (q_ref,), (o_ref,), (send, recv, loc) = ins, outs, scr
        z, xl, xh, y, c = coords()
        links = Links(send, recv)
        own = o_ref.at[z * 2 + xl]
        keep = pltpu.make_async_copy(q_ref, own, loc.at[0])
        keep.start()
        side = place(z, 1 - xl, xh, y, c)
        over_x = [links.copy(q_ref, own, side)]
        over_z = {d: links.copy(q_ref, own, place(ring(z, d), xl, xh, y, c)) for d in (2, 1, 3)}
        yield 0
        over_x[0].wait_recv()
        far = o_ref.at[z * 2 + 1 - xl, pl.ds(0, 128)]
        more = [links.copy(far, far, place(ring(z, d), xl, xh, y, c)) for d in (2, 1, 3)]
        yield 0
        for d in (1, 3, 2):
            over_z[d].wait_recv()
            got = o_ref.at[ring(z, 4 - d) * 2 + xl, pl.ds(128, 128)]
            over_x.append(links.copy(got, got, side))
        yield 0
        for cp in over_x[1:] + more:
            cp.wait_recv()
        for cp in over_x + more + list(over_z.values()):
            cp.wait_send()
        keep.wait()

    return Task(
        body, [(q, ANY)], [(jax.ShapeDtypeStruct((8, 256, 256), BF), ANY)], [], 10, 1, TOK_AG
    )


def exchange_tok(*arrays):
    def body(ins, outs, scr):
        send, recv, loc = scr
        z, xl, xh, y, c = coords()
        t = z * 2 + xl
        links = Links(send, recv)
        keep, cps = [], []
        for k, (src, dst) in enumerate(zip(ins, outs)):
            keep.append(pltpu.make_async_copy(src.at[t], dst.at[t], loc.at[k]))
            keep[-1].start()
        for dx, dz in REL8:
            z_, xl_ = ring(z, dz), lax.rem(xl + dx, 2)
            for src, dst in zip(ins, outs):
                cps.append(links.copy(src.at[z_ * 2 + xl_], dst.at[t], place(z_, xl_, xh, y, c)))
        yield 0
        for cp in cps:
            cp.wait()
        for cp in keep:
            cp.wait()

    n = len(arrays)
    return Task(
        body,
        [(a, ANY) for a in arrays],
        [(jax.ShapeDtypeStruct(a.shape, a.dtype), ANY) for a in arrays],
        [],
        7 * n,
        n,
        TOK_ALL,
    )


def unit_rows(v):
    return v * lax.rsqrt(jnp.mean(v * v, axis=-1, keepdims=True) + EPSILON)


def layer_end(before, total, gain):
    return (before.astype(F32) + unit_rows(total) * gain).astype(BF)


def reduce_layer(part, states_in, attn_gain, final_gain):
    def body(ins, outs, scr):
        part_ref, x_ref, again_ref, fgain_ref = ins
        mine, theirs, came, far, send, recv, loc = scr
        z, xl, xh, y, c = coords()
        links = Links(send, recv)
        cps = []
        l0 = pltpu.make_async_copy(part_ref.at[:, :, c], mine, loc.at[0])
        l0.start()
        swap = links.copy(part_ref.at[:, :, 1 - c], theirs, place(z, xl, xh, y, 1 - c))
        yield 0
        l0.wait()
        swap.wait_recv()

        def both(xh_, y_):
            return mine[xh_, y_].astype(F32) + theirs[xh_, y_].astype(F32)

        for dy in (2, 1, 3):
            y_ = ring(y, dy)
            for xh_ in (0, 1):
                mine[xh_, y_] = both(xh_, y_).astype(BF)
            cps.append(links.copy(mine.at[:, y_], came.at[:, y], place(z, xl, xh, y_, c)))
        total, away = both(xh, y), both(1 - xh, y)
        yield 0
        for cp in cps:
            cp.wait_recv()
        for dy in (1, 3, 2):
            y_ = ring(y, dy)
            away = away + came[1 - xh, y_].astype(F32)
            total = total + came[xh, y_].astype(F32)
        mine[1 - xh, y] = away.astype(BF)
        over = links.copy(mine.at[1 - xh, y], far, place(z, xl, 1 - xh, y, c))
        yield 0
        over.wait()
        total = total + far[...].astype(F32)
        for cp in cps:
            cp.wait_send()
        swap.wait_send()
        wide = layer_end(x_ref[...], total, again_ref[...]).astype(F32)
        squares = jnp.sum(wide * wide, axis=-1, keepdims=True)
        normed = wide * lax.rsqrt(squares * (1.0 / 4096) + EPSILON) * fgain_ref[...]
        outs[0][...] = normed.astype(BF)
        lane = lax.broadcasted_iota(jnp.int32, (8, 256), 1)
        row = lax.broadcasted_iota(jnp.int32, (8, 256), 0)
        outs[1][...] = jnp.where((lane == z * 2 + xl) & (row == 4), jnp.sum(squares), 0.0)

    block = pltpu.VMEM((2, 4, 16, 4096), BF)
    return Task(
        body,
        [(part, ANY), (states_in, VM), (attn_gain, VM), (final_gain, VM)],
        [(jax.ShapeDtypeStruct((16, 4096), BF), VM), (jax.ShapeDtypeStruct((8, 256), F32), VM)],
        [block, block, block, pltpu.VMEM((16, 4096), BF)],
        8,
        1,
        HEAD_AG,
    )


def along(axis, d):
    return shift(*{"x": (d, 0, 0, 0), "y": (0, d, 0, 0), "z": (0, 0, d, 0)}[axis])


CHUNKS = ((512, 512, 512), (512, 512, 512), (384, 384, 256))
STARTS = (0, 1536, 3072, 4096)
ORDERS = ("xyz", "yzx", "zxy")


def gather_logits(normed, squares, own_head, other_head, second, states_in, attn_gain):
    vocab = own_head.shape[0]
    n = len(CHUNKS)

    def body(ins, outs, scr):
        n_ref, sq_ref, x_ref, again_ref, own_ref, other_ref = ins[:6]
        top_ref, sum_ref, hid_ref = outs
        bufs = [scr[3 * i : 3 * i + 3] for i in range(n)]
        heads, acc = scr[9:11]
        held = scr[11:17]
        att, out, theirs, came, far, maxima, wide, deep, send, recv, loc = scr[17:]
        z, xl, xh, y, c = coords()
        x = xh * 2 + xl
        links = Links(send, recv)
        full = slice(None)
        loads = [
            pltpu.make_async_copy(src, heads.at[k], loc.at[k])
            for k, src in enumerate((own_ref, other_ref))
        ]

        def block(i, p, known, step=0, half=None):
            last = ORDERS[p][2]
            z_, y_, x_ = z, y, x
            if step:
                if last == "z":
                    z_ = ring(z, step)
                elif last == "y":
                    y_ = ring(y, step)
                else:
                    x_ = ring(x, step)
            at = [
                full if "z" in known else z_,
                full if "x" in known else lax.rem(x_, 2),
                full if "x" in known else x_ // 2,
                full if "y" in known else y_,
            ]
            if half is not None:
                if last == "z":
                    at[1] = half
                else:
                    at[0] = pl.ds(2 * half, 2)
            return bufs[i][p].at[tuple(at)]

        start = 0
        for i in range(n):
            for p in range(3):
                bufs[i][p][z, xl, xh, y] = n_ref[:, start : start + CHUNKS[i][p]]
                start += CHUNKS[i][p]

        everything = []

        def push(i, p, ref, axis, d):
            cp = links.copy(ref, ref, along(axis, d))
            everything.append(cp)
            return cp

        def spread(i, stage, before):
            out = []
            for p in range(3):
                if before is not None:
                    for cp in before[p]:
                        cp.wait_recv()
                ref = block(i, p, ORDERS[p][:stage])
                ds = (2, 1, 3) if stage < 2 else (1, 3)
                out.append([push(i, p, ref, ORDERS[p][stage], d) for d in ds])
            return out

        def relay(i, before):
            out = []
            for p in range(3):
                axis, known = ORDERS[p][2], ORDERS[p][:2]
                before[p][0].wait_recv()
                lower = push(i, p, block(i, p, known, 3, 0), axis, 1)
                before[p][1].wait_recv()
                upper = push(i, p, block(i, p, known, 1, 1), axis, 3)
                out.append([lower, upper])
            return out

        def multiply(i):
            cut = pl.ds(STARTS[i], STARTS[i + 1] - STARTS[i])

            def step(r, carry):
                rows = jnp.concatenate(
                    [bufs[i][p][r].reshape(256, CHUNKS[i][p]) for p in range(3)], axis=1
                )
                top = None
                for k in range(2):
                    part = lax.dot_general(
                        heads[k, :, cut], rows, (((1,), (1,)), ((), ())), preferred_element_type=F32
                    )
                    if i > 0:
                        part = acc[k, r] + part
                    if i < n - 1:
                        acc[k, r] = part
                    else:
                        m = jnp.max(part, axis=0, keepdims=True)
                        top = m if top is None else jnp.maximum(top, m)
                if i == n - 1:
                    maxima[0, pl.ds(r, 1), :] = top
                return carry

            lax.fori_loop(0, 4, step, 0)

        fetch = [
            pltpu.make_async_copy(src, dst, loc.at[2 + k])
            for k, (src, dst) in enumerate(zip(ins[6:], held))
        ]
        one = [spread(i, 0, None) for i in range(n)]
        for cp in fetch + loads:
            cp.start()
        two = [spread(i, 1, one[i]) for i in range(n)]
        three = {0: spread(0, 2, two[0]), 1: spread(1, 2, two[1])}
        for cp in fetch:
            cp.wait()
        attend(*held[:5], att)

        def times_out(k, carry):
            cut = pl.ds(pl.multiple_of(k * 1024, 1024), 1024)
            o = jnp.dot(att[...], held[5][:, cut], preferred_element_type=F32).astype(BF)
            out[:, :, :, :, cut] = o.reshape(2, 4, 2, 16, 1024)
            return carry

        lax.fori_loop(0, 4, times_out, 0)
        swap = links.copy(out.at[:, :, 1 - c], theirs, shift(0, 0, 0, 1))
        over_y = []
        four = {0: relay(0, three[0])}
        for i in range(n):
            if i + 1 < n:
                four[i + 1] = relay(i + 1, three[i + 1])
            if i + 2 < n:
                three[i + 2] = spread(i + 2, 2, two[i + 2])
            for pair in four[i]:
                for cp in pair:
                    cp.wait_recv()
            if i == 0:
                for cp in loads:
                    cp.wait()
            if i == n - 1:
                maxima[0] = sq_ref[...]
                swap.wait()
                for dy in (2, 1, 3, 0):
                    y_ = ring(y, dy)
                    for xh_ in (0, 1):
                        v = out[xh_, y_, c].astype(F32) + theirs[xh_, y_].astype(F32)
                        theirs[xh_, y_] = v.astype(BF)
                    if dy:
                        over_y.append(
                            links.copy(
                                theirs.at[:, y_], came.at[:, y], place(z, xl, xh, y_, c)
                            )
                        )
            multiply(i)
        top = lax.broadcasted_iota(jnp.int32, (8, 256), 0) < 4

        def join(v, w):
            return jnp.where(top, jnp.maximum(v, w), v + w)

        flat = [links.copy(maxima.at[0], wide.at[k], shift(*key)) for k, key in enumerate(PLANE)]
        for cp in flat:
            cp.wait()
        mine = maxima[0]
        for k in range(15):
            mine = join(mine, wide[k])
        maxima[1] = mine
        tall = [links.copy(maxima.at[1], deep.at[k], shift(*key)) for k, key in enumerate(DEEP)]
        for cp in over_y:
            cp.wait_recv()
        for xh_ in (0, 1):
            v = theirs[xh_, y].astype(F32)
            for dy in (1, 3, 2):
                v = v + came[xh_, ring(y, dy)].astype(F32)
            theirs[xh_, y] = v.astype(BF)
        over_x = links.copy(theirs.at[1 - xh, y], far, place(z, xl, 1 - xh, y, c))
        for cp in tall:
            cp.wait()
        for k in range(3):
            mine = join(mine, deep[k])
        other = deep[3]
        for k in range(4, 7):
            other = join(other, deep[k])
        top_ref[c] = mine
        top_ref[1 - c] = other
        sum_ref[...] = mine + other
        over_x.wait_recv()
        total = theirs[xh, y].astype(F32) + far[...].astype(F32)
        hid_ref[...] = layer_end(x_ref[...], total, again_ref[...])
        everything += over_y + [over_x]
        for cp in everything:
            cp.wait_send()
        yield 0

    scratch = [pltpu.VMEM((4, 2, 2, 4, 16, w), BF) for ws in CHUNKS for w in ws]
    scratch += [pltpu.VMEM((2, vocab, 4096), BF), pltpu.VMEM((2, 4, vocab, 256), F32)]
    scratch += [pltpu.VMEM(a.shape, a.dtype) for a in second]
    scratch += [
        pltpu.VMEM((256, 256), BF),
        pltpu.VMEM((2, 4, 2, 16, 4096), BF),
        pltpu.VMEM((2, 4, 16, 4096), BF),
        pltpu.VMEM((2, 4, 16, 4096), BF),
        pltpu.VMEM((16, 4096), BF),
        pltpu.VMEM((2, 8, 256), F32),
        pltpu.VMEM((15, 8, 256), F32),
        pltpu.VMEM((7, 8, 256), F32),
    ]
    return Task(
        body,
        [(normed, VM), (squares, VM), (states_in, VM), (attn_gain, VM)]
        + [(a, ANY) for a in (own_head, other_head) + second],
        [
            (jax.ShapeDtypeStruct((2, 8, 256), F32), VM),
            (jax.ShapeDtypeStruct((8, 256), F32), VM),
            (jax.ShapeDtypeStruct((16, 4096), BF), VM),
        ],
        scratch,
        3 * 3 * 10 + 5 + 22,
        8,
        AXES + PLANE + DEEP,
    )


def scores(q, k):
    return lax.dot_general(q, k, (((1,), (1,)), ((), ())), preferred_element_type=F32) * SCALE2


def cached_attention(begins, ends, queries, keys, values):
    rows = queries.shape[1]
    cuts = [slice(g * HEAD_DIM, (g + 1) * HEAD_DIM) for g in (0, 1)]

    def kernel(lo_ref, hi_ref, q_ref, k_ref, v_ref, o_ref, s_ref, v_sc, m_sc, a_sc):
        for g in range(2):
            v_sc[g, :, :HEAD_DIM] = v_ref[:, g * HEAD_DIM : (g + 1) * HEAD_DIM]
            v_sc[g, :, HEAD_DIM:] = jnp.ones((v_ref.shape[0], HEAD_DIM), BF)
        lane = lax.broadcasted_iota(jnp.int32, (rows, 128), 1)
        sub = lax.broadcasted_iota(jnp.int32, (8, rows), 0)

        def request(r, carry):
            lo, hi = lo_ref[r], hi_ref[r]

            @pl.when(hi <= lo)
            def _():
                o_ref[r] = jnp.zeros(o_ref.shape[1:], BF)
                s_ref[r] = jnp.where(sub < 2, NEG, 0.0)

            @pl.when(hi > lo)
            def _():
                m_sc[...] = jnp.full_like(m_sc, NEG)
                a_sc[...] = jnp.zeros_like(a_sc)

                def step(b, span):
                    at = pl.multiple_of(b * span, span)
                    pos = at + lax.broadcasted_iota(jnp.int32, (1, span), 1)
                    bias = jnp.where((pos >= lo) & (pos < hi), 0.0, NEG)
                    ss = [scores(q_ref[r, :, cut], k_ref[pl.ds(at, span), cut]) for cut in cuts]
                    ss = [s + bias for s in ss]
                    old = [m_sc[g] for g in (0, 1)]
                    new = [
                        jnp.maximum(o, jnp.max(s, axis=-1, keepdims=True)) for o, s in zip(old, ss)
                    ]
                    ps = [jnp.exp2(s - m[:, 0:1]).astype(BF) for s, m in zip(ss, new)]
                    fs = [jnp.exp2(o - m) for o, m in zip(old, new)]
                    ds = [
                        jnp.dot(p, v_sc[g, pl.ds(at, span), :], preferred_element_type=F32)
                        for g, p in enumerate(ps)
                    ]
                    for g in (0, 1):
                        a_sc[g] = a_sc[g] * jnp.concatenate([fs[g], fs[g]], axis=1) + ds[g]
                        m_sc[g] = new[g]

                small = lo // 256 == (hi - 1) // 256

                @pl.when(small)
                def _():
                    step(lo // 256, 256)

                @pl.when(jnp.logical_not(small))
                def _():
                    def wide_step(b, carry):
                        step(b, 512)
                        return carry

                    lax.fori_loop(lo // 512, (hi + 511) // 512, wide_step, 0)

                stats = jnp.where(lane == 0, m_sc[0], m_sc[1])
                stats = jnp.where(lane == 2, a_sc[0, :, HEAD_DIM:], stats)
                stats = jnp.where(lane == 3, a_sc[1, :, HEAD_DIM:], stats)
                s_ref[r] = jnp.transpose(stats)[:8]
                for g in range(2):
                    o_ref[r, :, g * HEAD_DIM : (g + 1) * HEAD_DIM] = a_sc[g, :, :HEAD_DIM].astype(BF)

            return carry

        lax.fori_loop(0, 8, request, 0)

    smem = pl.BlockSpec(memory_space=pltpu.SMEM)
    return pl.pallas_call(
        kernel,
        in_specs=[smem, smem, VM, VM, VM],
        out_specs=[VM, VM],
        scratch_shapes=[
            pltpu.VMEM((2, values.shape[0], 256), BF),
            pltpu.VMEM((2, rows, 128), F32),
            pltpu.VMEM((2, rows, 256), F32),
        ],
        out_shape=[
            jax.ShapeDtypeStruct((8, rows, 256), BF),
            jax.ShapeDtypeStruct((8, 8, rows), F32),
        ],
        compiler_params=pltpu.CompilerParams(vmem_limit_bytes=16 << 20),
        name="cached",
    )(begins, ends, queries, keys, values)


def attend(p_ref, s_ref, q_ref, k_ref, v_ref, att):
    st = jnp.concatenate([s_ref[...].reshape(64, 256), jnp.zeros((64, 256), F32)], axis=0)
    st = jnp.transpose(st)
    for g in range(2):
        cut = slice(g * HEAD_DIM, (g + 1) * HEAD_DIM)
        s = scores(q_ref[:, cut], k_ref[:, cut])
        top = jnp.max(s, axis=-1, keepdims=True)
        for i in range(8):
            top = jnp.maximum(top, st[:, i * 8 + g : i * 8 + g + 1])
        p = jnp.exp2(s - top)
        mass = jnp.sum(p, axis=-1, keepdims=True)
        acc = jnp.dot(p.astype(BF), v_ref[:, cut], preferred_element_type=F32)
        for i in range(8):
            f = jnp.exp2(st[:, i * 8 + g : i * 8 + g + 1] - top)
            mass = mass + f * st[:, i * 8 + g + 2 : i * 8 + g + 3]
            acc = acc + f * p_ref[i, :, cut].astype(F32)
        att[:, cut] = (acc / mass).astype(BF)


def combine(parts, stats, q, k, v, w_out):
    steps = 4
    wide = w_out.shape[1] // steps

    def kernel(p_ref, s_ref, q_ref, k_ref, v_ref, w_ref, o_ref, att):
        @pl.when(pl.program_id(0) == 0)
        def _():
            attend(p_ref, s_ref, q_ref, k_ref, v_ref, att)

        o = jnp.dot(att[...], w_ref[...], preferred_element_type=F32).astype(BF)
        o_ref[...] = o.reshape(o_ref.shape)

    def whole(a):
        return pl.BlockSpec(a.shape, lambda i: (0,) * a.ndim)

    return pl.pallas_call(
        kernel,
        grid=(steps,),
        in_specs=[whole(a) for a in (parts, stats, q, k, v)]
        + [pl.BlockSpec((256, wide), lambda i: (0, i))],
        out_specs=pl.BlockSpec((2, 4, 2, 16, wide), lambda i: (0, 0, 0, 0, i)),
        out_shape=jax.ShapeDtypeStruct((2, 4, 2, 16, w_out.shape[1]), BF),
        scratch_shapes=[pltpu.VMEM((256, 256), BF)],
        compiler_params=pltpu.CompilerParams(vmem_limit_bytes=16 << 20),
        name="combine",
    )(parts, stats, q, k, v, w_out)


def shards(
    block_states,
    token_ids,
    accept,
    cache_lengths,
    cache_keys,
    cache_values,
    w_query,
    w_key,
    w_value,
    w_out,
    attn_gain,
    final_gain,
    embed,
    lm_head,
):
    tok = lax.axis_index("tok")
    other_head = lax.ppermute(lm_head, "head", [(i, i ^ 1) for i in range(16)])
    cache_here = cache_keys.shape[0]
    offsets = jnp.cumsum(cache_lengths) - cache_lengths - tok * cache_here
    begins = jnp.clip(offsets, 0, cache_here)
    ends = jnp.clip(offsets + cache_lengths, 0, cache_here)
    attn_gain = attn_gain.reshape(1, -1)
    final_gain = final_gain.reshape(1, -1)

    vocab_here = embed.shape[0]
    local_ids = token_ids - tok * vocab_here
    inside = (local_ids >= 0) & (local_ids < vocab_here)
    looked_up = jnp.take(embed, jnp.clip(local_ids, 0, vocab_here - 1), axis=0)
    looked_up = jnp.where(inside[:, None], looked_up, jnp.zeros_like(looked_up))

    weights = (w_query, w_key, w_value)
    (rows1, q1, k1, v1), (came,) = comm(
        [
            gather_project(block_states, weights),
            exchange_tok(looked_up.reshape(8, 256, 256)),
        ],
        0,
        "comm_a",
        60,
    )
    embedded = jnp.sum(came.astype(F32), axis=0).astype(BF)
    swapped = jnp.where((accept == 1)[:, None], embedded, block_states)

    (qs1,), (rows2, q2, k2, v2) = comm(
        [gather_queries(q1), gather_project(swapped, weights)], 1, "comm_b", 60
    )
    part1, stat1 = cached_attention(begins, ends, qs1, cache_keys, cache_values)

    (part1, stat1), (qs2,) = comm([exchange_tok(part1, stat1), gather_queries(q2)], 2, "comm_c")
    sum1 = combine(part1, stat1, q1, k1, v1, w_out)
    part2, stat2 = cached_attention(begins, ends, qs2, cache_keys, cache_values)

    (normed, squares), (part2, stat2) = comm(
        [reduce_layer(sum1, rows1, attn_gain, final_gain), exchange_tok(part2, stat2)],
        3,
        "comm_d",
        12,
    )
    second = (part2, stat2, q2, k2, v2, w_out)
    ((top, sums, hiddens),) = comm(
        [gather_logits(normed, squares, lm_head, other_head, second, rows2, attn_gain)],
        4,
        "comm_e",
        56,
    )
    top_logits = top[:, :4].reshape(2, 64, 16).transpose(1, 0, 2).reshape(-1)
    request_norms = jnp.sqrt(sums[4, :8] / (256 * 4096))
    return (hiddens, request_norms, top_logits)


def solution(mesh):
    placed = (
        P("tok", "head"),
        P(),
        P("tok"),
        P(),
        P("tok", "head"),
        P("tok", "head"),
        P(None, "head"),
        P(None, "head"),
        P(None, "head"),
        P("head", None),
        P(),
        P(),
        P("tok", "head"),
        P(("tok", "head"), None),
    )
    return jax.shard_map(
        shards,
        mesh=mesh,
        in_specs=placed,
        out_specs=(P(("tok", "head"), None), P(), P()),
        check_vma=False,
    )
```

```python
import math

import jax
import jax.numpy as jnp
from jax import lax
from jax.experimental import pallas as pl
from jax.experimental.pallas import tpu as pltpu
from jax.sharding import PartitionSpec as P

HEAD_DIM = 128
EPSILON = 1e-06
NEG = -1e30
SCALE2 = (1.0 / math.sqrt(HEAD_DIM)) * math.log2(math.e)
MESH = pl.DeviceIdType.MESH
BF = jnp.bfloat16
F32 = jnp.float32
ANY = pl.BlockSpec(memory_space=pltpu.HBM)
VM = pl.BlockSpec(memory_space=pltpu.VMEM)
REL8 = ((0, 2), (1, 2), (1, 1), (1, 3), (0, 1), (0, 3), (1, 0))


def coords():
    t = lax.axis_index("tok")
    h = lax.axis_index("head")
    return t // 2, lax.rem(t, 2), h // 8, lax.rem(h // 2, 4), lax.rem(h, 2)


def place(z, xl, xh, y, c):
    return (z * 2 + xl, xh * 8 + y * 2 + c)


def ring(v, d):
    return lax.rem(v + d, 4)


class Links:
    def __init__(self, send, recv):
        self.send, self.recv, self.used = send, recv, 0

    def copy(self, src, dst, device):
        k = self.used
        self.used += 1
        cp = pltpu.make_async_remote_copy(
            src_ref=src,
            dst_ref=dst,
            send_sem=self.send.at[k],
            recv_sem=self.recv.at[k],
            device_id=device,
            device_id_type=MESH,
        )
        cp.start()
        return cp


class Task:
    def __init__(self, body, ins, outs, scratch, copies, local, peers):
        self.body, self.ins, self.outs = body, ins, outs
        self.scratch = list(scratch) + [
            pltpu.SemaphoreType.DMA((copies,)),
            pltpu.SemaphoreType.DMA((copies,)),
            pltpu.SemaphoreType.DMA((max(local, 1),)),
        ]
        self.peers = peers


def shift(dx, dy, dz, dc):
    z, xl, xh, y, c = coords()
    c_ = lax.rem(c + dc, 2)
    if dx == "s":
        return place(ring(z, dz), 1 - xl, xh, ring(y, dy), c_)
    x_ = ring(xh * 2 + xl, dx)
    return place(ring(z, dz), lax.rem(x_, 2), x_ // 2, ring(y, dy), c_)


HEAD_AG = [(0, 0, 0, 1), (2, 0, 0, 0), (0, 1, 0, 0), (0, 2, 0, 0), (0, 3, 0, 0)]
HEAD_ALL = [(0, 0, 0, 1)] + [(2 * dx, dy, 0, 0) for dx, dy in REL8]
TOK_AG = [("s", 0, 0, 0), (0, 0, 1, 0), (0, 0, 2, 0), (0, 0, 3, 0)]
TOK_ALL = [("s" if dx else 0, 0, dz, 0) for dx, dz in REL8]
AXES = [(d, 0, 0, 0) for d in (1, 2, 3)] + [(0, d, 0, 0) for d in (1, 2, 3)]
AXES += [(0, 0, d, 0) for d in (1, 2, 3)]
PLANE = [(k // 4, k % 4, 0, 0) for k in range(1, 16)]
DEEP = [(0, 0, k % 4, k // 4) for k in range(1, 8)]


def comm(tasks, cid, name, vmem=4):
    n_in = [len(t.ins) for t in tasks]
    n_out = [len(t.outs) for t in tasks]
    n_scr = [len(t.scratch) for t in tasks]

    def kernel(*refs):
        ins, rest = refs[: sum(n_in)], refs[sum(n_in) :]
        outs, scr = rest[: sum(n_out)], rest[sum(n_out) :]
        peers = {}
        for t in tasks:
            for key in t.peers:
                peers.setdefault(key, shift(*key))
        barrier = pltpu.get_barrier_semaphore()
        for device in peers.values():
            pl.semaphore_signal(barrier, inc=1, device_id=device, device_id_type=MESH)
        pl.semaphore_wait(barrier, len(peers))
        running, a, b, c = [], 0, 0, 0
        for k, t in enumerate(tasks):
            running.append(
                t.body(
                    ins[a : a + n_in[k]], outs[b : b + n_out[k]], scr[c : c + n_scr[k]]
                )
            )
            a, b, c = a + n_in[k], b + n_out[k], c + n_scr[k]
        while running:
            again = []
            for g in running:
                if next(g, StopIteration) is not StopIteration:
                    again.append(g)
            running = again

    flat = pl.pallas_call(
        kernel,
        out_shape=[o[0] for t in tasks for o in t.outs],
        in_specs=[i[1] for t in tasks for i in t.ins],
        out_specs=[o[1] for t in tasks for o in t.outs],
        scratch_shapes=[s for t in tasks for s in t.scratch],
        compiler_params=pltpu.CompilerParams(
            collective_id=cid, has_side_effects=True, vmem_limit_bytes=vmem << 20
        ),
        name=name,
    )(*[i[0] for t in tasks for i in t.ins])
    res, b = [], 0
    for n in n_out:
        res.append(flat[b : b + n])
        b += n
    return res


def gather_project(x, weights):
    rows, wide = x.shape

    def body(ins, outs, scr):
        x_ref, w_refs = ins[0], ins[1:]
        own_rows, outs = outs[0], outs[1:]
        f_ref, w_ref, acc, send, recv, loc = scr
        z, xl, xh, y, c = coords()
        links = Links(send, recv)

        def index(xh_, y_, c_):
            return xh_ * 8 + y_ * 2 + c_

        def slot(*at):
            return f_ref.at[index(*at)]

        def absorb(*at):
            k = index(*at)
            v = f_ref[k]
            for n in range(3):
                w = w_ref[n, pl.ds(pl.multiple_of(k * wide, wide), wide), :]
                acc[n] += jnp.dot(v, w, preferred_element_type=F32)

        core = place(z, xl, xh, y, 1 - c)
        own = slot(xh, y, c)
        keep = pltpu.make_async_copy(x_ref, own, loc.at[0])
        keep.start()
        landed = []
        over_x = links.copy(x_ref, own, place(z, xl, 1 - xh, y, c))
        over_y = {d: links.copy(x_ref, own, place(z, xl, xh, ring(y, d), c)) for d in (2, 1, 3)}
        landed.append(links.copy(x_ref, own, core))
        loads = [pltpu.make_async_copy(w_refs[n], w_ref.at[n], loc.at[1 + n]) for n in range(3)]
        for cp in loads:
            cp.start()
        acc[...] = jnp.zeros_like(acc)
        yield 0
        over_x.wait_recv()
        far = slot(1 - xh, y, c)
        far_y = {d: links.copy(far, far, place(z, xl, xh, ring(y, d), c)) for d in (2, 1, 3)}
        landed.append(links.copy(far, far, core))
        yield 0
        keep.wait()
        for cp in loads:
            cp.wait()
        absorb(xh, y, c)
        absorb(1 - xh, y, c)
        for k, xh_ in enumerate((xh, 1 - xh)):
            landed[k].wait_recv()
            absorb(xh_, y, 1 - c)
        yield 0
        for xh_, arrive in ((xh, over_y), (1 - xh, far_y)):
            for d in (1, 3, 2):
                y_ = ring(y, 4 - d)
                arrive[d].wait_recv()
                got = slot(xh_, y_, c)
                landed.append(links.copy(got, got, core))
                absorb(xh_, y_, c)
            for k, d in enumerate((1, 3, 2)):
                landed[k - 3].wait_recv()
                absorb(xh_, ring(y, 4 - d), 1 - c)
            yield 0
        h = pl.multiple_of(index(xh, y, c) * 16, 16)
        for k in range(16):
            own_rows[:, k * wide : (k + 1) * wide] = f_ref[k, pl.ds(h, 16), :]
        for n in range(3):
            outs[n][...] = acc[n].astype(BF)
        for cp in [over_x] + list(over_y.values()) + list(far_y.values()) + landed:
            cp.wait_send()

    return Task(
        body,
        [(x, ANY)] + [(w, ANY) for w in weights],
        [(jax.ShapeDtypeStruct((16, 16 * wide), BF), VM)]
        + [(jax.ShapeDtypeStruct((rows, wide), BF), VM)] * 3,
        [
            pltpu.VMEM((16, rows, wide), BF),
            pltpu.VMEM((3, 16 * wide, wide), BF),
            pltpu.VMEM((3, rows, wide), F32),
        ],
        15,
        4,
        HEAD_AG,
    )


def gather_queries(q):
    def body(ins, outs, scr):
        (q_ref,), (o_ref,), (send, recv, loc) = ins, outs, scr
        z, xl, xh, y, c = coords()
        links = Links(send, recv)
        own = o_ref.at[z * 2 + xl]
        keep = pltpu.make_async_copy(q_ref, own, loc.at[0])
        keep.start()
        side = place(z, 1 - xl, xh, y, c)
        over_x = [links.copy(q_ref, own, side)]
        over_z = {d: links.copy(q_ref, own, place(ring(z, d), xl, xh, y, c)) for d in (2, 1, 3)}
        yield 0
        over_x[0].wait_recv()
        far = o_ref.at[z * 2 + 1 - xl, pl.ds(0, 128)]
        more = [links.copy(far, far, place(ring(z, d), xl, xh, y, c)) for d in (2, 1, 3)]
        yield 0
        for d in (1, 3, 2):
            over_z[d].wait_recv()
            got = o_ref.at[ring(z, 4 - d) * 2 + xl, pl.ds(128, 128)]
            over_x.append(links.copy(got, got, side))
        yield 0
        for cp in over_x[1:] + more:
            cp.wait_recv()
        for cp in over_x + more + list(over_z.values()):
            cp.wait_send()
        keep.wait()

    return Task(
        body, [(q, ANY)], [(jax.ShapeDtypeStruct((8, 256, 256), BF), ANY)], [], 10, 1, TOK_AG
    )


def exchange_tok(*arrays):
    def body(ins, outs, scr):
        send, recv, loc = scr
        z, xl, xh, y, c = coords()
        t = z * 2 + xl
        links = Links(send, recv)
        keep, cps = [], []
        for k, (src, dst) in enumerate(zip(ins, outs)):
            keep.append(pltpu.make_async_copy(src.at[t], dst.at[t], loc.at[k]))
            keep[-1].start()
        for dx, dz in REL8:
            z_, xl_ = ring(z, dz), lax.rem(xl + dx, 2)
            for src, dst in zip(ins, outs):
                cps.append(links.copy(src.at[z_ * 2 + xl_], dst.at[t], place(z_, xl_, xh, y, c)))
        yield 0
        for cp in cps:
            cp.wait()
        for cp in keep:
            cp.wait()

    n = len(arrays)
    return Task(
        body,
        [(a, ANY) for a in arrays],
        [(jax.ShapeDtypeStruct(a.shape, a.dtype), ANY) for a in arrays],
        [],
        7 * n,
        n,
        TOK_ALL,
    )


def exchange_embedded(embed, slots, block_states, accept):
    vocab, wide = embed.shape
    piece = vocab // 4
    strip = piece // 7

    def body(ins, outs, scr):
        table_ref, slot_ref, old_ref, acc_ref = ins
        (new_ref,) = outs
        raw, table, stage, parts, came, send, recv, loc = scr
        z, xl, xh, y, c = coords()
        t = z * 2 + xl
        links = Links(send, recv)
        loads = [
            pltpu.make_async_copy(table_ref.at[pl.ds(k * piece, piece)], raw.at[k], loc.at[k])
            for k in range(4)
        ]
        for cp in loads:
            cp.start()
        table[pl.ds(vocab, 8), :] = jnp.zeros((8, wide), F32)
        for k in range(4):
            loads[k].wait()

            def widen(j, carry, k=k):
                at = pl.multiple_of(j * strip, strip)
                to = pl.multiple_of(k * piece + j * strip, strip)
                table[pl.ds(to, strip), :] = raw[k, pl.ds(at, strip), :].astype(F32)
                return carry

            lax.fori_loop(0, 7, widen, 0)
        yield 0

        def look_up(owner):
            def rows(j, carry):
                for k in range(16):
                    n = j * 16 + k
                    stage[pl.ds(n, 1), :] = table[pl.ds(slot_ref[owner * 256 + n], 1), :]
                return carry

            lax.fori_loop(0, 16, rows, 0)
            parts[owner] = stage[...].astype(BF)

        cps, sources = [], []
        for dx, dz in REL8:
            z_, xl_ = ring(z, dz), lax.rem(xl + dx, 2)
            look_up(z_ * 2 + xl_)
            cps.append(
                links.copy(parts.at[z_ * 2 + xl_], came.at[t], place(z_, xl_, xh, y, c))
            )
            sources.append(z_ * 2 + xl_)
        look_up(t)
        yield 0
        yield 0
        yield 0
        yield 0
        total = parts[t].astype(F32)
        for cp in cps:
            cp.wait()
        for source in sources:
            total = total + came[source].astype(F32)
        new_ref[...] = jnp.where(acc_ref[...] == 1, total, old_ref[...].astype(F32)).astype(BF)

    return Task(
        body,
        [
            (embed, ANY),
            (slots, pl.BlockSpec(memory_space=pltpu.SMEM)),
            (block_states, VM),
            (accept, VM),
        ],
        [(jax.ShapeDtypeStruct(block_states.shape, BF), VM)],
        [
            pltpu.VMEM((4, piece, wide), BF),
            pltpu.VMEM((vocab + 8, wide), F32),
            pltpu.VMEM((256, wide), F32),
            pltpu.VMEM((8, 256, wide), BF),
            pltpu.VMEM((8, 256, wide), BF),
        ],
        7,
        4,
        TOK_ALL,
    )


def unit_rows(v):
    return v * lax.rsqrt(jnp.mean(v * v, axis=-1, keepdims=True) + EPSILON)


def layer_end(before, total, gain):
    return (before.astype(F32) + unit_rows(total) * gain).astype(BF)


def reduce_layer(part, states_in, attn_gain, final_gain):
    def body(ins, outs, scr):
        part_ref, x_ref, again_ref, fgain_ref = ins
        mine, theirs, came, far, send, recv, loc = scr
        z, xl, xh, y, c = coords()
        links = Links(send, recv)
        cps = []
        l0 = pltpu.make_async_copy(part_ref.at[:, :, c], mine, loc.at[0])
        l0.start()
        swap = links.copy(part_ref.at[:, :, 1 - c], theirs, place(z, xl, xh, y, 1 - c))
        yield 0
        l0.wait()
        swap.wait_recv()

        def both(xh_, y_):
            return mine[xh_, y_].astype(F32) + theirs[xh_, y_].astype(F32)

        for dy in (2, 1, 3):
            y_ = ring(y, dy)
            for xh_ in (0, 1):
                mine[xh_, y_] = both(xh_, y_).astype(BF)
            cps.append(links.copy(mine.at[:, y_], came.at[:, y], place(z, xl, xh, y_, c)))
        total, away = both(xh, y), both(1 - xh, y)
        yield 0
        for cp in cps:
            cp.wait_recv()
        for dy in (1, 3, 2):
            y_ = ring(y, dy)
            away = away + came[1 - xh, y_].astype(F32)
            total = total + came[xh, y_].astype(F32)
        mine[1 - xh, y] = away.astype(BF)
        over = links.copy(mine.at[1 - xh, y], far, place(z, xl, 1 - xh, y, c))
        yield 0
        over.wait()
        total = total + far[...].astype(F32)
        for cp in cps:
            cp.wait_send()
        swap.wait_send()
        wide = layer_end(x_ref[...], total, again_ref[...]).astype(F32)
        squares = jnp.sum(wide * wide, axis=-1, keepdims=True)
        normed = wide * lax.rsqrt(squares * (1.0 / 4096) + EPSILON) * fgain_ref[...]
        outs[0][...] = normed.astype(BF)
        lane = lax.broadcasted_iota(jnp.int32, (8, 256), 1)
        row = lax.broadcasted_iota(jnp.int32, (8, 256), 0)
        outs[1][...] = jnp.where((lane == z * 2 + xl) & (row == 4), jnp.sum(squares), 0.0)

    block = pltpu.VMEM((2, 4, 16, 4096), BF)
    return Task(
        body,
        [(part, ANY), (states_in, VM), (attn_gain, VM), (final_gain, VM)],
        [(jax.ShapeDtypeStruct((16, 4096), BF), VM), (jax.ShapeDtypeStruct((8, 256), F32), VM)],
        [block, block, block, pltpu.VMEM((16, 4096), BF)],
        8,
        1,
        HEAD_AG,
    )


def along(axis, d):
    return shift(*{"x": (d, 0, 0, 0), "y": (0, d, 0, 0), "z": (0, 0, d, 0)}[axis])


CHUNKS = ((512, 512, 512), (512, 512, 512), (384, 384, 256))
STARTS = (0, 1536, 3072, 4096)
ORDERS = ("xyz", "yzx", "zxy")


def gather_logits(normed, squares, own_head, other_head, second, states_in, attn_gain):
    vocab = own_head.shape[0]
    n = len(CHUNKS)

    def body(ins, outs, scr):
        n_ref, sq_ref, x_ref, again_ref, own_ref, other_ref = ins[:6]
        top_ref, sum_ref, hid_ref = outs
        bufs = [scr[3 * i : 3 * i + 3] for i in range(n)]
        heads, acc = scr[9:11]
        held = scr[11:17]
        att, out, theirs, came, far, maxima, wide, deep, send, recv, loc = scr[17:]
        z, xl, xh, y, c = coords()
        x = xh * 2 + xl
        links = Links(send, recv)
        full = slice(None)
        loads = [
            pltpu.make_async_copy(src, heads.at[k], loc.at[k])
            for k, src in enumerate((own_ref, other_ref))
        ]

        def block(i, p, known, step=0, half=None):
            last = ORDERS[p][2]
            z_, y_, x_ = z, y, x
            if step:
                if last == "z":
                    z_ = ring(z, step)
                elif last == "y":
                    y_ = ring(y, step)
                else:
                    x_ = ring(x, step)
            at = [
                full if "z" in known else z_,
                full if "x" in known else lax.rem(x_, 2),
                full if "x" in known else x_ // 2,
                full if "y" in known else y_,
            ]
            if half is not None:
                if last == "z":
                    at[1] = half
                else:
                    at[0] = pl.ds(2 * half, 2)
            return bufs[i][p].at[tuple(at)]

        start = 0
        for i in range(n):
            for p in range(3):
                bufs[i][p][z, xl, xh, y] = n_ref[:, start : start + CHUNKS[i][p]]
                start += CHUNKS[i][p]

        everything = []

        def push(i, p, ref, axis, d):
            cp = links.copy(ref, ref, along(axis, d))
            everything.append(cp)
            return cp

        def spread(i, stage, before):
            out = []
            for p in range(3):
                if before is not None:
                    for cp in before[p]:
                        cp.wait_recv()
                ref = block(i, p, ORDERS[p][:stage])
                ds = (2, 1, 3) if stage < 2 else (1, 3)
                out.append([push(i, p, ref, ORDERS[p][stage], d) for d in ds])
            return out

        def relay(i, before):
            out = []
            for p in range(3):
                axis, known = ORDERS[p][2], ORDERS[p][:2]
                before[p][0].wait_recv()
                lower = push(i, p, block(i, p, known, 3, 0), axis, 1)
                before[p][1].wait_recv()
                upper = push(i, p, block(i, p, known, 1, 1), axis, 3)
                out.append([lower, upper])
            return out

        def multiply(i):
            cut = pl.ds(STARTS[i], STARTS[i + 1] - STARTS[i])

            def step(r, carry):
                rows = jnp.concatenate(
                    [bufs[i][p][r].reshape(256, CHUNKS[i][p]) for p in range(3)], axis=1
                )
                top = None
                for k in range(2):
                    part = lax.dot_general(
                        heads[k, :, cut], rows, (((1,), (1,)), ((), ())), preferred_element_type=F32
                    )
                    if i > 0:
                        part = acc[k, r] + part
                    if i < n - 1:
                        acc[k, r] = part
                    else:
                        m = jnp.max(part, axis=0, keepdims=True)
                        top = m if top is None else jnp.maximum(top, m)
                if i == n - 1:
                    maxima[0, pl.ds(r, 1), :] = top
                return carry

            lax.fori_loop(0, 4, step, 0)

        fetch = [
            pltpu.make_async_copy(src, dst, loc.at[2 + k])
            for k, (src, dst) in enumerate(zip(ins[6:], held))
        ]
        one = [spread(i, 0, None) for i in range(n)]
        for cp in fetch + loads:
            cp.start()
        two = [spread(i, 1, one[i]) for i in range(n)]
        three = {0: spread(0, 2, two[0]), 1: spread(1, 2, two[1])}
        for cp in fetch:
            cp.wait()
        attend(*held[:5], att)

        def times_out(k, carry):
            cut = pl.ds(pl.multiple_of(k * 1024, 1024), 1024)
            o = jnp.dot(att[...], held[5][:, cut], preferred_element_type=F32).astype(BF)
            out[:, :, :, :, cut] = o.reshape(2, 4, 2, 16, 1024)
            return carry

        lax.fori_loop(0, 4, times_out, 0)
        swap = links.copy(out.at[:, :, 1 - c], theirs, shift(0, 0, 0, 1))
        over_y = []
        four = {0: relay(0, three[0])}
        for i in range(n):
            if i + 1 < n:
                four[i + 1] = relay(i + 1, three[i + 1])
            if i + 2 < n:
                three[i + 2] = spread(i + 2, 2, two[i + 2])
            if i == n - 2:
                swap.wait()
                for dy in (2, 1, 3, 0):
                    y_ = ring(y, dy)
                    for xh_ in (0, 1):
                        v = out[xh_, y_, c].astype(F32) + theirs[xh_, y_].astype(F32)
                        theirs[xh_, y_] = v.astype(BF)
                    if dy:
                        over_y.append(
                            links.copy(
                                theirs.at[:, y_], came.at[:, y], place(z, xl, xh, y_, c)
                            )
                        )
            for pair in four[i]:
                for cp in pair:
                    cp.wait_recv()
            if i == 0:
                for cp in loads:
                    cp.wait()
            if i == n - 1:
                maxima[0] = sq_ref[...]
            multiply(i)
        top = lax.broadcasted_iota(jnp.int32, (8, 256), 0) < 4

        def join(v, w):
            return jnp.where(top, jnp.maximum(v, w), v + w)

        flat = [links.copy(maxima.at[0], wide.at[k], shift(*key)) for k, key in enumerate(PLANE)]
        for cp in flat:
            cp.wait()
        mine = maxima[0]
        for k in range(15):
            mine = join(mine, wide[k])
        maxima[1] = mine
        tall = [links.copy(maxima.at[1], deep.at[k], shift(*key)) for k, key in enumerate(DEEP)]
        for cp in over_y:
            cp.wait_recv()
        for xh_ in (0, 1):
            v = theirs[xh_, y].astype(F32)
            for dy in (1, 3, 2):
                v = v + came[xh_, ring(y, dy)].astype(F32)
            theirs[xh_, y] = v.astype(BF)
        over_x = links.copy(theirs.at[1 - xh, y], far, place(z, xl, 1 - xh, y, c))
        for cp in tall:
            cp.wait()
        for k in range(3):
            mine = join(mine, deep[k])
        other = deep[3]
        for k in range(4, 7):
            other = join(other, deep[k])
        even = jnp.where(c == 0, mine, other)
        odd = jnp.where(c == 0, other, mine)
        group = lax.broadcasted_iota(jnp.int32, (8, 128), 1) // 16
        for q in range(4):
            row = jnp.zeros((8, 128), F32)
            for a in range(4):
                for k, v in enumerate((even, odd)):
                    half = v[:, q // 2 * 128 : q // 2 * 128 + 128]
                    turn = (a * 16 + k * 16 - q % 2 * 64) % 128
                    turned = pltpu.roll(half, turn, 1) if turn else half
                    row = jnp.where(group == 2 * a + k, turned, row)
            top_ref[:, q * 128 : q * 128 + 128] = row[:4]
        sum_ref[...] = jnp.sqrt((mine + other) * (1.0 / (256 * 4096)))
        over_x.wait_recv()
        total = theirs[xh, y].astype(F32) + far[...].astype(F32)
        hid_ref[...] = layer_end(x_ref[...], total, again_ref[...])
        everything += over_y + [over_x]
        for cp in everything:
            cp.wait_send()
        yield 0

    scratch = [pltpu.VMEM((4, 2, 2, 4, 16, w), BF) for ws in CHUNKS for w in ws]
    scratch += [pltpu.VMEM((2, vocab, 4096), BF), pltpu.VMEM((2, 4, vocab, 256), F32)]
    scratch += [pltpu.VMEM(a.shape, a.dtype) for a in second]
    scratch += [
        pltpu.VMEM((256, 256), BF),
        pltpu.VMEM((2, 4, 2, 16, 4096), BF),
        pltpu.VMEM((2, 4, 16, 4096), BF),
        pltpu.VMEM((2, 4, 16, 4096), BF),
        pltpu.VMEM((16, 4096), BF),
        pltpu.VMEM((2, 8, 256), F32),
        pltpu.VMEM((15, 8, 256), F32),
        pltpu.VMEM((7, 8, 256), F32),
    ]
    return Task(
        body,
        [(normed, VM), (squares, VM), (states_in, VM), (attn_gain, VM)]
        + [(a, ANY) for a in (own_head, other_head) + second],
        [
            (jax.ShapeDtypeStruct((4, 512), F32), VM),
            (jax.ShapeDtypeStruct((8, 256), F32), VM),
            (jax.ShapeDtypeStruct((16, 4096), BF), VM),
        ],
        scratch,
        3 * 3 * 10 + 5 + 22,
        8,
        AXES + PLANE + DEEP,
    )


def scores(q, k):
    return lax.dot_general(q, k, (((1,), (1,)), ((), ())), preferred_element_type=F32) * SCALE2


def cached_attention(begins, ends, queries, keys, values):
    rows = queries.shape[1]
    cuts = [slice(g * HEAD_DIM, (g + 1) * HEAD_DIM) for g in (0, 1)]

    def kernel(lo_ref, hi_ref, q_ref, k_ref, v_ref, o_ref, s_ref, v_sc, m_sc, a_sc):
        for g in range(2):
            v_sc[g, :, :HEAD_DIM] = v_ref[:, g * HEAD_DIM : (g + 1) * HEAD_DIM]
            v_sc[g, :, HEAD_DIM:] = jnp.ones((v_ref.shape[0], HEAD_DIM), BF)
        lane = lax.broadcasted_iota(jnp.int32, (rows, 128), 1)
        sub = lax.broadcasted_iota(jnp.int32, (8, rows), 0)

        def request(r, carry):
            lo, hi = lo_ref[r], hi_ref[r]

            @pl.when(hi <= lo)
            def _():
                o_ref[r] = jnp.zeros(o_ref.shape[1:], BF)
                s_ref[r] = jnp.where(sub < 2, NEG, 0.0)

            @pl.when(hi > lo)
            def _():
                m_sc[...] = jnp.full_like(m_sc, NEG)
                a_sc[...] = jnp.zeros_like(a_sc)

                def step(b, span):
                    at = pl.multiple_of(b * span, span)
                    pos = at + lax.broadcasted_iota(jnp.int32, (1, span), 1)
                    bias = jnp.where((pos >= lo) & (pos < hi), 0.0, NEG)
                    ss = [scores(q_ref[r, :, cut], k_ref[pl.ds(at, span), cut]) for cut in cuts]
                    ss = [s + bias for s in ss]
                    old = [m_sc[g] for g in (0, 1)]
                    new = [
                        jnp.maximum(o, jnp.max(s, axis=-1, keepdims=True)) for o, s in zip(old, ss)
                    ]
                    ps = [jnp.exp2(s - m[:, 0:1]).astype(BF) for s, m in zip(ss, new)]
                    fs = [jnp.exp2(o - m) for o, m in zip(old, new)]
                    ds = [
                        jnp.dot(p, v_sc[g, pl.ds(at, span), :], preferred_element_type=F32)
                        for g, p in enumerate(ps)
                    ]
                    for g in (0, 1):
                        a_sc[g] = a_sc[g] * jnp.concatenate([fs[g], fs[g]], axis=1) + ds[g]
                        m_sc[g] = new[g]

                small = lo // 256 == (hi - 1) // 256

                @pl.when(small)
                def _():
                    step(lo // 256, 256)

                @pl.when(jnp.logical_not(small))
                def _():
                    def wide_step(b, carry):
                        step(b, 512)
                        return carry

                    lax.fori_loop(lo // 512, (hi + 511) // 512, wide_step, 0)

                stats = jnp.where(lane == 0, m_sc[0], m_sc[1])
                stats = jnp.where(lane == 2, a_sc[0, :, HEAD_DIM:], stats)
                stats = jnp.where(lane == 3, a_sc[1, :, HEAD_DIM:], stats)
                s_ref[r] = jnp.transpose(stats)[:8]
                for g in range(2):
                    o_ref[r, :, g * HEAD_DIM : (g + 1) * HEAD_DIM] = a_sc[g, :, :HEAD_DIM].astype(BF)

            return carry

        lax.fori_loop(0, 8, request, 0)

    smem = pl.BlockSpec(memory_space=pltpu.SMEM)
    return pl.pallas_call(
        kernel,
        in_specs=[smem, smem, VM, VM, VM],
        out_specs=[VM, VM],
        scratch_shapes=[
            pltpu.VMEM((2, values.shape[0], 256), BF),
            pltpu.VMEM((2, rows, 128), F32),
            pltpu.VMEM((2, rows, 256), F32),
        ],
        out_shape=[
            jax.ShapeDtypeStruct((8, rows, 256), BF),
            jax.ShapeDtypeStruct((8, 8, rows), F32),
        ],
        compiler_params=pltpu.CompilerParams(vmem_limit_bytes=16 << 20),
        name="cached",
    )(begins, ends, queries, keys, values)


def attend(p_ref, s_ref, q_ref, k_ref, v_ref, att):
    st = jnp.concatenate([s_ref[...].reshape(64, 256), jnp.zeros((64, 256), F32)], axis=0)
    st = jnp.transpose(st)
    for g in range(2):
        cut = slice(g * HEAD_DIM, (g + 1) * HEAD_DIM)
        s = scores(q_ref[:, cut], k_ref[:, cut])
        top = jnp.max(s, axis=-1, keepdims=True)
        for i in range(8):
            top = jnp.maximum(top, st[:, i * 8 + g : i * 8 + g + 1])
        p = jnp.exp2(s - top)
        mass = jnp.sum(p, axis=-1, keepdims=True)
        acc = jnp.dot(p.astype(BF), v_ref[:, cut], preferred_element_type=F32)
        for i in range(8):
            f = jnp.exp2(st[:, i * 8 + g : i * 8 + g + 1] - top)
            mass = mass + f * st[:, i * 8 + g + 2 : i * 8 + g + 3]
            acc = acc + f * p_ref[i, :, cut].astype(F32)
        att[:, cut] = (acc / mass).astype(BF)


def combine(parts, stats, q, k, v, w_out):
    steps = 4
    wide = w_out.shape[1] // steps

    def kernel(p_ref, s_ref, q_ref, k_ref, v_ref, w_ref, o_ref, att):
        @pl.when(pl.program_id(0) == 0)
        def _():
            attend(p_ref, s_ref, q_ref, k_ref, v_ref, att)

        o = jnp.dot(att[...], w_ref[...], preferred_element_type=F32).astype(BF)
        o_ref[...] = o.reshape(o_ref.shape)

    def whole(a):
        return pl.BlockSpec(a.shape, lambda i: (0,) * a.ndim)

    return pl.pallas_call(
        kernel,
        grid=(steps,),
        in_specs=[whole(a) for a in (parts, stats, q, k, v)]
        + [pl.BlockSpec((256, wide), lambda i: (0, i))],
        out_specs=pl.BlockSpec((2, 4, 2, 16, wide), lambda i: (0, 0, 0, 0, i)),
        out_shape=jax.ShapeDtypeStruct((2, 4, 2, 16, w_out.shape[1]), BF),
        scratch_shapes=[pltpu.VMEM((256, 256), BF)],
        compiler_params=pltpu.CompilerParams(vmem_limit_bytes=16 << 20),
        name="combine",
    )(parts, stats, q, k, v, w_out)


def shards(
    block_states,
    token_ids,
    accept,
    cache_lengths,
    cache_keys,
    cache_values,
    w_query,
    w_key,
    w_value,
    w_out,
    attn_gain,
    final_gain,
    embed,
    lm_head,
):
    tok = lax.axis_index("tok")
    other_head = lax.ppermute(lm_head, "head", [(i, i ^ 1) for i in range(16)])
    cache_here = cache_keys.shape[0]
    offsets = jnp.cumsum(cache_lengths) - cache_lengths - tok * cache_here
    begins = jnp.clip(offsets, 0, cache_here)
    ends = jnp.clip(offsets + cache_lengths, 0, cache_here)
    attn_gain = attn_gain.reshape(1, -1)
    final_gain = final_gain.reshape(1, -1)

    vocab_here = embed.shape[0]
    local_ids = token_ids - tok * vocab_here
    inside = (local_ids >= 0) & (local_ids < vocab_here)
    slots = jnp.where(inside, local_ids, vocab_here)

    weights = (w_query, w_key, w_value)
    (rows1, q1, k1, v1), (swapped,) = comm(
        [
            gather_project(block_states, weights),
            exchange_embedded(embed, slots, block_states, accept.reshape(-1, 1)),
        ],
        0,
        "comm_a",
        60,
    )

    (qs1,), (rows2, q2, k2, v2) = comm(
        [gather_queries(q1), gather_project(swapped, weights)], 1, "comm_b", 60
    )
    part1, stat1 = cached_attention(begins, ends, qs1, cache_keys, cache_values)

    (part1, stat1), (qs2,) = comm([exchange_tok(part1, stat1), gather_queries(q2)], 2, "comm_c")
    sum1 = combine(part1, stat1, q1, k1, v1, w_out)
    part2, stat2 = cached_attention(begins, ends, qs2, cache_keys, cache_values)

    (normed, squares), (part2, stat2) = comm(
        [reduce_layer(sum1, rows1, attn_gain, final_gain), exchange_tok(part2, stat2)],
        3,
        "comm_d",
        12,
    )
    second = (part2, stat2, q2, k2, v2, w_out)
    ((top, sums, hiddens),) = comm(
        [gather_logits(normed, squares, lm_head, other_head, second, rows2, attn_gain)],
        4,
        "comm_e",
        52,
    )
    return (hiddens, sums[4, :8], top.reshape(-1))


def solution(mesh):
    placed = (
        P("tok", "head"),
        P(),
        P("tok"),
        P(),
        P("tok", "head"),
        P("tok", "head"),
        P(None, "head"),
        P(None, "head"),
        P(None, "head"),
        P("head", None),
        P(),
        P(),
        P("tok", "head"),
        P(("tok", "head"), None),
    )
    return jax.shard_map(
        shards,
        mesh=mesh,
        in_specs=placed,
        out_specs=(P(("tok", "head"), None), P(), P()),
        check_vma=False,
    )
```

```python
import math

import jax
import jax.numpy as jnp
from jax import lax
from jax.experimental import pallas as pl
from jax.experimental.pallas import tpu as pltpu
from jax.sharding import PartitionSpec as P

HEAD_DIM = 128
EPSILON = 1e-06
NEG = -1e30
SCALE2 = (1.0 / math.sqrt(HEAD_DIM)) * math.log2(math.e)
MESH = pl.DeviceIdType.MESH
BF = jnp.bfloat16
F32 = jnp.float32
ANY = pl.BlockSpec(memory_space=pltpu.HBM)
VM = pl.BlockSpec(memory_space=pltpu.VMEM)
REL8 = ((0, 2), (1, 2), (1, 1), (1, 3), (0, 1), (0, 3), (1, 0))


def coords():
    t = lax.axis_index("tok")
    h = lax.axis_index("head")
    return t // 2, lax.rem(t, 2), h // 8, lax.rem(h // 2, 4), lax.rem(h, 2)


def place(z, xl, xh, y, c):
    return (z * 2 + xl, xh * 8 + y * 2 + c)


def ring(v, d):
    return lax.rem(v + d, 4)


class Links:
    def __init__(self, send, recv):
        self.send, self.recv, self.used = send, recv, 0

    def copy(self, src, dst, device):
        k = self.used
        self.used += 1
        cp = pltpu.make_async_remote_copy(
            src_ref=src,
            dst_ref=dst,
            send_sem=self.send.at[k],
            recv_sem=self.recv.at[k],
            device_id=device,
            device_id_type=MESH,
        )
        cp.start()
        return cp


class Task:
    def __init__(self, body, ins, outs, scratch, copies, local, peers):
        self.body, self.ins, self.outs = body, ins, outs
        self.scratch = list(scratch) + [
            pltpu.SemaphoreType.DMA((copies,)),
            pltpu.SemaphoreType.DMA((copies,)),
            pltpu.SemaphoreType.DMA((max(local, 1),)),
        ]
        self.peers = peers


def shift(dx, dy, dz, dc):
    z, xl, xh, y, c = coords()
    c_ = lax.rem(c + dc, 2)
    if dx == "s":
        return place(ring(z, dz), 1 - xl, xh, ring(y, dy), c_)
    x_ = ring(xh * 2 + xl, dx)
    return place(ring(z, dz), lax.rem(x_, 2), x_ // 2, ring(y, dy), c_)


HEAD_AG = [(0, 0, 0, 1), (2, 0, 0, 0), (0, 1, 0, 0), (0, 2, 0, 0), (0, 3, 0, 0)]
HEAD_ALL = [(0, 0, 0, 1)] + [(2 * dx, dy, 0, 0) for dx, dy in REL8]
TOK_AG = [("s", 0, 0, 0), (0, 0, 1, 0), (0, 0, 2, 0), (0, 0, 3, 0)]
TOK_ALL = [("s" if dx else 0, 0, dz, 0) for dx, dz in REL8]
AXES = [(d, 0, 0, 0) for d in (1, 2, 3)] + [(0, d, 0, 0) for d in (1, 2, 3)]
AXES += [(0, 0, d, 0) for d in (1, 2, 3)]
PLANE = [(k // 4, k % 4, 0, 0) for k in range(1, 16)]
DEEP = [(0, 0, k % 4, k // 4) for k in range(1, 8)]


def comm(tasks, cid, name, vmem=4):
    n_in = [len(t.ins) for t in tasks]
    n_out = [len(t.outs) for t in tasks]
    n_scr = [len(t.scratch) for t in tasks]

    def kernel(*refs):
        ins, rest = refs[: sum(n_in)], refs[sum(n_in) :]
        outs, scr = rest[: sum(n_out)], rest[sum(n_out) :]
        peers = {}
        for t in tasks:
            for key in t.peers:
                peers.setdefault(key, shift(*key))
        barrier = pltpu.get_barrier_semaphore()
        for device in peers.values():
            pl.semaphore_signal(barrier, inc=1, device_id=device, device_id_type=MESH)
        pl.semaphore_wait(barrier, len(peers))
        running, a, b, c = [], 0, 0, 0
        for k, t in enumerate(tasks):
            running.append(
                t.body(
                    ins[a : a + n_in[k]], outs[b : b + n_out[k]], scr[c : c + n_scr[k]]
                )
            )
            a, b, c = a + n_in[k], b + n_out[k], c + n_scr[k]
        while running:
            again = []
            for g in running:
                if next(g, StopIteration) is not StopIteration:
                    again.append(g)
            running = again

    flat = pl.pallas_call(
        kernel,
        out_shape=[o[0] for t in tasks for o in t.outs],
        in_specs=[i[1] for t in tasks for i in t.ins],
        out_specs=[o[1] for t in tasks for o in t.outs],
        scratch_shapes=[s for t in tasks for s in t.scratch],
        compiler_params=pltpu.CompilerParams(
            collective_id=cid, has_side_effects=True, vmem_limit_bytes=vmem << 20
        ),
        name=name,
    )(*[i[0] for t in tasks for i in t.ins])
    res, b = [], 0
    for n in n_out:
        res.append(flat[b : b + n])
        b += n
    return res


def project_steps(links, keep_sem, x_ref, f_ref, w_ref, acc, loads, own_rows, outs):
    wide = x_ref.shape[1]
    z, xl, xh, y, c = coords()

    def index(xh_, y_, c_):
        return xh_ * 8 + y_ * 2 + c_

    def slot(*at):
        return f_ref.at[index(*at)]

    def absorb(*at):
        k = index(*at)
        v = f_ref[k]
        for n in range(3):
            w = w_ref[n, pl.ds(pl.multiple_of(k * wide, wide), wide), :]
            acc[n] += jnp.dot(v, w, preferred_element_type=F32)

    core = place(z, xl, xh, y, 1 - c)
    own = slot(xh, y, c)
    keep = pltpu.make_async_copy(x_ref, own, keep_sem)
    keep.start()
    landed = []
    over_x = links.copy(x_ref, own, place(z, xl, 1 - xh, y, c))
    over_y = {d: links.copy(x_ref, own, place(z, xl, xh, ring(y, d), c)) for d in (2, 1, 3)}
    landed.append(links.copy(x_ref, own, core))
    acc[...] = jnp.zeros_like(acc)
    yield 0
    over_x.wait_recv()
    far = slot(1 - xh, y, c)
    far_y = {d: links.copy(far, far, place(z, xl, xh, ring(y, d), c)) for d in (2, 1, 3)}
    landed.append(links.copy(far, far, core))
    yield 0
    keep.wait()
    for cp in loads:
        cp.wait()
    absorb(xh, y, c)
    absorb(1 - xh, y, c)
    for k, xh_ in enumerate((xh, 1 - xh)):
        landed[k].wait_recv()
        absorb(xh_, y, 1 - c)
    yield 0
    for xh_, arrive in ((xh, over_y), (1 - xh, far_y)):
        for d in (1, 3, 2):
            y_ = ring(y, 4 - d)
            arrive[d].wait_recv()
            got = slot(xh_, y_, c)
            landed.append(links.copy(got, got, core))
            absorb(xh_, y_, c)
        for k, d in enumerate((1, 3, 2)):
            landed[k - 3].wait_recv()
            absorb(xh_, ring(y, 4 - d), 1 - c)
        yield 0
    h = pl.multiple_of(index(xh, y, c) * 16, 16)
    for k in range(16):
        own_rows[:, k * wide : (k + 1) * wide] = f_ref[k, pl.ds(h, 16), :]
    for n in range(3):
        outs[n][...] = acc[n].astype(BF)
    yield 0
    for cp in [over_x] + list(over_y.values()) + list(far_y.values()) + landed:
        cp.wait_send()


def query_steps(links, keep_sem, q_ref, o_ref):
    z, xl, xh, y, c = coords()
    own = o_ref.at[z * 2 + xl]
    keep = pltpu.make_async_copy(q_ref, own, keep_sem)
    keep.start()
    side = place(z, 1 - xl, xh, y, c)
    over_x = [links.copy(q_ref, own, side)]
    over_z = {d: links.copy(q_ref, own, place(ring(z, d), xl, xh, y, c)) for d in (2, 1, 3)}
    yield 0
    over_x[0].wait_recv()
    far = o_ref.at[z * 2 + 1 - xl, pl.ds(0, 128)]
    more = [links.copy(far, far, place(ring(z, d), xl, xh, y, c)) for d in (2, 1, 3)]
    yield 0
    for d in (1, 3, 2):
        over_z[d].wait_recv()
        got = o_ref.at[ring(z, 4 - d) * 2 + xl, pl.ds(128, 128)]
        over_x.append(links.copy(got, got, side))
    yield 0
    for cp in over_x[1:] + more:
        cp.wait_recv()
    for cp in over_x + more + list(over_z.values()):
        cp.wait_send()
    keep.wait()


def gather_queries(q):
    def body(ins, outs, scr):
        send, recv, loc = scr
        yield from query_steps(Links(send, recv), loc.at[0], ins[0], outs[0])

    return Task(
        body, [(q, ANY)], [(jax.ShapeDtypeStruct((8, 256, 256), BF), ANY)], [], 10, 1, TOK_AG
    )


def exchange_tok(*arrays):
    def body(ins, outs, scr):
        send, recv, loc = scr
        z, xl, xh, y, c = coords()
        t = z * 2 + xl
        links = Links(send, recv)
        keep, cps = [], []
        for k, (src, dst) in enumerate(zip(ins, outs)):
            keep.append(pltpu.make_async_copy(src.at[t], dst.at[t], loc.at[k]))
            keep[-1].start()
        for dx, dz in REL8:
            z_, xl_ = ring(z, dz), lax.rem(xl + dx, 2)
            for src, dst in zip(ins, outs):
                cps.append(links.copy(src.at[z_ * 2 + xl_], dst.at[t], place(z_, xl_, xh, y, c)))
        yield 0
        for cp in cps:
            cp.wait()
        for cp in keep:
            cp.wait()

    n = len(arrays)
    return Task(
        body,
        [(a, ANY) for a in arrays],
        [(jax.ShapeDtypeStruct(a.shape, a.dtype), ANY) for a in arrays],
        [],
        7 * n,
        n,
        TOK_ALL,
    )


def embed_steps(links, sems, table_ref, slot_ref, old_ref, acc_ref, new_ref, scr):
    raw, table, stage, parts, came = scr
    vocab, wide = table_ref.shape
    piece = vocab // 4
    strip = piece // 7
    z, xl, xh, y, c = coords()
    t = z * 2 + xl
    loads = [
        pltpu.make_async_copy(table_ref.at[pl.ds(k * piece, piece)], raw.at[k], sems.at[k])
        for k in range(4)
    ]
    for cp in loads:
        cp.start()
    table[pl.ds(vocab, 8), :] = jnp.zeros((8, wide), F32)
    for k in range(4):
        loads[k].wait()

        def widen(j, carry, k=k):
            at = pl.multiple_of(j * strip, strip)
            to = pl.multiple_of(k * piece + j * strip, strip)
            table[pl.ds(to, strip), :] = raw[k, pl.ds(at, strip), :].astype(F32)
            return carry

        lax.fori_loop(0, 7, widen, 0)
    yield 0

    def look_up(owner):
        def rows(j, carry):
            for k in range(16):
                n = j * 16 + k
                stage[pl.ds(n, 1), :] = table[pl.ds(slot_ref[owner * 256 + n], 1), :]
            return carry

        lax.fori_loop(0, 16, rows, 0)
        parts[owner] = stage[...].astype(BF)

    cps, sources = [], []
    for dx, dz in REL8:
        z_, xl_ = ring(z, dz), lax.rem(xl + dx, 2)
        look_up(z_ * 2 + xl_)
        cps.append(links.copy(parts.at[z_ * 2 + xl_], came.at[t], place(z_, xl_, xh, y, c)))
        sources.append(z_ * 2 + xl_)
    look_up(t)
    yield 0
    total = parts[t].astype(F32)
    for cp in cps:
        cp.wait()
    for source in sources:
        total = total + came[source].astype(F32)
    new_ref[...] = jnp.where(acc_ref[...] == 1, total, old_ref[...].astype(F32)).astype(BF)


def front(block_states, weights, embed, slots, accept):
    rows, wide = block_states.shape
    vocab = embed.shape[0]

    def body(ins, outs, scr):
        x_ref, w_refs, table_ref, slot_ref, old_ref, acc_ref = (
            ins[0],
            ins[1:4],
            ins[4],
            ins[5],
            ins[6],
            ins[7],
        )
        rows1, q1, k1, v1, qs1, rows2, q2, k2, v2 = outs
        f1, f2, w_ref, acc, swapped = scr[:5]
        send, recv, loc = scr[10:]
        links = Links(send, recv)
        loads = [pltpu.make_async_copy(w_refs[n], w_ref.at[n], loc.at[n]) for n in range(3)]
        one = project_steps(
            links, loc.at[3], x_ref, f1, w_ref, acc, loads, rows1, (q1, k1, v1)
        )
        swap = embed_steps(
            links, loc.at[pl.ds(6, 4)], table_ref, slot_ref, old_ref, acc_ref, swapped, scr[5:10]
        )
        next(one)
        next(swap)
        for cp in loads:
            cp.start()
        next(one)
        next(swap)
        for _ in range(4):
            next(one)
        ask = query_steps(links, loc.at[4], q1, qs1)
        next(ask)
        next(swap, None)
        two = project_steps(links, loc.at[5], swapped, f2, w_ref, acc, [], rows2, (q2, k2, v2))
        next(two)
        next(ask)
        next(two)
        next(ask)
        for _ in range(4):
            next(two)
        for left in (one, ask, two):
            next(left, None)
        yield 0

    def out(*shape):
        return jax.ShapeDtypeStruct(shape, BF)

    half = [(out(16, 16 * wide), VM)] + [(out(rows, wide), VM)] * 3
    return Task(
        body,
        [(block_states, ANY)]
        + [(w, ANY) for w in weights]
        + [(embed, ANY), (slots, pl.BlockSpec(memory_space=pltpu.SMEM))]
        + [(block_states, VM), (accept, VM)],
        half + [(out(8, rows, wide), ANY)] + half,
        [
            pltpu.VMEM((16, rows, wide), BF),
            pltpu.VMEM((16, rows, wide), BF),
            pltpu.VMEM((3, 16 * wide, wide), BF),
            pltpu.VMEM((3, rows, wide), F32),
            pltpu.VMEM((rows, wide), BF),
            pltpu.VMEM((4, vocab // 4, wide), BF),
            pltpu.VMEM((vocab + 8, wide), F32),
            pltpu.VMEM((rows, wide), F32),
            pltpu.VMEM((8, rows, wide), BF),
            pltpu.VMEM((8, rows, wide), BF),
        ],
        15 + 7 + 10 + 15,
        10,
        HEAD_AG + TOK_ALL,
    )


def unit_rows(v):
    return v * lax.rsqrt(jnp.mean(v * v, axis=-1, keepdims=True) + EPSILON)


def layer_end(before, total, gain):
    return (before.astype(F32) + unit_rows(total) * gain).astype(BF)


def end_first(first, states_in, attn_gain, final_gain):
    chunks = 4

    def body(ins, outs, scr):
        x_ref, again_ref, fgain_ref = ins[6:]
        held = scr[:6]
        att, out, theirs, came, far, total, send, recv, loc = scr[6:]
        z, xl, xh, y, c = coords()
        links = Links(send, recv)
        cuts = [pl.ds(k * 1024, 1024) for k in range(chunks)]
        fetch = [
            pltpu.make_async_copy(src, dst, loc.at[k])
            for k, (src, dst) in enumerate(zip(ins[:6], held))
        ]
        for cp in fetch:
            cp.start()
        for cp in fetch:
            cp.wait()
        attend(*held[:5], att)
        core = place(z, xl, xh, y, 1 - c)
        swaps, over_y, over_x = [], [], []
        for cut in cuts:
            o = jnp.dot(att[...], held[5][:, cut], preferred_element_type=F32).astype(BF)
            out[:, :, :, :, cut] = o.reshape(2, 4, 2, 16, 1024)
            swaps.append(
                links.copy(out.at[:, :, 1 - c, :, cut], theirs.at[:, :, :, cut], core)
            )

        def both(xh_, y_, cut):
            return out[xh_, y_, c, :, cut].astype(F32) + theirs[xh_, y_, :, cut].astype(F32)

        for k, cut in enumerate(cuts):
            swaps[k].wait_recv()
            over_y.append([])
            for dy in (2, 1, 3):
                y_ = ring(y, dy)
                for xh_ in (0, 1):
                    theirs[xh_, y_, :, cut] = both(xh_, y_, cut).astype(BF)
                over_y[k].append(
                    links.copy(
                        theirs.at[:, y_, :, cut],
                        came.at[:, y, :, cut],
                        place(z, xl, xh, y_, c),
                    )
                )
        for k, cut in enumerate(cuts):
            for cp in over_y[k]:
                cp.wait_recv()
            away, mine = both(1 - xh, y, cut), both(xh, y, cut)
            for dy in (1, 3, 2):
                y_ = ring(y, dy)
                away = away + came[1 - xh, y_, :, cut].astype(F32)
                mine = mine + came[xh, y_, :, cut].astype(F32)
            theirs[1 - xh, y, :, cut] = away.astype(BF)
            over_x.append(
                links.copy(
                    theirs.at[1 - xh, y, :, cut], far.at[:, cut], place(z, xl, 1 - xh, y, c)
                )
            )
            total[:, cut] = mine
        for cp in over_x:
            cp.wait_recv()
        wide = layer_end(
            x_ref[...], total[...] + far[...].astype(F32), again_ref[...]
        ).astype(F32)
        squares = jnp.sum(wide * wide, axis=-1, keepdims=True)
        normed = wide * lax.rsqrt(squares * (1.0 / 4096) + EPSILON) * fgain_ref[...]
        outs[0][...] = normed.astype(BF)
        lane = lax.broadcasted_iota(jnp.int32, (8, 256), 1)
        row = lax.broadcasted_iota(jnp.int32, (8, 256), 0)
        outs[1][...] = jnp.where((lane == z * 2 + xl) & (row == 4), jnp.sum(squares), 0.0)
        for cp in swaps + [cp for k in over_y for cp in k] + over_x:
            cp.wait_send()
        yield 0

    block = pltpu.VMEM((2, 4, 16, 4096), BF)
    return Task(
        body,
        [(a, ANY) for a in first] + [(states_in, VM), (attn_gain, VM), (final_gain, VM)],
        [(jax.ShapeDtypeStruct((16, 4096), BF), VM), (jax.ShapeDtypeStruct((8, 256), F32), VM)],
        [pltpu.VMEM(a.shape, a.dtype) for a in first]
        + [
            pltpu.VMEM((256, 256), BF),
            pltpu.VMEM((2, 4, 2, 16, 4096), BF),
            block,
            block,
            pltpu.VMEM((16, 4096), BF),
            pltpu.VMEM((16, 4096), F32),
        ],
        5 * chunks,
        6,
        HEAD_AG,
    )


def along(axis, d):
    return shift(*{"x": (d, 0, 0, 0), "y": (0, d, 0, 0), "z": (0, 0, d, 0)}[axis])


CHUNKS = ((512, 512, 512), (512, 512, 512), (384, 384, 256))
STARTS = (0, 1536, 3072, 4096)
ORDERS = ("xyz", "yzx", "zxy")


def gather_logits(normed, squares, own_head, other_head, second, states_in, attn_gain):
    vocab = own_head.shape[0]
    n = len(CHUNKS)

    def body(ins, outs, scr):
        n_ref, sq_ref, x_ref, again_ref, own_ref, other_ref = ins[:6]
        top_ref, sum_ref, hid_ref = outs
        bufs = [scr[3 * i : 3 * i + 3] for i in range(n)]
        heads, acc = scr[9:11]
        held = scr[11:17]
        att, out, theirs, came, far, maxima, wide, deep, send, recv, loc = scr[17:]
        z, xl, xh, y, c = coords()
        x = xh * 2 + xl
        links = Links(send, recv)
        full = slice(None)
        loads = [
            pltpu.make_async_copy(src, heads.at[k], loc.at[k])
            for k, src in enumerate((own_ref, other_ref))
        ]

        def block(i, p, known, step=0, half=None):
            last = ORDERS[p][2]
            z_, y_, x_ = z, y, x
            if step:
                if last == "z":
                    z_ = ring(z, step)
                elif last == "y":
                    y_ = ring(y, step)
                else:
                    x_ = ring(x, step)
            at = [
                full if "z" in known else z_,
                full if "x" in known else lax.rem(x_, 2),
                full if "x" in known else x_ // 2,
                full if "y" in known else y_,
            ]
            if half is not None:
                if last == "z":
                    at[1] = half
                else:
                    at[0] = pl.ds(2 * half, 2)
            return bufs[i][p].at[tuple(at)]

        start = 0
        for i in range(n):
            for p in range(3):
                bufs[i][p][z, xl, xh, y] = n_ref[:, start : start + CHUNKS[i][p]]
                start += CHUNKS[i][p]

        everything = []

        def push(i, p, ref, axis, d):
            cp = links.copy(ref, ref, along(axis, d))
            everything.append(cp)
            return cp

        def spread(i, stage, before):
            out = []
            for p in range(3):
                if before is not None:
                    for cp in before[p]:
                        cp.wait_recv()
                ref = block(i, p, ORDERS[p][:stage])
                ds = (2, 1, 3) if stage < 2 else (1, 3)
                out.append([push(i, p, ref, ORDERS[p][stage], d) for d in ds])
            return out

        def relay(i, before):
            out = []
            for p in range(3):
                axis, known = ORDERS[p][2], ORDERS[p][:2]
                before[p][0].wait_recv()
                lower = push(i, p, block(i, p, known, 3, 0), axis, 1)
                before[p][1].wait_recv()
                upper = push(i, p, block(i, p, known, 1, 1), axis, 3)
                out.append([lower, upper])
            return out

        def multiply(i):
            cut = pl.ds(STARTS[i], STARTS[i + 1] - STARTS[i])

            def step(r, carry):
                rows = jnp.concatenate(
                    [bufs[i][p][r].reshape(256, CHUNKS[i][p]) for p in range(3)], axis=1
                )
                top = None
                for k in range(2):
                    part = lax.dot_general(
                        heads[k, :, cut], rows, (((1,), (1,)), ((), ())), preferred_element_type=F32
                    )
                    if i > 0:
                        part = acc[k, r] + part
                    if i < n - 1:
                        acc[k, r] = part
                    else:
                        m = jnp.max(part, axis=0, keepdims=True)
                        top = m if top is None else jnp.maximum(top, m)
                if i == n - 1:
                    maxima[0, pl.ds(r, 1), :] = top
                return carry

            lax.fori_loop(0, 4, step, 0)

        fetch = [
            pltpu.make_async_copy(src, dst, loc.at[2 + k])
            for k, (src, dst) in enumerate(zip(ins[6:], held))
        ]
        one = [spread(i, 0, None) for i in range(n)]
        for cp in fetch + loads:
            cp.start()
        two = [spread(i, 1, one[i]) for i in range(n)]
        three = {0: spread(0, 2, two[0]), 1: spread(1, 2, two[1])}
        for cp in fetch:
            cp.wait()
        attend(*held[:5], att)

        def times_out(k, carry):
            cut = pl.ds(pl.multiple_of(k * 1024, 1024), 1024)
            o = jnp.dot(att[...], held[5][:, cut], preferred_element_type=F32).astype(BF)
            out[:, :, :, :, cut] = o.reshape(2, 4, 2, 16, 1024)
            return carry

        lax.fori_loop(0, 4, times_out, 0)
        swap = links.copy(out.at[:, :, 1 - c], theirs, shift(0, 0, 0, 1))
        over_y = []
        four = {0: relay(0, three[0])}
        for i in range(n):
            if i + 1 < n:
                four[i + 1] = relay(i + 1, three[i + 1])
            if i + 2 < n:
                three[i + 2] = spread(i + 2, 2, two[i + 2])
            if i == n - 2:
                swap.wait()
                for dy in (2, 1, 3, 0):
                    y_ = ring(y, dy)
                    for xh_ in (0, 1):
                        v = out[xh_, y_, c].astype(F32) + theirs[xh_, y_].astype(F32)
                        theirs[xh_, y_] = v.astype(BF)
                    if dy:
                        over_y.append(
                            links.copy(
                                theirs.at[:, y_], came.at[:, y], place(z, xl, xh, y_, c)
                            )
                        )
            for pair in four[i]:
                for cp in pair:
                    cp.wait_recv()
            if i == 0:
                for cp in loads:
                    cp.wait()
            if i == n - 1:
                maxima[0] = sq_ref[...]
            multiply(i)
        top = lax.broadcasted_iota(jnp.int32, (8, 256), 0) < 4

        def join(v, w):
            return jnp.where(top, jnp.maximum(v, w), v + w)

        flat = [links.copy(maxima.at[0], wide.at[k], shift(*key)) for k, key in enumerate(PLANE)]
        for cp in flat:
            cp.wait()
        mine = maxima[0]
        for k in range(15):
            mine = join(mine, wide[k])
        maxima[1] = mine
        tall = [links.copy(maxima.at[1], deep.at[k], shift(*key)) for k, key in enumerate(DEEP)]
        for cp in over_y:
            cp.wait_recv()
        for xh_ in (0, 1):
            v = theirs[xh_, y].astype(F32)
            for dy in (1, 3, 2):
                v = v + came[xh_, ring(y, dy)].astype(F32)
            theirs[xh_, y] = v.astype(BF)
        over_x = links.copy(theirs.at[1 - xh, y], far, place(z, xl, 1 - xh, y, c))
        for cp in tall:
            cp.wait()
        for k in range(3):
            mine = join(mine, deep[k])
        other = deep[3]
        for k in range(4, 7):
            other = join(other, deep[k])
        even = jnp.where(c == 0, mine, other)
        odd = jnp.where(c == 0, other, mine)
        group = lax.broadcasted_iota(jnp.int32, (8, 128), 1) // 16
        for q in range(4):
            row = jnp.zeros((8, 128), F32)
            for a in range(4):
                for k, v in enumerate((even, odd)):
                    half = v[:, q // 2 * 128 : q // 2 * 128 + 128]
                    turn = (a * 16 + k * 16 - q % 2 * 64) % 128
                    turned = pltpu.roll(half, turn, 1) if turn else half
                    row = jnp.where(group == 2 * a + k, turned, row)
            top_ref[:, q * 128 : q * 128 + 128] = row[:4]
        sum_ref[...] = jnp.sqrt((mine + other) * (1.0 / (256 * 4096)))
        over_x.wait_recv()
        total = theirs[xh, y].astype(F32) + far[...].astype(F32)
        hid_ref[...] = layer_end(x_ref[...], total, again_ref[...])
        everything += over_y + [over_x]
        for cp in everything:
            cp.wait_send()
        yield 0

    scratch = [pltpu.VMEM((4, 2, 2, 4, 16, w), BF) for ws in CHUNKS for w in ws]
    scratch += [pltpu.VMEM((2, vocab, 4096), BF), pltpu.VMEM((2, 4, vocab, 256), F32)]
    scratch += [pltpu.VMEM(a.shape, a.dtype) for a in second]
    scratch += [
        pltpu.VMEM((256, 256), BF),
        pltpu.VMEM((2, 4, 2, 16, 4096), BF),
        pltpu.VMEM((2, 4, 16, 4096), BF),
        pltpu.VMEM((2, 4, 16, 4096), BF),
        pltpu.VMEM((16, 4096), BF),
        pltpu.VMEM((2, 8, 256), F32),
        pltpu.VMEM((15, 8, 256), F32),
        pltpu.VMEM((7, 8, 256), F32),
    ]
    return Task(
        body,
        [(normed, VM), (squares, VM), (states_in, VM), (attn_gain, VM)]
        + [(a, ANY) for a in (own_head, other_head) + second],
        [
            (jax.ShapeDtypeStruct((4, 512), F32), VM),
            (jax.ShapeDtypeStruct((8, 256), F32), VM),
            (jax.ShapeDtypeStruct((16, 4096), BF), VM),
        ],
        scratch,
        3 * 3 * 10 + 5 + 22,
        8,
        AXES + PLANE + DEEP,
    )


def scores(q, k):
    return lax.dot_general(q, k, (((1,), (1,)), ((), ())), preferred_element_type=F32) * SCALE2


def cached_attention(begins, ends, queries, keys, values):
    rows = queries.shape[1]
    cuts = [slice(g * HEAD_DIM, (g + 1) * HEAD_DIM) for g in (0, 1)]

    def kernel(lo_ref, hi_ref, q_ref, k_ref, v_ref, o_ref, s_ref, v_sc, m_sc, a_sc):
        for g in range(2):
            v_sc[g, :, :HEAD_DIM] = v_ref[:, g * HEAD_DIM : (g + 1) * HEAD_DIM]
            v_sc[g, :, HEAD_DIM:] = jnp.ones((v_ref.shape[0], HEAD_DIM), BF)
        lane = lax.broadcasted_iota(jnp.int32, (rows, 128), 1)
        sub = lax.broadcasted_iota(jnp.int32, (8, rows), 0)

        def request(r, carry):
            lo, hi = lo_ref[r], hi_ref[r]

            @pl.when(hi <= lo)
            def _():
                o_ref[r] = jnp.zeros(o_ref.shape[1:], BF)
                s_ref[r] = jnp.where(sub < 2, NEG, 0.0)

            @pl.when(hi > lo)
            def _():
                m_sc[...] = jnp.full_like(m_sc, NEG)
                a_sc[...] = jnp.zeros_like(a_sc)

                def step(b, span):
                    at = pl.multiple_of(b * span, span)
                    pos = at + lax.broadcasted_iota(jnp.int32, (1, span), 1)
                    bias = jnp.where((pos >= lo) & (pos < hi), 0.0, NEG)
                    ss = [scores(q_ref[r, :, cut], k_ref[pl.ds(at, span), cut]) for cut in cuts]
                    ss = [s + bias for s in ss]
                    old = [m_sc[g] for g in (0, 1)]
                    new = [
                        jnp.maximum(o, jnp.max(s, axis=-1, keepdims=True)) for o, s in zip(old, ss)
                    ]
                    ps = [jnp.exp2(s - m[:, 0:1]).astype(BF) for s, m in zip(ss, new)]
                    fs = [jnp.exp2(o - m) for o, m in zip(old, new)]
                    ds = [
                        jnp.dot(p, v_sc[g, pl.ds(at, span), :], preferred_element_type=F32)
                        for g, p in enumerate(ps)
                    ]
                    for g in (0, 1):
                        a_sc[g] = a_sc[g] * jnp.concatenate([fs[g], fs[g]], axis=1) + ds[g]
                        m_sc[g] = new[g]

                small = lo // 256 == (hi - 1) // 256

                @pl.when(small)
                def _():
                    step(lo // 256, 256)

                @pl.when(jnp.logical_not(small))
                def _():
                    def wide_step(b, carry):
                        step(b, 512)
                        return carry

                    lax.fori_loop(lo // 512, (hi + 511) // 512, wide_step, 0)

                stats = jnp.where(lane == 0, m_sc[0], m_sc[1])
                stats = jnp.where(lane == 2, a_sc[0, :, HEAD_DIM:], stats)
                stats = jnp.where(lane == 3, a_sc[1, :, HEAD_DIM:], stats)
                s_ref[r] = jnp.transpose(stats)[:8]
                for g in range(2):
                    o_ref[r, :, g * HEAD_DIM : (g + 1) * HEAD_DIM] = a_sc[g, :, :HEAD_DIM].astype(BF)

            return carry

        lax.fori_loop(0, 8, request, 0)

    smem = pl.BlockSpec(memory_space=pltpu.SMEM)
    return pl.pallas_call(
        kernel,
        in_specs=[smem, smem, VM, VM, VM],
        out_specs=[VM, VM],
        scratch_shapes=[
            pltpu.VMEM((2, values.shape[0], 256), BF),
            pltpu.VMEM((2, rows, 128), F32),
            pltpu.VMEM((2, rows, 256), F32),
        ],
        out_shape=[
            jax.ShapeDtypeStruct((8, rows, 256), BF),
            jax.ShapeDtypeStruct((8, 8, rows), F32),
        ],
        compiler_params=pltpu.CompilerParams(vmem_limit_bytes=16 << 20),
        name="cached",
    )(begins, ends, queries, keys, values)


def attend(p_ref, s_ref, q_ref, k_ref, v_ref, att):
    st = jnp.concatenate([s_ref[...].reshape(64, 256), jnp.zeros((64, 256), F32)], axis=0)
    st = jnp.transpose(st)
    for g in range(2):
        cut = slice(g * HEAD_DIM, (g + 1) * HEAD_DIM)
        s = scores(q_ref[:, cut], k_ref[:, cut])
        top = jnp.max(s, axis=-1, keepdims=True)
        for i in range(8):
            top = jnp.maximum(top, st[:, i * 8 + g : i * 8 + g + 1])
        p = jnp.exp2(s - top)
        mass = jnp.sum(p, axis=-1, keepdims=True)
        acc = jnp.dot(p.astype(BF), v_ref[:, cut], preferred_element_type=F32)
        for i in range(8):
            f = jnp.exp2(st[:, i * 8 + g : i * 8 + g + 1] - top)
            mass = mass + f * st[:, i * 8 + g + 2 : i * 8 + g + 3]
            acc = acc + f * p_ref[i, :, cut].astype(F32)
        att[:, cut] = (acc / mass).astype(BF)


def shards(
    block_states,
    token_ids,
    accept,
    cache_lengths,
    cache_keys,
    cache_values,
    w_query,
    w_key,
    w_value,
    w_out,
    attn_gain,
    final_gain,
    embed,
    lm_head,
):
    tok = lax.axis_index("tok")
    other_head = lax.ppermute(lm_head, "head", [(i, i ^ 1) for i in range(16)])
    cache_here = cache_keys.shape[0]
    offsets = jnp.cumsum(cache_lengths) - cache_lengths - tok * cache_here
    begins = jnp.clip(offsets, 0, cache_here)
    ends = jnp.clip(offsets + cache_lengths, 0, cache_here)
    attn_gain = attn_gain.reshape(1, -1)
    final_gain = final_gain.reshape(1, -1)

    vocab_here = embed.shape[0]
    local_ids = token_ids - tok * vocab_here
    inside = (local_ids >= 0) & (local_ids < vocab_here)
    slots = jnp.where(inside, local_ids, vocab_here)

    weights = (w_query, w_key, w_value)
    ((rows1, q1, k1, v1, qs1, rows2, q2, k2, v2),) = comm(
        [front(block_states, weights, embed, slots, accept.reshape(-1, 1))], 0, "comm_a", 60
    )
    part1, stat1 = cached_attention(begins, ends, qs1, cache_keys, cache_values)

    (qs2,), (part1, stat1) = comm(
        [gather_queries(q2), exchange_tok(part1, stat1)], 2, "comm_c"
    )
    part2, stat2 = cached_attention(begins, ends, qs2, cache_keys, cache_values)

    first = (part1, stat1, q1, k1, v1, w_out)
    (part2, stat2), (normed, squares) = comm(
        [exchange_tok(part2, stat2), end_first(first, rows1, attn_gain, final_gain)],
        3,
        "comm_d",
        16,
    )
    second = (part2, stat2, q2, k2, v2, w_out)
    ((top, sums, hiddens),) = comm(
        [gather_logits(normed, squares, lm_head, other_head, second, rows2, attn_gain)],
        4,
        "comm_e",
        52,
    )
    return (hiddens, sums[4, :8], top.reshape(-1))


def solution(mesh):
    placed = (
        P("tok", "head"),
        P(),
        P("tok"),
        P(),
        P("tok", "head"),
        P("tok", "head"),
        P(None, "head"),
        P(None, "head"),
        P(None, "head"),
        P("head", None),
        P(),
        P(),
        P("tok", "head"),
        P(("tok", "head"), None),
    )
    return jax.shard_map(
        shards,
        mesh=mesh,
        in_specs=placed,
        out_specs=(P(("tok", "head"), None), P(), P()),
        check_vma=False,
    )
```

```python
import math

import jax
import jax.numpy as jnp
from jax import lax
from jax.experimental import pallas as pl
from jax.experimental.pallas import tpu as pltpu
from jax.sharding import PartitionSpec as P

HEAD_DIM = 128
EPSILON = 1e-06
NEG = -1e30
SCALE2 = (1.0 / math.sqrt(HEAD_DIM)) * math.log2(math.e)
MESH = pl.DeviceIdType.MESH
BF = jnp.bfloat16
F32 = jnp.float32
ANY = pl.BlockSpec(memory_space=pltpu.HBM)
VM = pl.BlockSpec(memory_space=pltpu.VMEM)
REL8 = ((0, 2), (1, 2), (1, 1), (1, 3), (0, 1), (0, 3), (1, 0))


def coords():
    t = lax.axis_index("tok")
    h = lax.axis_index("head")
    return t // 2, lax.rem(t, 2), h // 8, lax.rem(h // 2, 4), lax.rem(h, 2)


def place(z, xl, xh, y, c):
    return (z * 2 + xl, xh * 8 + y * 2 + c)


def ring(v, d):
    return lax.rem(v + d, 4)


class Links:
    def __init__(self, send, recv):
        self.send, self.recv, self.used = send, recv, 0

    def copy(self, src, dst, device):
        k = self.used
        self.used += 1
        cp = pltpu.make_async_remote_copy(
            src_ref=src,
            dst_ref=dst,
            send_sem=self.send.at[k],
            recv_sem=self.recv.at[k],
            device_id=device,
            device_id_type=MESH,
        )
        cp.start()
        return cp


class Task:
    def __init__(self, body, ins, outs, scratch, copies, local, peers):
        self.body, self.ins, self.outs = body, ins, outs
        self.scratch = list(scratch) + [
            pltpu.SemaphoreType.DMA((copies,)),
            pltpu.SemaphoreType.DMA((copies,)),
            pltpu.SemaphoreType.DMA((max(local, 1),)),
        ]
        self.peers = peers


def shift(dx, dy, dz, dc):
    z, xl, xh, y, c = coords()
    c_ = lax.rem(c + dc, 2)
    if dx == "s":
        return place(ring(z, dz), 1 - xl, xh, ring(y, dy), c_)
    x_ = ring(xh * 2 + xl, dx)
    return place(ring(z, dz), lax.rem(x_, 2), x_ // 2, ring(y, dy), c_)


HEAD_AG = [(0, 0, 0, 1), (2, 0, 0, 0), (0, 1, 0, 0), (0, 2, 0, 0), (0, 3, 0, 0)]
HEAD_ALL = [(0, 0, 0, 1)] + [(2 * dx, dy, 0, 0) for dx, dy in REL8]
TOK_AG = [("s", 0, 0, 0), (0, 0, 1, 0), (0, 0, 2, 0), (0, 0, 3, 0)]
TOK_ALL = [("s" if dx else 0, 0, dz, 0) for dx, dz in REL8]
AXES = [(d, 0, 0, 0) for d in (1, 2, 3)] + [(0, d, 0, 0) for d in (1, 2, 3)]
AXES += [(0, 0, d, 0) for d in (1, 2, 3)]
PLANE = [(k // 4, k % 4, 0, 0) for k in range(1, 16)]
DEEP = [(0, 0, k % 4, k // 4) for k in range(1, 8)]


def comm(tasks, cid, name, vmem=4):
    n_in = [len(t.ins) for t in tasks]
    n_out = [len(t.outs) for t in tasks]
    n_scr = [len(t.scratch) for t in tasks]

    def kernel(*refs):
        ins, rest = refs[: sum(n_in)], refs[sum(n_in) :]
        outs, scr = rest[: sum(n_out)], rest[sum(n_out) :]
        peers = {}
        for t in tasks:
            for key in t.peers:
                peers.setdefault(key, shift(*key))
        barrier = pltpu.get_barrier_semaphore()
        for device in peers.values():
            pl.semaphore_signal(barrier, inc=1, device_id=device, device_id_type=MESH)
        pl.semaphore_wait(barrier, len(peers))
        running, a, b, c = [], 0, 0, 0
        for k, t in enumerate(tasks):
            running.append(
                t.body(
                    ins[a : a + n_in[k]], outs[b : b + n_out[k]], scr[c : c + n_scr[k]]
                )
            )
            a, b, c = a + n_in[k], b + n_out[k], c + n_scr[k]
        while running:
            again = []
            for g in running:
                if next(g, StopIteration) is not StopIteration:
                    again.append(g)
            running = again

    flat = pl.pallas_call(
        kernel,
        out_shape=[o[0] for t in tasks for o in t.outs],
        in_specs=[i[1] for t in tasks for i in t.ins],
        out_specs=[o[1] for t in tasks for o in t.outs],
        scratch_shapes=[s for t in tasks for s in t.scratch],
        compiler_params=pltpu.CompilerParams(
            collective_id=cid, has_side_effects=True, vmem_limit_bytes=vmem << 20
        ),
        name=name,
    )(*[i[0] for t in tasks for i in t.ins])
    res, b = [], 0
    for n in n_out:
        res.append(flat[b : b + n])
        b += n
    return res


def project_steps(links, keep_sem, x_ref, f_ref, w_ref, acc, loads, own_rows, outs):
    wide = x_ref.shape[1]
    z, xl, xh, y, c = coords()

    def index(xh_, y_, c_):
        return xh_ * 8 + y_ * 2 + c_

    def slot(*at):
        return f_ref.at[index(*at)]

    def absorb(*at):
        k = index(*at)
        v = f_ref[k]
        for n in range(3):
            w = w_ref[n, pl.ds(pl.multiple_of(k * wide, wide), wide), :]
            acc[n] += jnp.dot(v, w, preferred_element_type=F32)

    core = place(z, xl, xh, y, 1 - c)
    own = slot(xh, y, c)
    keep = pltpu.make_async_copy(x_ref, own, keep_sem)
    keep.start()
    landed = []
    over_x = links.copy(x_ref, own, place(z, xl, 1 - xh, y, c))
    over_y = {d: links.copy(x_ref, own, place(z, xl, xh, ring(y, d), c)) for d in (2, 1, 3)}
    landed.append(links.copy(x_ref, own, core))
    acc[...] = jnp.zeros_like(acc)
    yield 0
    over_x.wait_recv()
    far = slot(1 - xh, y, c)
    far_y = {d: links.copy(far, far, place(z, xl, xh, ring(y, d), c)) for d in (2, 1, 3)}
    landed.append(links.copy(far, far, core))
    yield 0
    keep.wait()
    for cp in loads:
        cp.wait()
    absorb(xh, y, c)
    absorb(1 - xh, y, c)
    for k, xh_ in enumerate((xh, 1 - xh)):
        landed[k].wait_recv()
        absorb(xh_, y, 1 - c)
    yield 0
    for xh_, arrive in ((xh, over_y), (1 - xh, far_y)):
        for d in (1, 3, 2):
            y_ = ring(y, 4 - d)
            arrive[d].wait_recv()
            got = slot(xh_, y_, c)
            landed.append(links.copy(got, got, core))
            absorb(xh_, y_, c)
        for k, d in enumerate((1, 3, 2)):
            landed[k - 3].wait_recv()
            absorb(xh_, ring(y, 4 - d), 1 - c)
        yield 0
    h = pl.multiple_of(index(xh, y, c) * 16, 16)
    for k in range(16):
        own_rows[:, k * wide : (k + 1) * wide] = f_ref[k, pl.ds(h, 16), :]
    for n in range(3):
        outs[n][...] = acc[n].astype(BF)
    yield 0
    for cp in [over_x] + list(over_y.values()) + list(far_y.values()) + landed:
        cp.wait_send()


def query_steps(links, keep_sem, q_ref, o_ref):
    z, xl, xh, y, c = coords()
    own = o_ref.at[z * 2 + xl]
    keep = pltpu.make_async_copy(q_ref, own, keep_sem)
    keep.start()
    side = place(z, 1 - xl, xh, y, c)
    over_x = [links.copy(q_ref, own, side)]
    over_z = {d: links.copy(q_ref, own, place(ring(z, d), xl, xh, y, c)) for d in (2, 1, 3)}
    yield 0
    over_x[0].wait_recv()
    far = o_ref.at[z * 2 + 1 - xl, pl.ds(0, 128)]
    more = [links.copy(far, far, place(ring(z, d), xl, xh, y, c)) for d in (2, 1, 3)]
    yield 0
    for d in (1, 3, 2):
        over_z[d].wait_recv()
        got = o_ref.at[ring(z, 4 - d) * 2 + xl, pl.ds(128, 128)]
        over_x.append(links.copy(got, got, side))
    yield 0
    for cp in over_x[1:] + more:
        cp.wait_recv()
    for cp in over_x + more + list(over_z.values()):
        cp.wait_send()
    keep.wait()


def gather_queries(q):
    def body(ins, outs, scr):
        send, recv, loc = scr
        yield from query_steps(Links(send, recv), loc.at[0], ins[0], outs[0])

    return Task(
        body, [(q, ANY)], [(jax.ShapeDtypeStruct((8, 256, 256), BF), ANY)], [], 10, 1, TOK_AG
    )


def exchange_tok(*arrays):
    def body(ins, outs, scr):
        send, recv, loc = scr
        z, xl, xh, y, c = coords()
        t = z * 2 + xl
        links = Links(send, recv)
        keep, cps = [], []
        for k, (src, dst) in enumerate(zip(ins, outs)):
            keep.append(pltpu.make_async_copy(src.at[t], dst.at[t], loc.at[k]))
            keep[-1].start()
        for dx, dz in REL8:
            z_, xl_ = ring(z, dz), lax.rem(xl + dx, 2)
            for src, dst in zip(ins, outs):
                cps.append(links.copy(src.at[z_ * 2 + xl_], dst.at[t], place(z_, xl_, xh, y, c)))
        yield 0
        for cp in cps:
            cp.wait()
        for cp in keep:
            cp.wait()

    n = len(arrays)
    return Task(
        body,
        [(a, ANY) for a in arrays],
        [(jax.ShapeDtypeStruct(a.shape, a.dtype), ANY) for a in arrays],
        [],
        7 * n,
        n,
        TOK_ALL,
    )


def embed_steps(links, sems, table_ref, slot_ref, old_ref, acc_ref, new_ref, scr):
    raw, table, stage, parts, came = scr
    vocab, wide = table_ref.shape
    piece = vocab // 4
    strip = piece // 7
    z, xl, xh, y, c = coords()
    t = z * 2 + xl
    loads = [
        pltpu.make_async_copy(table_ref.at[pl.ds(k * piece, piece)], raw.at[k], sems.at[k])
        for k in range(4)
    ]
    for cp in loads:
        cp.start()
    table[pl.ds(vocab, 8), :] = jnp.zeros((8, wide), F32)
    for k in range(4):
        loads[k].wait()

        def widen(j, carry, k=k):
            at = pl.multiple_of(j * strip, strip)
            to = pl.multiple_of(k * piece + j * strip, strip)
            table[pl.ds(to, strip), :] = raw[k, pl.ds(at, strip), :].astype(F32)
            return carry

        lax.fori_loop(0, 7, widen, 0)
    yield 0

    def look_up(owner):
        def rows(j, carry):
            for k in range(16):
                n = j * 16 + k
                stage[pl.ds(n, 1), :] = table[pl.ds(slot_ref[owner * 256 + n], 1), :]
            return carry

        lax.fori_loop(0, 16, rows, 0)
        parts[owner] = stage[...].astype(BF)

    cps, sources = [], []
    for dx, dz in REL8:
        z_, xl_ = ring(z, dz), lax.rem(xl + dx, 2)
        look_up(z_ * 2 + xl_)
        cps.append(links.copy(parts.at[z_ * 2 + xl_], came.at[t], place(z_, xl_, xh, y, c)))
        sources.append(z_ * 2 + xl_)
    look_up(t)
    yield 0
    total = parts[t].astype(F32)
    for cp in cps:
        cp.wait()
    for source in sources:
        total = total + came[source].astype(F32)
    taken = jnp.transpose(jnp.broadcast_to(acc_ref[...].astype(F32), (256, 256)))
    new_ref[...] = jnp.where(taken == 1.0, total, old_ref[...].astype(F32)).astype(BF)


def front(block_states, weights, embed, slots, accept):
    rows, wide = block_states.shape
    vocab = embed.shape[0]

    def body(ins, outs, scr):
        x_ref, w_refs, table_ref, slot_ref, old_ref, acc_ref = (
            ins[0],
            ins[1:4],
            ins[4],
            ins[5],
            ins[6],
            ins[7],
        )
        rows1, q1, k1, v1, qs1, rows2, q2, k2, v2 = outs
        f1, f2, w_ref, acc, swapped = scr[:5]
        send, recv, loc = scr[10:]
        links = Links(send, recv)
        loads = [pltpu.make_async_copy(w_refs[n], w_ref.at[n], loc.at[n]) for n in range(3)]
        one = project_steps(
            links, loc.at[3], x_ref, f1, w_ref, acc, loads, rows1, (q1, k1, v1)
        )
        swap = embed_steps(
            links, loc.at[pl.ds(6, 4)], table_ref, slot_ref, old_ref, acc_ref, swapped, scr[5:10]
        )
        next(one)
        next(swap)
        for cp in loads:
            cp.start()
        next(one)
        next(swap)
        for _ in range(4):
            next(one)
        ask = query_steps(links, loc.at[4], q1, qs1)
        next(ask)
        next(swap, None)
        two = project_steps(links, loc.at[5], swapped, f2, w_ref, acc, [], rows2, (q2, k2, v2))
        next(two)
        next(ask)
        next(two)
        next(ask)
        for _ in range(4):
            next(two)
        for left in (one, ask, two):
            next(left, None)
        yield 0

    def out(*shape):
        return jax.ShapeDtypeStruct(shape, BF)

    half = [(out(16, 16 * wide), VM)] + [(out(rows, wide), VM)] * 3
    return Task(
        body,
        [(block_states, ANY)]
        + [(w, ANY) for w in weights]
        + [(embed, ANY), (slots, pl.BlockSpec(memory_space=pltpu.SMEM))]
        + [(block_states, VM), (accept, VM)],
        half + [(out(8, rows, wide), ANY)] + half,
        [
            pltpu.VMEM((16, rows, wide), BF),
            pltpu.VMEM((16, rows, wide), BF),
            pltpu.VMEM((3, 16 * wide, wide), BF),
            pltpu.VMEM((3, rows, wide), F32),
            pltpu.VMEM((rows, wide), BF),
            pltpu.VMEM((4, vocab // 4, wide), BF),
            pltpu.VMEM((vocab + 8, wide), F32),
            pltpu.VMEM((rows, wide), F32),
            pltpu.VMEM((8, rows, wide), BF),
            pltpu.VMEM((8, rows, wide), BF),
        ],
        15 + 7 + 10 + 15,
        10,
        HEAD_AG + TOK_ALL,
    )


def unit_rows(v):
    return v * lax.rsqrt(jnp.mean(v * v, axis=-1, keepdims=True) + EPSILON)


def layer_end(before, total, gain):
    return (before.astype(F32) + unit_rows(total) * gain).astype(BF)


def end_first(first, states_in, attn_gain, final_gain):
    chunks = 4

    def body(ins, outs, scr):
        x_ref, again_ref, fgain_ref = ins[6:]
        held = scr[:6]
        att, out, theirs, came, far, total, send, recv, loc = scr[6:]
        z, xl, xh, y, c = coords()
        links = Links(send, recv)
        cuts = [pl.ds(k * 1024, 1024) for k in range(chunks)]
        fetch = [
            pltpu.make_async_copy(src, dst, loc.at[k])
            for k, (src, dst) in enumerate(zip(ins[:6], held))
        ]
        for cp in fetch:
            cp.start()
        for cp in fetch:
            cp.wait()
        attend(*held[:5], att)
        core = place(z, xl, xh, y, 1 - c)
        swaps, over_y, over_x = [], [], []
        for cut in cuts:
            o = jnp.dot(att[...], held[5][:, cut], preferred_element_type=F32).astype(BF)
            out[:, :, :, :, cut] = o.reshape(2, 4, 2, 16, 1024)
            swaps.append(
                links.copy(out.at[:, :, 1 - c, :, cut], theirs.at[:, :, :, cut], core)
            )

        def both(xh_, y_, cut):
            return out[xh_, y_, c, :, cut].astype(F32) + theirs[xh_, y_, :, cut].astype(F32)

        for k, cut in enumerate(cuts):
            swaps[k].wait_recv()
            over_y.append([])
            for dy in (2, 1, 3):
                y_ = ring(y, dy)
                for xh_ in (0, 1):
                    theirs[xh_, y_, :, cut] = both(xh_, y_, cut).astype(BF)
                over_y[k].append(
                    links.copy(
                        theirs.at[:, y_, :, cut],
                        came.at[:, y, :, cut],
                        place(z, xl, xh, y_, c),
                    )
                )
        for k, cut in enumerate(cuts):
            for cp in over_y[k]:
                cp.wait_recv()
            away, mine = both(1 - xh, y, cut), both(xh, y, cut)
            for dy in (1, 3, 2):
                y_ = ring(y, dy)
                away = away + came[1 - xh, y_, :, cut].astype(F32)
                mine = mine + came[xh, y_, :, cut].astype(F32)
            theirs[1 - xh, y, :, cut] = away.astype(BF)
            over_x.append(
                links.copy(
                    theirs.at[1 - xh, y, :, cut], far.at[:, cut], place(z, xl, 1 - xh, y, c)
                )
            )
            total[:, cut] = mine
        for cp in over_x:
            cp.wait_recv()
        wide = layer_end(
            x_ref[...], total[...] + far[...].astype(F32), again_ref[...]
        ).astype(F32)
        squares = jnp.sum(wide * wide, axis=-1, keepdims=True)
        normed = wide * lax.rsqrt(squares * (1.0 / 4096) + EPSILON) * fgain_ref[...]
        outs[0][...] = normed.astype(BF)
        lane = lax.broadcasted_iota(jnp.int32, (8, 256), 1)
        row = lax.broadcasted_iota(jnp.int32, (8, 256), 0)
        outs[1][...] = jnp.where((lane == z * 2 + xl) & (row == 4), jnp.sum(squares), 0.0)
        for cp in swaps + [cp for k in over_y for cp in k] + over_x:
            cp.wait_send()
        yield 0

    block = pltpu.VMEM((2, 4, 16, 4096), BF)
    return Task(
        body,
        [(a, ANY) for a in first] + [(states_in, VM), (attn_gain, VM), (final_gain, VM)],
        [(jax.ShapeDtypeStruct((16, 4096), BF), VM), (jax.ShapeDtypeStruct((8, 256), F32), VM)],
        [pltpu.VMEM(a.shape, a.dtype) for a in first]
        + [
            pltpu.VMEM((256, 256), BF),
            pltpu.VMEM((2, 4, 2, 16, 4096), BF),
            block,
            block,
            pltpu.VMEM((16, 4096), BF),
            pltpu.VMEM((16, 4096), F32),
        ],
        5 * chunks,
        6,
        HEAD_AG,
    )


def along(axis, d):
    return shift(*{"x": (d, 0, 0, 0), "y": (0, d, 0, 0), "z": (0, 0, d, 0)}[axis])


CHUNKS = ((512, 512, 512), (512, 512, 512), (384, 384, 256))
STARTS = (0, 1536, 3072, 4096)
ORDERS = ("xyz", "yzx", "zxy")


def gather_logits(normed, squares, own_head, other_head, second, states_in, attn_gain):
    vocab = own_head.shape[0]
    n = len(CHUNKS)

    def body(ins, outs, scr):
        n_ref, sq_ref, x_ref, again_ref, own_ref, other_ref = ins[:6]
        top_ref, sum_ref, hid_ref = outs
        bufs = [scr[3 * i : 3 * i + 3] for i in range(n)]
        heads, acc = scr[9:11]
        held = scr[11:17]
        att, out, theirs, came, far, maxima, wide, deep, send, recv, loc = scr[17:]
        z, xl, xh, y, c = coords()
        x = xh * 2 + xl
        links = Links(send, recv)
        full = slice(None)
        loads = [
            pltpu.make_async_copy(src, heads.at[k], loc.at[k])
            for k, src in enumerate((own_ref, other_ref))
        ]

        for cp in loads:
            cp.start()
        yield 0

        def block(i, p, known, step=0, half=None):
            last = ORDERS[p][2]
            z_, y_, x_ = z, y, x
            if step:
                if last == "z":
                    z_ = ring(z, step)
                elif last == "y":
                    y_ = ring(y, step)
                else:
                    x_ = ring(x, step)
            at = [
                full if "z" in known else z_,
                full if "x" in known else lax.rem(x_, 2),
                full if "x" in known else x_ // 2,
                full if "y" in known else y_,
            ]
            if half is not None:
                if last == "z":
                    at[1] = half
                else:
                    at[0] = pl.ds(2 * half, 2)
            return bufs[i][p].at[tuple(at)]

        start = 0
        for i in range(n):
            for p in range(3):
                bufs[i][p][z, xl, xh, y] = n_ref[:, start : start + CHUNKS[i][p]]
                start += CHUNKS[i][p]

        everything = []

        def push(i, p, ref, axis, d):
            cp = links.copy(ref, ref, along(axis, d))
            everything.append(cp)
            return cp

        def spread(i, stage, before):
            out = []
            for p in range(3):
                if before is not None:
                    for cp in before[p]:
                        cp.wait_recv()
                ref = block(i, p, ORDERS[p][:stage])
                ds = (2, 1, 3) if stage < 2 else (1, 3)
                out.append([push(i, p, ref, ORDERS[p][stage], d) for d in ds])
            return out

        def relay(i, before):
            out = []
            for p in range(3):
                axis, known = ORDERS[p][2], ORDERS[p][:2]
                before[p][0].wait_recv()
                lower = push(i, p, block(i, p, known, 3, 0), axis, 1)
                before[p][1].wait_recv()
                upper = push(i, p, block(i, p, known, 1, 1), axis, 3)
                out.append([lower, upper])
            return out

        def multiply(i):
            cut = pl.ds(STARTS[i], STARTS[i + 1] - STARTS[i])

            def step(r, carry):
                rows = jnp.concatenate(
                    [bufs[i][p][r].reshape(256, CHUNKS[i][p]) for p in range(3)], axis=1
                )
                top = None
                for k in range(2):
                    part = lax.dot_general(
                        heads[k, :, cut], rows, (((1,), (1,)), ((), ())), preferred_element_type=F32
                    )
                    if i > 0:
                        part = acc[k, r] + part
                    if i < n - 1:
                        acc[k, r] = part
                    else:
                        m = jnp.max(part, axis=0, keepdims=True)
                        top = m if top is None else jnp.maximum(top, m)
                if i == n - 1:
                    maxima[0, pl.ds(r, 1), :] = top
                return carry

            lax.fori_loop(0, 4, step, 0)

        fetch = [
            pltpu.make_async_copy(src, dst, loc.at[2 + k])
            for k, (src, dst) in enumerate(zip(ins[6:], held))
        ]
        one = [spread(i, 0, None) for i in range(n)]
        for cp in fetch:
            cp.start()
        two = [spread(i, 1, one[i]) for i in range(n)]
        three = {0: spread(0, 2, two[0]), 1: spread(1, 2, two[1])}
        for cp in fetch:
            cp.wait()
        attend(*held[:5], att)

        def times_out(k, carry):
            cut = pl.ds(pl.multiple_of(k * 1024, 1024), 1024)
            o = jnp.dot(att[...], held[5][:, cut], preferred_element_type=F32).astype(BF)
            out[:, :, :, :, cut] = o.reshape(2, 4, 2, 16, 1024)
            return carry

        lax.fori_loop(0, 4, times_out, 0)
        swap = links.copy(out.at[:, :, 1 - c], theirs, shift(0, 0, 0, 1))
        over_y = []
        four = {0: relay(0, three[0])}
        for i in range(n):
            if i + 1 < n:
                four[i + 1] = relay(i + 1, three[i + 1])
            if i + 2 < n:
                three[i + 2] = spread(i + 2, 2, two[i + 2])
            if i == n - 2:
                swap.wait()
                for dy in (2, 1, 3, 0):
                    y_ = ring(y, dy)
                    for xh_ in (0, 1):
                        v = out[xh_, y_, c].astype(F32) + theirs[xh_, y_].astype(F32)
                        theirs[xh_, y_] = v.astype(BF)
                    if dy:
                        over_y.append(
                            links.copy(
                                theirs.at[:, y_], came.at[:, y], place(z, xl, xh, y_, c)
                            )
                        )
            for pair in four[i]:
                for cp in pair:
                    cp.wait_recv()
            if i == 0:
                for cp in loads:
                    cp.wait()
            if i == n - 1:
                maxima[0] = sq_ref[...]
            multiply(i)
        top = lax.broadcasted_iota(jnp.int32, (8, 256), 0) < 4

        def join(v, w):
            return jnp.where(top, jnp.maximum(v, w), v + w)

        flat = [links.copy(maxima.at[0], wide.at[k], shift(*key)) for k, key in enumerate(PLANE)]
        for cp in flat:
            cp.wait()
        mine = maxima[0]
        for k in range(15):
            mine = join(mine, wide[k])
        maxima[1] = mine
        tall = [links.copy(maxima.at[1], deep.at[k], shift(*key)) for k, key in enumerate(DEEP)]
        for cp in over_y:
            cp.wait_recv()
        for xh_ in (0, 1):
            v = theirs[xh_, y].astype(F32)
            for dy in (1, 3, 2):
                v = v + came[xh_, ring(y, dy)].astype(F32)
            theirs[xh_, y] = v.astype(BF)
        over_x = links.copy(theirs.at[1 - xh, y], far, place(z, xl, 1 - xh, y, c))
        for cp in tall:
            cp.wait()
        for k in range(3):
            mine = join(mine, deep[k])
        other = deep[3]
        for k in range(4, 7):
            other = join(other, deep[k])
        even = jnp.where(c == 0, mine, other)
        odd = jnp.where(c == 0, other, mine)
        group = lax.broadcasted_iota(jnp.int32, (8, 128), 1) // 16
        for q in range(4):
            row = jnp.zeros((8, 128), F32)
            for a in range(4):
                for k, v in enumerate((even, odd)):
                    half = v[:, q // 2 * 128 : q // 2 * 128 + 128]
                    turn = (a * 16 + k * 16 - q % 2 * 64) % 128
                    turned = pltpu.roll(half, turn, 1) if turn else half
                    row = jnp.where(group == 2 * a + k, turned, row)
            top_ref[:, q * 128 : q * 128 + 128] = row[:4]
        sum_ref[...] = jnp.sqrt((mine + other) * (1.0 / (256 * 4096)))
        over_x.wait_recv()
        total = theirs[xh, y].astype(F32) + far[...].astype(F32)
        hid_ref[...] = layer_end(x_ref[...], total, again_ref[...])
        everything += over_y + [over_x]
        for cp in everything:
            cp.wait_send()
        yield 0

    scratch = [pltpu.VMEM((4, 2, 2, 4, 16, w), BF) for ws in CHUNKS for w in ws]
    scratch += [pltpu.VMEM((2, vocab, 4096), BF), pltpu.VMEM((2, 4, vocab, 256), F32)]
    scratch += [pltpu.VMEM(a.shape, a.dtype) for a in second]
    scratch += [
        pltpu.VMEM((256, 256), BF),
        pltpu.VMEM((2, 4, 2, 16, 4096), BF),
        pltpu.VMEM((2, 4, 16, 4096), BF),
        pltpu.VMEM((2, 4, 16, 4096), BF),
        pltpu.VMEM((16, 4096), BF),
        pltpu.VMEM((2, 8, 256), F32),
        pltpu.VMEM((15, 8, 256), F32),
        pltpu.VMEM((7, 8, 256), F32),
    ]
    return Task(
        body,
        [(normed, VM), (squares, VM), (states_in, VM), (attn_gain, VM)]
        + [(a, ANY) for a in (own_head, other_head) + second],
        [
            (jax.ShapeDtypeStruct((4, 512), F32), VM),
            (jax.ShapeDtypeStruct((8, 256), F32), VM),
            (jax.ShapeDtypeStruct((16, 4096), BF), VM),
        ],
        scratch,
        3 * 3 * 10 + 5 + 22,
        8,
        AXES + PLANE + DEEP,
    )


def back(part2, stat2, first, rows1, gains, heads, second, rows2):
    attn_gain, final_gain = gains
    home = exchange_tok(part2, stat2)
    end = end_first(first, rows1, attn_gain, final_gain)
    normed, squares = (o[0] for o in end.outs)
    shapes = [o[0] for o in home.outs]
    last = gather_logits(normed, squares, *heads, (*shapes, *second), rows2, attn_gain)
    tasks = (home, end, last)
    extra = [(rows2, VM), (heads[0], ANY), (heads[1], ANY)] + [(v, ANY) for v in second]

    def body(ins, outs, scr):
        n_home, n_end = len(home.ins), len(home.ins) + len(end.ins)
        in_home, in_end, more = ins[:n_home], ins[n_home:n_end], ins[n_end:]
        again = in_end[7]
        parts, k = [], 0
        for task in tasks:
            parts.append(scr[k : k + len(task.scratch)])
            k += len(task.scratch)
        n_ref, sq_ref = scr[k:]
        in_last = (n_ref, sq_ref, more[0], again, more[1], more[2], *outs[:2], *more[3:])
        three = last.body(in_last, outs[2:], parts[2])
        one = home.body(in_home, outs[:2], parts[0])
        two = end.body(in_end, (n_ref, sq_ref), parts[1])
        next(one)
        next(three)
        next(two)
        next(one, None)
        next(three)
        next(two, None)
        next(three, None)
        yield 0

    task = Task(
        body,
        list(home.ins) + list(end.ins) + extra,
        list(home.outs) + list(last.outs),
        [],
        1,
        1,
        HEAD_AG + TOK_ALL + AXES + PLANE + DEEP,
    )
    task.scratch = [v for t in tasks for v in t.scratch]
    task.scratch += [pltpu.VMEM(v.shape, v.dtype) for v in (normed, squares)]
    return task


def scores(q, k):
    return lax.dot_general(q, k, (((1,), (1,)), ((), ())), preferred_element_type=F32) * SCALE2


def cached_attention(lengths, queries, keys, values):
    rows = queries.shape[1]
    cuts = [slice(g * HEAD_DIM, (g + 1) * HEAD_DIM) for g in (0, 1)]

    def kernel(len_ref, q_ref, k_ref, v_ref, o_ref, s_ref, v_sc, m_sc, a_sc):
        for g in range(2):
            v_sc[g, :, :HEAD_DIM] = v_ref[:, g * HEAD_DIM : (g + 1) * HEAD_DIM]
            v_sc[g, :, HEAD_DIM:] = jnp.ones((v_ref.shape[0], HEAD_DIM), BF)
        lane = lax.broadcasted_iota(jnp.int32, (rows, 128), 1)
        sub = lax.broadcasted_iota(jnp.int32, (8, rows), 0)

        held = k_ref.shape[0]

        def request(r, before):
            after = before + len_ref[r]
            lo = jnp.minimum(jnp.maximum(before, 0), held)
            hi = jnp.minimum(jnp.maximum(after, 0), held)

            @pl.when(hi <= lo)
            def _():
                o_ref[r] = jnp.zeros(o_ref.shape[1:], BF)
                s_ref[r] = jnp.where(sub < 2, NEG, 0.0)

            @pl.when(hi > lo)
            def _():
                m_sc[...] = jnp.full_like(m_sc, NEG)
                a_sc[...] = jnp.zeros_like(a_sc)

                def step(b, span):
                    at = pl.multiple_of(b * span, span)
                    pos = at + lax.broadcasted_iota(jnp.int32, (1, span), 1)
                    bias = jnp.where((pos >= lo) & (pos < hi), 0.0, NEG)
                    ss = [scores(q_ref[r, :, cut], k_ref[pl.ds(at, span), cut]) for cut in cuts]
                    ss = [s + bias for s in ss]
                    old = [m_sc[g] for g in (0, 1)]
                    new = [
                        jnp.maximum(o, jnp.max(s, axis=-1, keepdims=True)) for o, s in zip(old, ss)
                    ]
                    ps = [jnp.exp2(s - m[:, 0:1]).astype(BF) for s, m in zip(ss, new)]
                    fs = [jnp.exp2(o - m) for o, m in zip(old, new)]
                    ds = [
                        jnp.dot(p, v_sc[g, pl.ds(at, span), :], preferred_element_type=F32)
                        for g, p in enumerate(ps)
                    ]
                    for g in (0, 1):
                        a_sc[g] = a_sc[g] * jnp.concatenate([fs[g], fs[g]], axis=1) + ds[g]
                        m_sc[g] = new[g]

                small = lo // 256 == (hi - 1) // 256

                @pl.when(small)
                def _():
                    step(lo // 256, 256)

                @pl.when(jnp.logical_not(small))
                def _():
                    def wide_step(b, carry):
                        step(b, 512)
                        return carry

                    lax.fori_loop(lo // 512, (hi + 511) // 512, wide_step, 0)

                stats = jnp.where(lane == 0, m_sc[0], m_sc[1])
                stats = jnp.where(lane == 2, a_sc[0, :, HEAD_DIM:], stats)
                stats = jnp.where(lane == 3, a_sc[1, :, HEAD_DIM:], stats)
                s_ref[r] = jnp.transpose(stats)[:8]
                for g in range(2):
                    o_ref[r, :, g * HEAD_DIM : (g + 1) * HEAD_DIM] = a_sc[g, :, :HEAD_DIM].astype(BF)

            return after

        lax.fori_loop(0, 8, request, -lax.axis_index("tok") * held)

    smem = pl.BlockSpec(memory_space=pltpu.SMEM)
    return pl.pallas_call(
        kernel,
        in_specs=[smem, VM, VM, VM],
        out_specs=[VM, VM],
        scratch_shapes=[
            pltpu.VMEM((2, values.shape[0], 256), BF),
            pltpu.VMEM((2, rows, 128), F32),
            pltpu.VMEM((2, rows, 256), F32),
        ],
        out_shape=[
            jax.ShapeDtypeStruct((8, rows, 256), BF),
            jax.ShapeDtypeStruct((8, 8, rows), F32),
        ],
        compiler_params=pltpu.CompilerParams(vmem_limit_bytes=16 << 20),
        name="cached",
    )(lengths, queries, keys, values)


def attend(p_ref, s_ref, q_ref, k_ref, v_ref, att):
    st = jnp.concatenate([s_ref[...].reshape(64, 256), jnp.zeros((64, 256), F32)], axis=0)
    st = jnp.transpose(st)
    for g in range(2):
        cut = slice(g * HEAD_DIM, (g + 1) * HEAD_DIM)
        s = scores(q_ref[:, cut], k_ref[:, cut])
        top = jnp.max(s, axis=-1, keepdims=True)
        for i in range(8):
            top = jnp.maximum(top, st[:, i * 8 + g : i * 8 + g + 1])
        p = jnp.exp2(s - top)
        mass = jnp.sum(p, axis=-1, keepdims=True)
        acc = jnp.dot(p.astype(BF), v_ref[:, cut], preferred_element_type=F32)
        for i in range(8):
            f = jnp.exp2(st[:, i * 8 + g : i * 8 + g + 1] - top)
            mass = mass + f * st[:, i * 8 + g + 2 : i * 8 + g + 3]
            acc = acc + f * p_ref[i, :, cut].astype(F32)
        att[:, cut] = (acc / mass).astype(BF)


def shards(
    block_states,
    token_ids,
    accept,
    cache_lengths,
    cache_keys,
    cache_values,
    w_query,
    w_key,
    w_value,
    w_out,
    attn_gain,
    final_gain,
    embed,
    lm_head,
):
    tok = lax.axis_index("tok")
    other_head = lax.ppermute(lm_head, "head", [(i, i ^ 1) for i in range(16)])
    attn_gain = attn_gain.reshape(1, -1)
    final_gain = final_gain.reshape(1, -1)

    vocab_here = embed.shape[0]
    local_ids = token_ids - tok * vocab_here
    inside = (local_ids >= 0) & (local_ids < vocab_here)
    slots = jnp.where(inside, local_ids, vocab_here)

    weights = (w_query, w_key, w_value)
    ((rows1, q1, k1, v1, qs1, rows2, q2, k2, v2),) = comm(
        [front(block_states, weights, embed, slots, accept.reshape(1, -1))], 0, "comm_a", 60
    )
    part1, stat1 = cached_attention(cache_lengths, qs1, cache_keys, cache_values)

    (qs2,), (part1, stat1) = comm(
        [gather_queries(q2), exchange_tok(part1, stat1)], 2, "comm_c"
    )
    part2, stat2 = cached_attention(cache_lengths, qs2, cache_keys, cache_values)

    first = (part1, stat1, q1, k1, v1, w_out)
    ((_, _, top, sums, hiddens),) = comm(
        [
            back(
                part2,
                stat2,
                first,
                rows1,
                (attn_gain, final_gain),
                (lm_head, other_head),
                (q2, k2, v2, w_out),
                rows2,
            )
        ],
        3,
        "comm_d",
        50,
    )
    return (hiddens, sums[4, :8], top.reshape(-1))


def solution(mesh):
    placed = (
        P("tok", "head"),
        P(),
        P("tok"),
        P(),
        P("tok", "head"),
        P("tok", "head"),
        P(None, "head"),
        P(None, "head"),
        P(None, "head"),
        P("head", None),
        P(),
        P(),
        P("tok", "head"),
        P(("tok", "head"), None),
    )
    return jax.shard_map(
        shards,
        mesh=mesh,
        in_specs=placed,
        out_specs=(P(("tok", "head"), None), P(), P()),
        check_vma=False,
    )
```

```python
import math

import jax
import jax.numpy as jnp
from jax import lax
from jax.experimental import pallas as pl
from jax.experimental.pallas import tpu as pltpu
from jax.sharding import PartitionSpec as P

HEAD_DIM = 128
EPSILON = 1e-06
NEG = -1e30
SCALE2 = (1.0 / math.sqrt(HEAD_DIM)) * math.log2(math.e)
MESH = pl.DeviceIdType.MESH
BF = jnp.bfloat16
F32 = jnp.float32
ANY = pl.BlockSpec(memory_space=pltpu.HBM)
VM = pl.BlockSpec(memory_space=pltpu.VMEM)
REL8 = ((0, 2), (1, 2), (1, 1), (1, 3), (0, 1), (0, 3), (1, 0))


def coords():
    t = lax.axis_index("tok")
    h = lax.axis_index("head")
    return t // 2, lax.rem(t, 2), h // 8, lax.rem(h // 2, 4), lax.rem(h, 2)


def place(z, xl, xh, y, c):
    return (z * 2 + xl, xh * 8 + y * 2 + c)


def ring(v, d):
    return lax.rem(v + d, 4)


class Links:
    def __init__(self, send, recv):
        self.send, self.recv, self.used = send, recv, 0

    def copy(self, src, dst, device):
        k = self.used
        self.used += 1
        cp = pltpu.make_async_remote_copy(
            src_ref=src,
            dst_ref=dst,
            send_sem=self.send.at[k],
            recv_sem=self.recv.at[k],
            device_id=device,
            device_id_type=MESH,
        )
        cp.start()
        return cp


class Task:
    def __init__(self, body, ins, outs, scratch, copies, local, peers):
        self.body, self.ins, self.outs = body, ins, outs
        self.scratch = list(scratch) + [
            pltpu.SemaphoreType.DMA((copies,)),
            pltpu.SemaphoreType.DMA((copies,)),
            pltpu.SemaphoreType.DMA((max(local, 1),)),
        ]
        self.peers = peers


def shift(dx, dy, dz, dc):
    z, xl, xh, y, c = coords()
    c_ = lax.rem(c + dc, 2)
    if dx == "s":
        return place(ring(z, dz), 1 - xl, xh, ring(y, dy), c_)
    x_ = ring(xh * 2 + xl, dx)
    return place(ring(z, dz), lax.rem(x_, 2), x_ // 2, ring(y, dy), c_)


HEAD_AG = [(0, 0, 0, 1), (2, 0, 0, 0), (0, 1, 0, 0), (0, 2, 0, 0), (0, 3, 0, 0)]
HEAD_ALL = [(0, 0, 0, 1)] + [(2 * dx, dy, 0, 0) for dx, dy in REL8]
TOK_AG = [("s", 0, 0, 0), (0, 0, 1, 0), (0, 0, 2, 0), (0, 0, 3, 0)]
TOK_ALL = [("s" if dx else 0, 0, dz, 0) for dx, dz in REL8]
AXES = [(d, 0, 0, 0) for d in (1, 2, 3)] + [(0, d, 0, 0) for d in (1, 2, 3)]
AXES += [(0, 0, d, 0) for d in (1, 2, 3)]
PLANE = [(k // 4, k % 4, 0, 0) for k in range(1, 16)]
DEEP = [(0, 0, k % 4, k // 4) for k in range(1, 8)]


def comm(tasks, cid, name, vmem=4):
    n_in = [len(t.ins) for t in tasks]
    n_out = [len(t.outs) for t in tasks]
    n_scr = [len(t.scratch) for t in tasks]

    def kernel(*refs):
        ins, rest = refs[: sum(n_in)], refs[sum(n_in) :]
        outs, scr = rest[: sum(n_out)], rest[sum(n_out) :]
        peers = {}
        for t in tasks:
            for key in t.peers:
                peers.setdefault(key, shift(*key))
        barrier = pltpu.get_barrier_semaphore()
        for device in peers.values():
            pl.semaphore_signal(barrier, inc=1, device_id=device, device_id_type=MESH)
        pl.semaphore_wait(barrier, len(peers))
        running, a, b, c = [], 0, 0, 0
        for k, t in enumerate(tasks):
            running.append(
                t.body(
                    ins[a : a + n_in[k]], outs[b : b + n_out[k]], scr[c : c + n_scr[k]]
                )
            )
            a, b, c = a + n_in[k], b + n_out[k], c + n_scr[k]
        while running:
            again = []
            for g in running:
                if next(g, StopIteration) is not StopIteration:
                    again.append(g)
            running = again

    flat = pl.pallas_call(
        kernel,
        out_shape=[o[0] for t in tasks for o in t.outs],
        in_specs=[i[1] for t in tasks for i in t.ins],
        out_specs=[o[1] for t in tasks for o in t.outs],
        scratch_shapes=[s for t in tasks for s in t.scratch],
        compiler_params=pltpu.CompilerParams(
            collective_id=cid, has_side_effects=True, vmem_limit_bytes=vmem << 20
        ),
        name=name,
    )(*[i[0] for t in tasks for i in t.ins])
    res, b = [], 0
    for n in n_out:
        res.append(flat[b : b + n])
        b += n
    return res


def project_steps(links, keep_sem, x_ref, f_ref, w_ref, acc, loads, own_rows, outs):
    wide = x_ref.shape[1]
    z, xl, xh, y, c = coords()

    def index(xh_, y_, c_):
        return xh_ * 8 + y_ * 2 + c_

    def slot(*at):
        return f_ref.at[index(*at)]

    def absorb(*at):
        k = index(*at)
        v = f_ref[k]
        for n in range(3):
            w = w_ref[n, pl.ds(pl.multiple_of(k * wide, wide), wide), :]
            acc[n] += jnp.dot(v, w, preferred_element_type=F32)

    core = place(z, xl, xh, y, 1 - c)
    own = slot(xh, y, c)
    keep = pltpu.make_async_copy(x_ref, own, keep_sem)
    keep.start()
    landed = []
    over_x = links.copy(x_ref, own, place(z, xl, 1 - xh, y, c))
    over_y = {d: links.copy(x_ref, own, place(z, xl, xh, ring(y, d), c)) for d in (2, 1, 3)}
    landed.append(links.copy(x_ref, own, core))
    acc[...] = jnp.zeros_like(acc)
    yield 0
    over_x.wait_recv()
    far = slot(1 - xh, y, c)
    far_y = {d: links.copy(far, far, place(z, xl, xh, ring(y, d), c)) for d in (2, 1, 3)}
    landed.append(links.copy(far, far, core))
    yield 0
    keep.wait()
    for cp in loads:
        cp.wait()
    absorb(xh, y, c)
    absorb(1 - xh, y, c)
    for k, xh_ in enumerate((xh, 1 - xh)):
        landed[k].wait_recv()
        absorb(xh_, y, 1 - c)
    yield 0
    for xh_, arrive in ((xh, over_y), (1 - xh, far_y)):
        for d in (1, 3, 2):
            y_ = ring(y, 4 - d)
            arrive[d].wait_recv()
            got = slot(xh_, y_, c)
            landed.append(links.copy(got, got, core))
            absorb(xh_, y_, c)
        for k, d in enumerate((1, 3, 2)):
            landed[k - 3].wait_recv()
            absorb(xh_, ring(y, 4 - d), 1 - c)
        yield 0
    h = pl.multiple_of(index(xh, y, c) * 16, 16)
    for k in range(16):
        own_rows[:, k * wide : (k + 1) * wide] = f_ref[k, pl.ds(h, 16), :]
    for n in range(3):
        outs[n][...] = acc[n].astype(BF)
    yield 0
    for cp in [over_x] + list(over_y.values()) + list(far_y.values()) + landed:
        cp.wait_send()


def query_steps(links, keep_sem, q_ref, o_ref):
    z, xl, xh, y, c = coords()
    own = o_ref.at[z * 2 + xl]
    keep = pltpu.make_async_copy(q_ref, own, keep_sem)
    keep.start()
    side = place(z, 1 - xl, xh, y, c)
    over_x = [links.copy(q_ref, own, side)]
    over_z = {d: links.copy(q_ref, own, place(ring(z, d), xl, xh, y, c)) for d in (2, 1, 3)}
    yield 0
    over_x[0].wait_recv()
    far = o_ref.at[z * 2 + 1 - xl, pl.ds(0, 128)]
    more = [links.copy(far, far, place(ring(z, d), xl, xh, y, c)) for d in (2, 1, 3)]
    yield 0
    for d in (1, 3, 2):
        over_z[d].wait_recv()
        got = o_ref.at[ring(z, 4 - d) * 2 + xl, pl.ds(128, 128)]
        over_x.append(links.copy(got, got, side))
    yield 0
    for cp in over_x[1:] + more:
        cp.wait_recv()
    for cp in over_x + more + list(over_z.values()):
        cp.wait_send()
    keep.wait()


def gather_queries(q):
    def body(ins, outs, scr):
        send, recv, loc = scr
        yield from query_steps(Links(send, recv), loc.at[0], ins[0], outs[0])

    return Task(
        body, [(q, ANY)], [(jax.ShapeDtypeStruct((8, 256, 256), BF), ANY)], [], 10, 1, TOK_AG
    )


def exchange_tok(*arrays):
    def body(ins, outs, scr):
        send, recv, loc = scr
        z, xl, xh, y, c = coords()
        t = z * 2 + xl
        links = Links(send, recv)
        keep, cps = [], []
        for k, (src, dst) in enumerate(zip(ins, outs)):
            keep.append(pltpu.make_async_copy(src.at[t], dst.at[t], loc.at[k]))
            keep[-1].start()
        for dx, dz in REL8:
            z_, xl_ = ring(z, dz), lax.rem(xl + dx, 2)
            for src, dst in zip(ins, outs):
                cps.append(links.copy(src.at[z_ * 2 + xl_], dst.at[t], place(z_, xl_, xh, y, c)))
        yield 0
        for cp in cps:
            cp.wait()
        for cp in keep:
            cp.wait()

    n = len(arrays)
    return Task(
        body,
        [(a, ANY) for a in arrays],
        [(jax.ShapeDtypeStruct(a.shape, a.dtype), ANY) for a in arrays],
        [],
        7 * n,
        n,
        TOK_ALL,
    )


def embed_steps(links, sems, table_ref, slot_ref, old_ref, acc_ref, new_ref, scr):
    raw, table, stage, parts, came = scr
    vocab, wide = table_ref.shape
    piece = vocab // 4
    strip = piece // 7
    z, xl, xh, y, c = coords()
    t = z * 2 + xl
    loads = [
        pltpu.make_async_copy(table_ref.at[pl.ds(k * piece, piece)], raw.at[k], sems.at[k])
        for k in range(4)
    ]
    for cp in loads:
        cp.start()
    table[pl.ds(vocab, 8), :] = jnp.zeros((8, wide), F32)
    for k in range(4):
        loads[k].wait()

        def widen(j, carry, k=k):
            at = pl.multiple_of(j * strip, strip)
            to = pl.multiple_of(k * piece + j * strip, strip)
            table[pl.ds(to, strip), :] = raw[k, pl.ds(at, strip), :].astype(F32)
            return carry

        lax.fori_loop(0, 7, widen, 0)
    yield 0

    def look_up(owner):
        def rows(j, carry):
            for k in range(16):
                n = j * 16 + k
                stage[pl.ds(n, 1), :] = table[pl.ds(slot_ref[owner * 256 + n], 1), :]
            return carry

        lax.fori_loop(0, 16, rows, 0)
        parts[owner] = stage[...].astype(BF)

    cps, sources = [], []
    for dx, dz in REL8:
        z_, xl_ = ring(z, dz), lax.rem(xl + dx, 2)
        look_up(z_ * 2 + xl_)
        cps.append(links.copy(parts.at[z_ * 2 + xl_], came.at[t], place(z_, xl_, xh, y, c)))
        sources.append(z_ * 2 + xl_)
    look_up(t)
    yield 0
    total = parts[t].astype(F32)
    for cp in cps:
        cp.wait()
    for source in sources:
        total = total + came[source].astype(F32)
    taken = jnp.transpose(jnp.broadcast_to(acc_ref[...].astype(F32), (256, 256)))
    new_ref[...] = jnp.where(taken == 1.0, total, old_ref[...].astype(F32)).astype(BF)


def front(block_states, weights, embed, slots, accept):
    rows, wide = block_states.shape
    vocab = embed.shape[0]

    def body(ins, outs, scr):
        x_ref, w_refs, table_ref, slot_ref, old_ref, acc_ref = (
            ins[0],
            ins[1:4],
            ins[4],
            ins[5],
            ins[6],
            ins[7],
        )
        rows1, q1, k1, v1, qs1, rows2, q2, k2, v2 = outs
        f1, f2, w_ref, acc, swapped = scr[:5]
        send, recv, loc = scr[10:]
        links = Links(send, recv)
        loads = [pltpu.make_async_copy(w_refs[n], w_ref.at[n], loc.at[n]) for n in range(3)]
        one = project_steps(
            links, loc.at[3], x_ref, f1, w_ref, acc, loads, rows1, (q1, k1, v1)
        )
        swap = embed_steps(
            links, loc.at[pl.ds(6, 4)], table_ref, slot_ref, old_ref, acc_ref, swapped, scr[5:10]
        )
        next(one)
        next(swap)
        for cp in loads:
            cp.start()
        next(one)
        next(swap)
        for _ in range(4):
            next(one)
        ask = query_steps(links, loc.at[4], q1, qs1)
        next(ask)
        next(swap, None)
        two = project_steps(links, loc.at[5], swapped, f2, w_ref, acc, [], rows2, (q2, k2, v2))
        next(two)
        next(ask)
        next(two)
        next(ask)
        for _ in range(4):
            next(two)
        for left in (one, ask, two):
            next(left, None)
        yield 0

    def out(*shape):
        return jax.ShapeDtypeStruct(shape, BF)

    half = [(out(16, 16 * wide), VM)] + [(out(rows, wide), VM)] * 3
    return Task(
        body,
        [(block_states, ANY)]
        + [(w, ANY) for w in weights]
        + [(embed, ANY), (slots, pl.BlockSpec(memory_space=pltpu.SMEM))]
        + [(block_states, VM), (accept, VM)],
        half + [(out(8, rows, wide), ANY)] + half,
        [
            pltpu.VMEM((16, rows, wide), BF),
            pltpu.VMEM((16, rows, wide), BF),
            pltpu.VMEM((3, 16 * wide, wide), BF),
            pltpu.VMEM((3, rows, wide), F32),
            pltpu.VMEM((rows, wide), BF),
            pltpu.VMEM((4, vocab // 4, wide), BF),
            pltpu.VMEM((vocab + 8, wide), F32),
            pltpu.VMEM((rows, wide), F32),
            pltpu.VMEM((8, rows, wide), BF),
            pltpu.VMEM((8, rows, wide), BF),
        ],
        15 + 7 + 10 + 15,
        10,
        HEAD_AG + TOK_ALL,
    )


def unit_rows(v):
    return v * lax.rsqrt(jnp.mean(v * v, axis=-1, keepdims=True) + EPSILON)


def layer_end(before, total, gain):
    return (before.astype(F32) + unit_rows(total) * gain).astype(BF)


def end_first(first, states_in, attn_gain, final_gain):
    chunks = 4

    def body(ins, outs, scr):
        x_ref, again_ref, fgain_ref = ins[6:]
        held = scr[:6]
        att, out, theirs, came, far, total, send, recv, loc = scr[6:]
        z, xl, xh, y, c = coords()
        links = Links(send, recv)
        cuts = [pl.ds(k * 1024, 1024) for k in range(chunks)]
        fetch = [
            pltpu.make_async_copy(src, dst, loc.at[k])
            for k, (src, dst) in enumerate(zip(ins[:6], held))
        ]
        for cp in fetch:
            cp.start()
        for cp in fetch:
            cp.wait()
        attend(*held[:5], att)
        core = place(z, xl, xh, y, 1 - c)
        swaps, over_y, over_x = [], [], []
        for cut in cuts:
            o = jnp.dot(att[...], held[5][:, cut], preferred_element_type=F32).astype(BF)
            out[:, :, :, :, cut] = o.reshape(2, 4, 2, 16, 1024)
            swaps.append(
                links.copy(out.at[:, :, 1 - c, :, cut], theirs.at[:, :, :, cut], core)
            )
        yield 0

        def both(xh_, y_, cut):
            return out[xh_, y_, c, :, cut].astype(F32) + theirs[xh_, y_, :, cut].astype(F32)

        for k, cut in enumerate(cuts):
            swaps[k].wait_recv()
            over_y.append([])
            for dy in (2, 1, 3):
                y_ = ring(y, dy)
                for xh_ in (0, 1):
                    theirs[xh_, y_, :, cut] = both(xh_, y_, cut).astype(BF)
                over_y[k].append(
                    links.copy(
                        theirs.at[:, y_, :, cut],
                        came.at[:, y, :, cut],
                        place(z, xl, xh, y_, c),
                    )
                )
        for k, cut in enumerate(cuts):
            for cp in over_y[k]:
                cp.wait_recv()
            away, mine = both(1 - xh, y, cut), both(xh, y, cut)
            for dy in (1, 3, 2):
                y_ = ring(y, dy)
                away = away + came[1 - xh, y_, :, cut].astype(F32)
                mine = mine + came[xh, y_, :, cut].astype(F32)
            theirs[1 - xh, y, :, cut] = away.astype(BF)
            over_x.append(
                links.copy(
                    theirs.at[1 - xh, y, :, cut], far.at[:, cut], place(z, xl, 1 - xh, y, c)
                )
            )
            total[:, cut] = mine
        for cp in over_x:
            cp.wait_recv()
        wide = layer_end(
            x_ref[...], total[...] + far[...].astype(F32), again_ref[...]
        ).astype(F32)
        squares = jnp.sum(wide * wide, axis=-1, keepdims=True)
        normed = wide * lax.rsqrt(squares * (1.0 / 4096) + EPSILON) * fgain_ref[...]
        outs[0][...] = normed.astype(BF)
        lane = lax.broadcasted_iota(jnp.int32, (8, 256), 1)
        row = lax.broadcasted_iota(jnp.int32, (8, 256), 0)
        outs[1][...] = jnp.where((lane == z * 2 + xl) & (row == 4), jnp.sum(squares), 0.0)
        for cp in swaps + [cp for k in over_y for cp in k] + over_x:
            cp.wait_send()
        yield 0

    block = pltpu.VMEM((2, 4, 16, 4096), BF)
    return Task(
        body,
        [(a, ANY) for a in first] + [(states_in, VM), (attn_gain, VM), (final_gain, VM)],
        [(jax.ShapeDtypeStruct((16, 4096), BF), VM), (jax.ShapeDtypeStruct((8, 256), F32), VM)],
        [pltpu.VMEM(a.shape, a.dtype) for a in first]
        + [
            pltpu.VMEM((256, 256), BF),
            pltpu.VMEM((2, 4, 2, 16, 4096), BF),
            block,
            block,
            pltpu.VMEM((16, 4096), BF),
            pltpu.VMEM((16, 4096), F32),
        ],
        5 * chunks,
        6,
        HEAD_AG,
    )


def along(axis, d):
    return shift(*{"x": (d, 0, 0, 0), "y": (0, d, 0, 0), "z": (0, 0, d, 0)}[axis])


CHUNKS = ((512, 512, 512), (512, 512, 512), (384, 384, 256))
STARTS = (0, 1536, 3072, 4096)
ORDERS = ("xyz", "yzx", "zxy")


def gather_logits(normed, squares, own_head, other_head, second, states_in, attn_gain):
    vocab = own_head.shape[0]
    n = len(CHUNKS)

    def body(ins, outs, scr):
        n_ref, sq_ref, x_ref, again_ref, own_ref, other_ref = ins[:6]
        top_ref, sum_ref, hid_ref = outs
        bufs = [scr[3 * i : 3 * i + 3] for i in range(n)]
        heads, acc = scr[9:11]
        held = scr[11:17]
        att, out, theirs, came, far, maxima, wide, deep, send, recv, loc = scr[17:]
        z, xl, xh, y, c = coords()
        x = xh * 2 + xl
        links = Links(send, recv)
        full = slice(None)
        loads = [
            pltpu.make_async_copy(src, heads.at[k], loc.at[k])
            for k, src in enumerate((own_ref, other_ref))
        ]

        for cp in loads:
            cp.start()
        yield 0

        def block(i, p, known, step=0, half=None):
            last = ORDERS[p][2]
            z_, y_, x_ = z, y, x
            if step:
                if last == "z":
                    z_ = ring(z, step)
                elif last == "y":
                    y_ = ring(y, step)
                else:
                    x_ = ring(x, step)
            at = [
                full if "z" in known else z_,
                full if "x" in known else lax.rem(x_, 2),
                full if "x" in known else x_ // 2,
                full if "y" in known else y_,
            ]
            if half is not None:
                if last == "z":
                    at[1] = half
                else:
                    at[0] = pl.ds(2 * half, 2)
            return bufs[i][p].at[tuple(at)]

        start = 0
        for i in range(n):
            for p in range(3):
                bufs[i][p][z, xl, xh, y] = n_ref[:, start : start + CHUNKS[i][p]]
                start += CHUNKS[i][p]

        everything = []

        def push(i, p, ref, axis, d):
            cp = links.copy(ref, ref, along(axis, d))
            everything.append(cp)
            return cp

        def spread(i, stage, before):
            out = []
            for p in range(3):
                if before is not None:
                    for cp in before[p]:
                        cp.wait_recv()
                ref = block(i, p, ORDERS[p][:stage])
                ds = (2, 1, 3) if stage < 2 else (1, 3)
                out.append([push(i, p, ref, ORDERS[p][stage], d) for d in ds])
            return out

        def relay(i, before):
            out = []
            for p in range(3):
                axis, known = ORDERS[p][2], ORDERS[p][:2]
                before[p][0].wait_recv()
                lower = push(i, p, block(i, p, known, 3, 0), axis, 1)
                before[p][1].wait_recv()
                upper = push(i, p, block(i, p, known, 1, 1), axis, 3)
                out.append([lower, upper])
            return out

        def multiply(i):
            cut = pl.ds(STARTS[i], STARTS[i + 1] - STARTS[i])

            def step(r, carry):
                rows = jnp.concatenate(
                    [bufs[i][p][r].reshape(256, CHUNKS[i][p]) for p in range(3)], axis=1
                )
                top = None
                for k in range(2):
                    part = lax.dot_general(
                        heads[k, :, cut], rows, (((1,), (1,)), ((), ())), preferred_element_type=F32
                    )
                    if i > 0:
                        part = acc[k, r] + part
                    if i < n - 1:
                        acc[k, r] = part
                    else:
                        m = jnp.max(part, axis=0, keepdims=True)
                        top = m if top is None else jnp.maximum(top, m)
                if i == n - 1:
                    maxima[0, pl.ds(r, 1), :] = top
                return carry

            lax.fori_loop(0, 4, step, 0)

        fetch = [
            pltpu.make_async_copy(src, dst, loc.at[2 + k])
            for k, (src, dst) in enumerate(zip(ins[6:], held))
        ]
        one = [spread(i, 0, None) for i in range(n)]
        for cp in fetch:
            cp.start()
        two = [spread(i, 1, one[i]) for i in range(n)]
        three = {0: spread(0, 2, two[0]), 1: spread(1, 2, two[1])}
        for cp in fetch:
            cp.wait()
        attend(*held[:5], att)

        def times_out(k, carry):
            cut = pl.ds(pl.multiple_of(k * 1024, 1024), 1024)
            o = jnp.dot(att[...], held[5][:, cut], preferred_element_type=F32).astype(BF)
            out[:, :, :, :, cut] = o.reshape(2, 4, 2, 16, 1024)
            return carry

        lax.fori_loop(0, 4, times_out, 0)
        swap = links.copy(out.at[:, :, 1 - c], theirs, shift(0, 0, 0, 1))
        over_y = []
        four = {0: relay(0, three[0])}
        for i in range(n):
            if i + 1 < n:
                four[i + 1] = relay(i + 1, three[i + 1])
            if i + 2 < n:
                three[i + 2] = spread(i + 2, 2, two[i + 2])
            if i == n - 2:
                swap.wait()
                for dy in (2, 1, 3, 0):
                    y_ = ring(y, dy)
                    for xh_ in (0, 1):
                        v = out[xh_, y_, c].astype(F32) + theirs[xh_, y_].astype(F32)
                        theirs[xh_, y_] = v.astype(BF)
                    if dy:
                        over_y.append(
                            links.copy(
                                theirs.at[:, y_], came.at[:, y], place(z, xl, xh, y_, c)
                            )
                        )
            for pair in four[i]:
                for cp in pair:
                    cp.wait_recv()
            if i == 0:
                for cp in loads:
                    cp.wait()
            if i == n - 1:
                maxima[0] = sq_ref[...]
            multiply(i)
        top = lax.broadcasted_iota(jnp.int32, (8, 256), 0) < 4

        def join(v, w):
            return jnp.where(top, jnp.maximum(v, w), v + w)

        flat = [links.copy(maxima.at[0], wide.at[k], shift(*key)) for k, key in enumerate(PLANE)]
        for cp in flat:
            cp.wait()
        mine = maxima[0]
        for k in range(15):
            mine = join(mine, wide[k])
        maxima[1] = mine
        tall = [links.copy(maxima.at[1], deep.at[k], shift(*key)) for k, key in enumerate(DEEP)]
        for cp in over_y:
            cp.wait_recv()
        for xh_ in (0, 1):
            v = theirs[xh_, y].astype(F32)
            for dy in (1, 3, 2):
                v = v + came[xh_, ring(y, dy)].astype(F32)
            theirs[xh_, y] = v.astype(BF)
        over_x = links.copy(theirs.at[1 - xh, y], far, place(z, xl, 1 - xh, y, c))
        for cp in tall:
            cp.wait()
        for k in range(3):
            mine = join(mine, deep[k])
        other = deep[3]
        for k in range(4, 7):
            other = join(other, deep[k])
        even = jnp.where(c == 0, mine, other)
        odd = jnp.where(c == 0, other, mine)
        group = lax.broadcasted_iota(jnp.int32, (8, 128), 1) // 16
        for q in range(4):
            row = jnp.zeros((8, 128), F32)
            for a in range(4):
                for k, v in enumerate((even, odd)):
                    half = v[:, q // 2 * 128 : q // 2 * 128 + 128]
                    turn = (a * 16 + k * 16 - q % 2 * 64) % 128
                    turned = pltpu.roll(half, turn, 1) if turn else half
                    row = jnp.where(group == 2 * a + k, turned, row)
            top_ref[:, q * 128 : q * 128 + 128] = row[:4]
        sum_ref[...] = jnp.sqrt((mine + other) * (1.0 / (256 * 4096)))
        over_x.wait_recv()
        total = theirs[xh, y].astype(F32) + far[...].astype(F32)
        hid_ref[...] = layer_end(x_ref[...], total, again_ref[...])
        everything += over_y + [over_x]
        for cp in everything:
            cp.wait_send()
        yield 0

    scratch = [pltpu.VMEM((4, 2, 2, 4, 16, w), BF) for ws in CHUNKS for w in ws]
    scratch += [pltpu.VMEM((2, vocab, 4096), BF), pltpu.VMEM((2, 4, vocab, 256), F32)]
    scratch += [pltpu.VMEM(a.shape, a.dtype) for a in second]
    scratch += [
        pltpu.VMEM((256, 256), BF),
        pltpu.VMEM((2, 4, 2, 16, 4096), BF),
        pltpu.VMEM((2, 4, 16, 4096), BF),
        pltpu.VMEM((2, 4, 16, 4096), BF),
        pltpu.VMEM((16, 4096), BF),
        pltpu.VMEM((2, 8, 256), F32),
        pltpu.VMEM((15, 8, 256), F32),
        pltpu.VMEM((7, 8, 256), F32),
    ]
    return Task(
        body,
        [(normed, VM), (squares, VM), (states_in, VM), (attn_gain, VM)]
        + [(a, ANY) for a in (own_head, other_head) + second],
        [
            (jax.ShapeDtypeStruct((4, 512), F32), VM),
            (jax.ShapeDtypeStruct((8, 256), F32), VM),
            (jax.ShapeDtypeStruct((16, 4096), BF), VM),
        ],
        scratch,
        3 * 3 * 10 + 5 + 22,
        8,
        AXES + PLANE + DEEP,
    )


def back(part2, stat2, first, rows1, gains, heads, second, rows2):
    attn_gain, final_gain = gains
    home = exchange_tok(part2, stat2)
    end = end_first(first, rows1, attn_gain, final_gain)
    normed, squares = (o[0] for o in end.outs)
    shapes = [o[0] for o in home.outs]
    last = gather_logits(normed, squares, *heads, (*shapes, *second), rows2, attn_gain)
    tasks = (home, end, last)
    extra = [(rows2, VM), (heads[0], ANY), (heads[1], ANY)] + [(v, ANY) for v in second]

    def body(ins, outs, scr):
        n_home, n_end = len(home.ins), len(home.ins) + len(end.ins)
        in_home, in_end, more = ins[:n_home], ins[n_home:n_end], ins[n_end:]
        again = in_end[7]
        parts, k = [], 0
        for task in tasks:
            parts.append(scr[k : k + len(task.scratch)])
            k += len(task.scratch)
        n_ref, sq_ref = scr[k:]
        in_last = (n_ref, sq_ref, more[0], again, more[1], more[2], *outs[:2], *more[3:])
        three = last.body(in_last, outs[2:], parts[2])
        one = home.body(in_home, outs[:2], parts[0])
        two = end.body(in_end, (n_ref, sq_ref), parts[1])
        next(one)
        next(two)
        next(three)
        next(two)
        next(one, None)
        next(three)
        next(two, None)
        next(three, None)
        yield 0

    task = Task(
        body,
        list(home.ins) + list(end.ins) + extra,
        list(home.outs) + list(last.outs),
        [],
        1,
        1,
        HEAD_AG + TOK_ALL + AXES + PLANE + DEEP,
    )
    task.scratch = [v for t in tasks for v in t.scratch]
    task.scratch += [pltpu.VMEM(v.shape, v.dtype) for v in (normed, squares)]
    return task


def scores(q, k):
    return lax.dot_general(q, k, (((1,), (1,)), ((), ())), preferred_element_type=F32) * SCALE2


def cached_attention(lengths, queries, keys, values):
    rows = queries.shape[1]
    cuts = [slice(g * HEAD_DIM, (g + 1) * HEAD_DIM) for g in (0, 1)]

    def kernel(len_ref, q_ref, k_ref, v_ref, o_ref, s_ref, v_sc, m_sc, a_sc):
        for g in range(2):
            v_sc[g, :, :HEAD_DIM] = v_ref[:, g * HEAD_DIM : (g + 1) * HEAD_DIM]
            v_sc[g, :, HEAD_DIM:] = jnp.ones((v_ref.shape[0], HEAD_DIM), BF)
        lane = lax.broadcasted_iota(jnp.int32, (rows, 128), 1)
        sub = lax.broadcasted_iota(jnp.int32, (8, rows), 0)

        held = k_ref.shape[0]

        def request(r, before):
            after = before + len_ref[r]
            lo = jnp.minimum(jnp.maximum(before, 0), held)
            hi = jnp.minimum(jnp.maximum(after, 0), held)

            @pl.when(hi <= lo)
            def _():
                o_ref[r] = jnp.zeros(o_ref.shape[1:], BF)
                s_ref[r] = jnp.where(sub < 2, NEG, 0.0)

            @pl.when(hi > lo)
            def _():
                m_sc[...] = jnp.full_like(m_sc, NEG)
                a_sc[...] = jnp.zeros_like(a_sc)

                def step(b, span):
                    at = pl.multiple_of(b * span, span)
                    pos = at + lax.broadcasted_iota(jnp.int32, (1, span), 1)
                    bias = jnp.where((pos >= lo) & (pos < hi), 0.0, NEG)
                    ss = [scores(q_ref[r, :, cut], k_ref[pl.ds(at, span), cut]) for cut in cuts]
                    ss = [s + bias for s in ss]
                    old = [m_sc[g] for g in (0, 1)]
                    new = [
                        jnp.maximum(o, jnp.max(s, axis=-1, keepdims=True)) for o, s in zip(old, ss)
                    ]
                    ps = [jnp.exp2(s - m[:, 0:1]).astype(BF) for s, m in zip(ss, new)]
                    fs = [jnp.exp2(o - m) for o, m in zip(old, new)]
                    ds = [
                        jnp.dot(p, v_sc[g, pl.ds(at, span), :], preferred_element_type=F32)
                        for g, p in enumerate(ps)
                    ]
                    for g in (0, 1):
                        a_sc[g] = a_sc[g] * jnp.concatenate([fs[g], fs[g]], axis=1) + ds[g]
                        m_sc[g] = new[g]

                small = lo // 256 == (hi - 1) // 256

                @pl.when(small)
                def _():
                    step(lo // 256, 256)

                @pl.when(jnp.logical_not(small))
                def _():
                    def wide_step(b, carry):
                        step(b, 512)
                        return carry

                    lax.fori_loop(lo // 512, (hi + 511) // 512, wide_step, 0)

                stats = jnp.where(lane == 0, m_sc[0], m_sc[1])
                stats = jnp.where(lane == 2, a_sc[0, :, HEAD_DIM:], stats)
                stats = jnp.where(lane == 3, a_sc[1, :, HEAD_DIM:], stats)
                s_ref[r] = jnp.transpose(stats)[:8]
                for g in range(2):
                    o_ref[r, :, g * HEAD_DIM : (g + 1) * HEAD_DIM] = a_sc[g, :, :HEAD_DIM].astype(BF)

            return after

        lax.fori_loop(0, 8, request, -lax.axis_index("tok") * held)

    smem = pl.BlockSpec(memory_space=pltpu.SMEM)
    return pl.pallas_call(
        kernel,
        in_specs=[smem, VM, VM, VM],
        out_specs=[VM, VM],
        scratch_shapes=[
            pltpu.VMEM((2, values.shape[0], 256), BF),
            pltpu.VMEM((2, rows, 128), F32),
            pltpu.VMEM((2, rows, 256), F32),
        ],
        out_shape=[
            jax.ShapeDtypeStruct((8, rows, 256), BF),
            jax.ShapeDtypeStruct((8, 8, rows), F32),
        ],
        compiler_params=pltpu.CompilerParams(vmem_limit_bytes=16 << 20),
        name="cached",
    )(lengths, queries, keys, values)


def attend(p_ref, s_ref, q_ref, k_ref, v_ref, att):
    st = jnp.concatenate([s_ref[...].reshape(64, 256), jnp.zeros((64, 256), F32)], axis=0)
    st = jnp.transpose(st)
    for g in range(2):
        cut = slice(g * HEAD_DIM, (g + 1) * HEAD_DIM)
        s = scores(q_ref[:, cut], k_ref[:, cut])
        top = jnp.max(s, axis=-1, keepdims=True)
        for i in range(8):
            top = jnp.maximum(top, st[:, i * 8 + g : i * 8 + g + 1])
        p = jnp.exp2(s - top)
        mass = jnp.sum(p, axis=-1, keepdims=True)
        acc = jnp.dot(p.astype(BF), v_ref[:, cut], preferred_element_type=F32)
        for i in range(8):
            f = jnp.exp2(st[:, i * 8 + g : i * 8 + g + 1] - top)
            mass = mass + f * st[:, i * 8 + g + 2 : i * 8 + g + 3]
            acc = acc + f * p_ref[i, :, cut].astype(F32)
        att[:, cut] = (acc / mass).astype(BF)


def shards(
    block_states,
    token_ids,
    accept,
    cache_lengths,
    cache_keys,
    cache_values,
    w_query,
    w_key,
    w_value,
    w_out,
    attn_gain,
    final_gain,
    embed,
    lm_head,
):
    tok = lax.axis_index("tok")
    other_head = lax.ppermute(lm_head, "head", [(i, i ^ 1) for i in range(16)])
    attn_gain = attn_gain.reshape(1, -1)
    final_gain = final_gain.reshape(1, -1)

    vocab_here = embed.shape[0]
    local_ids = token_ids - tok * vocab_here
    inside = (local_ids >= 0) & (local_ids < vocab_here)
    slots = jnp.where(inside, local_ids, vocab_here)

    weights = (w_query, w_key, w_value)
    ((rows1, q1, k1, v1, qs1, rows2, q2, k2, v2),) = comm(
        [front(block_states, weights, embed, slots, accept.reshape(1, -1))], 0, "comm_a", 60
    )
    part1, stat1 = cached_attention(cache_lengths, qs1, cache_keys, cache_values)

    (qs2,), (part1, stat1) = comm(
        [gather_queries(q2), exchange_tok(part1, stat1)], 2, "comm_c"
    )
    part2, stat2 = cached_attention(cache_lengths, qs2, cache_keys, cache_values)

    first = (part1, stat1, q1, k1, v1, w_out)
    ((_, _, top, sums, hiddens),) = comm(
        [
            back(
                part2,
                stat2,
                first,
                rows1,
                (attn_gain, final_gain),
                (lm_head, other_head),
                (q2, k2, v2, w_out),
                rows2,
            )
        ],
        3,
        "comm_d",
        47,
    )
    return (hiddens, sums[4, :8], top.reshape(-1))


def solution(mesh):
    placed = (
        P("tok", "head"),
        P(),
        P("tok"),
        P(),
        P("tok", "head"),
        P("tok", "head"),
        P(None, "head"),
        P(None, "head"),
        P(None, "head"),
        P("head", None),
        P(),
        P(),
        P("tok", "head"),
        P(("tok", "head"), None),
    )
    return jax.shard_map(
        shards,
        mesh=mesh,
        in_specs=placed,
        out_specs=(P(("tok", "head"), None), P(), P()),
        check_vma=False,
    )
```
